32 devices in a mesh: shard: 4 (over z), ctx: 4 (over y, core), tp: 2 (over x).
Axes of the slice: x: 2, y: 2, z: 4, core: 2. Of those that a mesh axis runs over, the one named last changes fastest.
Arguments:
- block_input: float32 [2048, 640], P(('shard', 'ctx')), may hold values from -6 to 6
- out_cotangent: float32 [2048, 640], P(('shard', 'ctx')), may hold values from -6 to 6
- seq_lengths: int32 [4, 4], P('shard'), may hold values from 1 to 256, 512 in all within a row
- q_weight: bfloat16 [640, 1024], P('shard', 'tp'), may hold values from -0.25 to 0.25
- k_weight: bfloat16 [640, 256], P('shard'), may hold values from -0.25 to 0.25
- v_weight: bfloat16 [640, 256], P('shard'), may hold values from -0.25 to 0.25
- o_weight: bfloat16 [640, 1024], P('shard', 'tp'), may hold values from -0.1875 to 0.1875
- gate_weight: bfloat16 [640, 2048], P('shard', 'tp'), may hold values from -0.25 to 0.25
- up_weight: bfloat16 [640, 2048], P('shard', 'tp'), may hold values from -0.25 to 0.25
- down_weight: bfloat16 [640, 2048], P('shard', 'tp'), may hold values from -0.125 to 0.125
- attn_in_gain: bfloat16 [640], P('shard'), may hold values from 0.25 to 1.75
- attn_out_gain: bfloat16 [640], P('shard'), may hold values from 0.25 to 1.75
- ffn_in_gain: bfloat16 [640], P('shard'), may hold values from 0.25 to 1.75
- ffn_out_gain: bfloat16 [640], P('shard'), may hold values from 0.25 to 1.75
- query_gain: bfloat16 [256], P('shard'), may hold values from 0.25 to 1.75
- key_gain: bfloat16 [256], P('shard'), may hold values from 0.25 to 1.75
Outputs:
- block_output: float32 [2048, 640], P(('shard', 'ctx'))
- input_grad: float32 [2048, 640], P(('shard', 'ctx'))
- q_weight_grad: float32 [640, 1024], P('shard', 'tp')
- k_weight_grad: float32 [640, 256], P('shard')
- v_weight_grad: float32 [640, 256], P('shard')
- o_weight_grad: float32 [640, 1024], P('shard', 'tp')
- gate_weight_grad: float32 [640, 2048], P('shard', 'tp')
- up_weight_grad: float32 [640, 2048], P('shard', 'tp')
- down_weight_grad: float32 [640, 2048], P('shard', 'tp')
- attn_in_gain_grad: float32 [640], P('shard')
- attn_out_gain_grad: float32 [640], P('shard')
- ffn_in_gain_grad: float32 [640], P('shard')
- ffn_out_gain_grad: float32 [640], P('shard')
- query_gain_grad: float32 [256], P('shard')
- key_gain_grad: float32 [256], P('shard')
The draws below stay inside these ranges and needn't reach their ends.
Inputs may be any that keep to these rules, and one draw needn't show every extreme that they name: Row b of seq_lengths lists the 4 sequences packed into row b in order; they sum to 512, and the longest of every row has exactly 256 tokens.
All inputs are finite; a program needn't handle non-finite values.
Results may differ from the reference program's by a relative error of at most 0.015.
Values may be sent and summed in bfloat16 or wider, within the bound.
A program may use at most 64 MiB of HBM per device.

```python
import math
import jax
import jax.numpy as jnp
import numpy as np
from jax import lax

D = 640
HEADS = 4
HD = 256
FF = 2048
SEQS = 4
LENGTH = 512
MOST = 256
TOKENS = 2048
N_SHARD = 4


def levels(rng, extent, split, low, high):
    gain, own = 1.0, jax.random.fold_in(rng, 6)
    for axis_at, blocks in split:
        steps = jnp.exp(jax.random.uniform(jax.random.fold_in(own, axis_at), (blocks,), jnp.float32, low / len(split), high / len(split)))
        gain = gain * jnp.repeat(steps, extent[axis_at] // blocks).reshape([-1 if axis == axis_at else 1 for axis in range(len(extent))])
    return gain


def length_profile(count, total, limit, skew):
    loads = [(1 << 20) // math.isqrt(standing ** skew) + 1 for standing in range(2, count + 1)]
    surplus, given = total - limit - (count - 1), [1] * (count - 1)
    while surplus > 0:
        movable = [i for i in range(count - 1) if given[i] < limit]
        pool, left = sum([loads[i] for i in movable]), surplus
        for i in movable:
            extra = min(limit - given[i], max(1, left * loads[i] // pool), surplus)
            given[i] = given[i] + extra
            surplus = surplus - extra
    return np.array([limit] + given)


def ragged(rng, count, total, most, skew):
    if count == 2:
        one = jax.random.randint(rng, (), max(1, total - most), min(most, total - 1) + 1)
        return jnp.stack([one, total - one])
    sizes = jnp.asarray(length_profile(count, total, most, skew), jnp.int32)
    twos = (count - 1) // 2
    giver, taker = sizes[1:1 + 2 * twos:2], sizes[2:2 + 2 * twos:2]
    room = jnp.minimum(giver - 1, most - taker)
    moved = jax.random.randint(jax.random.fold_in(rng, 1), (twos,), 0, 1 << 20) % (room + 1)
    sizes = sizes.at[1:1 + 2 * twos:2].set(giver - moved).at[2:2 + 2 * twos:2].set(taker + moved)
    return sizes[jax.random.permutation(jax.random.fold_in(rng, 2), count)]


def gaussian(key, shape, deviation, reach, split=(), dtype=jnp.bfloat16):
    values = deviation * jax.random.normal(key, shape, jnp.float32)
    if split:
        values = values * levels(key, shape, split, -0.22, 0.18)
    return jnp.clip(values, -reach, reach).astype(dtype)


def setup_inputs(seed: int = 0) -> dict:
    arg_keys = jax.random.split(jax.random.key(seed), 17)
    block_input = gaussian(arg_keys[0], (TOKENS, D), 1.0, 6.0, ((0, 16),), jnp.float32)
    out_cotangent = gaussian(arg_keys[1], (TOKENS, D), 1.0, 6.0, ((0, 16),), jnp.float32)
    seq_lengths = jax.vmap(lambda own: ragged(own, SEQS, LENGTH, MOST, 2))(jax.random.split(arg_keys[2], N_SHARD)).reshape((N_SHARD, SEQS)).astype(jnp.int32)
    q_weight = gaussian(arg_keys[3], (D, HEADS * HD), D ** -0.5, 0.25, ((0, 4), (1, 2)))
    k_weight = gaussian(arg_keys[4], (D, HD), D ** -0.5, 0.25, ((0, 4),))
    v_weight = gaussian(arg_keys[5], (D, HD), D ** -0.5, 0.25, ((0, 4),))
    o_weight = gaussian(arg_keys[6], (D, HEADS * HD), (HEADS * HD) ** -0.5, 0.1875, ((0, 4), (1, 2)))
    gate_weight = gaussian(arg_keys[7], (D, FF), D ** -0.5, 0.25, ((0, 4), (1, 2)))
    up_weight = gaussian(arg_keys[8], (D, FF), D ** -0.5, 0.25, ((0, 4), (1, 2)))
    down_weight = gaussian(arg_keys[9], (D, FF), FF ** -0.5, 0.125, ((0, 4), (1, 2)))
    attn_in_gain = jnp.clip(1.0 + 0.15 * jax.random.normal(arg_keys[10], (D,), jnp.float32), 0.25, 1.75).astype(jnp.bfloat16)
    attn_out_gain = jnp.clip(1.0 + 0.15 * jax.random.normal(arg_keys[11], (D,), jnp.float32), 0.25, 1.75).astype(jnp.bfloat16)
    ffn_in_gain = jnp.clip(1.0 + 0.15 * jax.random.normal(arg_keys[12], (D,), jnp.float32), 0.25, 1.75).astype(jnp.bfloat16)
    ffn_out_gain = jnp.clip(1.0 + 0.15 * jax.random.normal(arg_keys[13], (D,), jnp.float32), 0.25, 1.75).astype(jnp.bfloat16)
    query_gain = jnp.clip(1.0 + 0.15 * jax.random.normal(arg_keys[14], (HD,), jnp.float32), 0.25, 1.75).astype(jnp.bfloat16)
    key_gain = jnp.clip(1.0 + 0.15 * jax.random.normal(arg_keys[15], (HD,), jnp.float32), 0.25, 1.75).astype(jnp.bfloat16)
    return dict(block_input=block_input, out_cotangent=out_cotangent, seq_lengths=seq_lengths, q_weight=q_weight, k_weight=k_weight, v_weight=v_weight, o_weight=o_weight, gate_weight=gate_weight, up_weight=up_weight, down_weight=down_weight, attn_in_gain=attn_in_gain, attn_out_gain=attn_out_gain, ffn_in_gain=ffn_in_gain, ffn_out_gain=ffn_out_gain, query_gain=query_gain, key_gain=key_gain)


eps = 1e-06
rope_base = 1000000.0

def dot_plain(left, right):
    return jnp.dot(left.astype(jnp.float32), right.astype(jnp.float32), preferred_element_type=jnp.float32)

def dot_last(left, right):
    return lax.dot_general(left.astype(jnp.float32), right.astype(jnp.float32), (((1,), (1,)), ((), ())), preferred_element_type=jnp.float32)

def dot_first(left, right):
    return lax.dot_general(left.astype(jnp.float32), right.astype(jnp.float32), (((0,), (0,)), ((), ())), preferred_element_type=jnp.float32)

def norm_parts(value):
    scale = lax.rsqrt(lax.optimization_barrier(jnp.mean(value * value, axis=-1, keepdims=True)) + eps)
    return (value * scale, scale)

def norm_back(dnormed, unit, scale):
    return scale * (dnormed - unit * lax.optimization_barrier(jnp.mean(dnormed * unit, axis=-1, keepdims=True)))

def rope_tables(position):
    freq = rope_base ** (-jnp.arange(HD // 2).astype(jnp.float32) * (2.0 / HD))
    angle = position.astype(jnp.float32)[:, None] * freq[None, :]
    return (jnp.cos(angle), jnp.sin(angle))

def rotate(value, cosine, sine):
    half = value.shape[-1] // 2
    first, second = (value[..., :half], value[..., half:])
    return jnp.concatenate([first * cosine - second * sine, second * cosine + first * sine], axis=-1)

def unrotate(value, cosine, sine):
    half = value.shape[-1] // 2
    first, second = (value[..., :half], value[..., half:])
    return jnp.concatenate([first * cosine + second * sine, second * cosine - first * sine], axis=-1)

def layout(lengths, count):
    index = jnp.arange(count).astype(jnp.int32)
    ends = jnp.cumsum(lengths).astype(jnp.int32)
    after = (index[:, None] >= ends[None, :]).astype(jnp.int32)
    segment = lax.optimization_barrier(jnp.sum(after, axis=1)).astype(jnp.int32)
    position = (index - lax.optimization_barrier(jnp.sum(after * lengths[None, :], axis=1))).astype(jnp.int32)
    return (segment, position)

def gelu_tanh(value):
    return jax.nn.gelu(value, approximate=True)

def reference(block_input, out_cotangent, seq_lengths, q_weight, k_weight, v_weight, o_weight, gate_weight, up_weight, down_weight, attn_in_gain, attn_out_gain, ffn_in_gain, ffn_out_gain, query_gain, key_gain):
    g_ai = attn_in_gain.astype(jnp.float32)
    g_ao = attn_out_gain.astype(jnp.float32)
    g_fi = ffn_in_gain.astype(jnp.float32)
    g_fo = ffn_out_gain.astype(jnp.float32)
    g_q = query_gain.astype(jnp.float32)
    g_k = key_gain.astype(jnp.float32)
    scaling = HD ** (-0.5)
    inputs = block_input.reshape(N_SHARD, LENGTH, D)
    cotangents = out_cotangent.reshape(N_SHARD, LENGTH, D)

    def one_row(carry, items):
        x_row, dy_row, lengths = items
        segment, position = layout(lengths, LENGTH)
        index = jnp.arange(LENGTH).astype(jnp.int32)
        allowed = (segment[:, None] == segment[None, :]) & (index[None, :] <= index[:, None])
        cosine, sine = rope_tables(position)
        unit1, r1 = norm_parts(x_row)
        xn1 = (unit1 * g_ai).astype(jnp.bfloat16)
        qp = dot_plain(xn1, q_weight).reshape(LENGTH, HEADS, HD)
        qunit, rq = norm_parts(qp)
        queries = rotate(qunit * g_q, cosine[:, None, :], sine[:, None, :]).astype(jnp.bfloat16)
        kp = dot_plain(xn1, k_weight)
        kunit, rk = norm_parts(kp)
        keys = rotate(kunit * g_k, cosine, sine).astype(jnp.bfloat16)
        values = dot_plain(xn1, v_weight).astype(jnp.bfloat16)

        def scores(query_head):
            raw = dot_last(query_head, keys) * scaling
            return jnp.where(allowed, raw, -1e+30)

        def head_forward(query_head):
            logits = scores(query_head)
            peak = lax.optimization_barrier(jnp.max(logits, axis=1, keepdims=True))
            lse = peak + jnp.log(lax.optimization_barrier(jnp.sum(jnp.exp(logits - peak), axis=1, keepdims=True)))
            weights = jnp.exp(logits - lse).astype(jnp.bfloat16)
            return (dot_plain(weights, values), lse)
        queries_t = jnp.transpose(queries, (1, 0, 2))
        head_out, lses = lax.map(head_forward, queries_t)
        attended = jnp.transpose(head_out, (1, 0, 2)).reshape(LENGTH, HEADS * HD).astype(jnp.bfloat16)
        proj = dot_last(attended, o_weight)
        aunit, ra = norm_parts(proj)
        h1 = x_row + aunit * g_ao
        unit2, r2 = norm_parts(h1)
        xn2 = (unit2 * g_fi).astype(jnp.bfloat16)
        gate = dot_plain(xn2, gate_weight)
        up = dot_plain(xn2, up_weight)
        act, gelu_back = jax.vjp(gelu_tanh, gate)
        hidden = (act * up).astype(jnp.bfloat16)
        ffn = dot_last(hidden, down_weight)
        funit, rf = norm_parts(ffn)
        out_row = h1 + funit * g_fo
        dg_fo = lax.optimization_barrier(jnp.sum(dy_row * funit, axis=0))
        dffn = norm_back(dy_row * g_fo, funit, rf).astype(jnp.bfloat16)
        dhid = dot_plain(dffn, down_weight)
        d_down = dot_first(dffn, hidden)
        dup = (dhid * act).astype(jnp.bfloat16)
        dgate = gelu_back(dhid * up)[0].astype(jnp.bfloat16)
        d_gate_w = dot_first(xn2, dgate)
        d_up_w = dot_first(xn2, dup)
        dxn2 = dot_last(dgate, gate_weight) + dot_last(dup, up_weight)
        dg_fi = lax.optimization_barrier(jnp.sum(dxn2 * unit2, axis=0))
        dh1 = dy_row + norm_back(dxn2 * g_fi, unit2, r2)
        dg_ao = lax.optimization_barrier(jnp.sum(dh1 * aunit, axis=0))
        dproj = norm_back(dh1 * g_ao, aunit, ra).astype(jnp.bfloat16)
        d_o_w = dot_first(dproj, attended)
        dattended = dot_plain(dproj, o_weight).astype(jnp.bfloat16)

        def head_backward(acc, items_head):
            query_head, out_head, dout_head, lse = items_head
            logits = scores(query_head)
            weights = jnp.exp(logits - lse)
            weights_low = weights.astype(jnp.bfloat16)
            delta = lax.optimization_barrier(jnp.sum(dout_head.astype(jnp.float32) * out_head.astype(jnp.float32), axis=1, keepdims=True))
            dprob = dot_last(dout_head, values)
            dscore = (weights * (dprob - delta) * scaling).astype(jnp.bfloat16)
            dq_head = dot_plain(dscore, keys)
            return ((acc[0] + dot_first(dscore, query_head), acc[1] + dot_first(weights_low, dout_head)), dq_head)
        out_t = jnp.transpose(attended.reshape(LENGTH, HEADS, HD), (1, 0, 2))
        dout_t = jnp.transpose(dattended.reshape(LENGTH, HEADS, HD), (1, 0, 2))
        start = (jnp.zeros((LENGTH, HD), jnp.float32), jnp.zeros((LENGTH, HD), jnp.float32))
        (dkeys, dvalues), dq_t = lax.scan(head_backward, start, (queries_t, out_t, dout_t, lses))
        dq = jnp.transpose(dq_t, (1, 0, 2))
        dqn = unrotate(dq, cosine[:, None, :], sine[:, None, :])
        dg_q = lax.optimization_barrier(jnp.sum(dqn * qunit, axis=(0, 1)))
        dqp = norm_back(dqn * g_q, qunit, rq).reshape(LENGTH, HEADS * HD).astype(jnp.bfloat16)
        dkn = unrotate(dkeys, cosine, sine)
        dg_k = lax.optimization_barrier(jnp.sum(dkn * kunit, axis=0))
        dkp = norm_back(dkn * g_k, kunit, rk).astype(jnp.bfloat16)
        dvr = dvalues.astype(jnp.bfloat16)
        dxn1 = dot_last(dqp, q_weight) + dot_last(dkp, k_weight) + dot_last(dvr, v_weight)
        d_q_w = dot_first(xn1, dqp)
        d_k_w = dot_first(xn1, dkp)
        d_v_w = dot_first(xn1, dvr)
        dg_ai = lax.optimization_barrier(jnp.sum(dxn1 * unit1, axis=0))
        dx_row = dh1 + norm_back(dxn1 * g_ai, unit1, r1)
        terms = (d_q_w, d_k_w, d_v_w, d_o_w, d_gate_w, d_up_w, d_down, dg_ai, dg_ao, dg_fi, dg_fo, dg_q, dg_k)
        carry = tuple((total + term for total, term in zip(carry, terms)))
        return (carry, (out_row, dx_row))
    shapes = [q_weight, k_weight, v_weight, o_weight, gate_weight, up_weight, down_weight, attn_in_gain, attn_out_gain, ffn_in_gain, ffn_out_gain, query_gain, key_gain]
    start = tuple((jnp.zeros(item.shape, jnp.float32) for item in shapes))
    grads, (outs, dxs) = lax.scan(one_row, start, (inputs, cotangents, seq_lengths))
    block_output = outs.reshape(TOKENS, D)
    input_grad = dxs.reshape(TOKENS, D)
    return (block_output, input_grad, grads[0], grads[1], grads[2], grads[3], grads[4], grads[5], grads[6], grads[7], grads[8], grads[9], grads[10], grads[11], grads[12])
```

```python
import functools

import jax
import jax.numpy as jnp
from jax import lax
from jax.experimental import pallas as pl
from jax.experimental.pallas import tpu as pltpu
from jax.sharding import PartitionSpec as P

HD = 256


eps = 1e-06
rope_base = 1000000.0


def dot_plain(left, right):
    return jnp.dot(left, right, preferred_element_type=jnp.float32)


def dot_last(left, right):
    return lax.dot_general(
        left, right, (((1,), (1,)), ((), ())), preferred_element_type=jnp.float32
    )


def dot_first(left, right):
    return lax.dot_general(
        left, right, (((0,), (0,)), ((), ())), preferred_element_type=jnp.float32
    )


def norm_parts(value):
    scale = lax.rsqrt(jnp.mean(value * value, axis=-1, keepdims=True) + eps)
    return (value * scale, scale)


def norm_back(dnormed, unit, scale):
    return scale * (dnormed - unit * jnp.mean(dnormed * unit, axis=-1, keepdims=True))


def rope_tables(position):
    freq = rope_base ** (-jnp.arange(HD // 2).astype(jnp.float32) * (2.0 / HD))
    angle = position.astype(jnp.float32)[:, None] * freq[None, :]
    return (jnp.cos(angle), jnp.sin(angle))


def rotate(value, cosine, sine):
    half = value.shape[-1] // 2
    first, second = (value[..., :half], value[..., half:])
    return jnp.concatenate(
        [first * cosine - second * sine, second * cosine + first * sine], axis=-1
    )


def unrotate(value, cosine, sine):
    half = value.shape[-1] // 2
    first, second = (value[..., :half], value[..., half:])
    return jnp.concatenate(
        [first * cosine + second * sine, second * cosine - first * sine], axis=-1
    )


def layout(lengths, count):
    index = jnp.arange(count)
    order = jnp.arange(lengths.shape[0])
    ends = jnp.sum(jnp.where(order[None, :] <= order[:, None], lengths[None, :], 0), axis=1)
    after = (index[:, None] >= ends[None, :]).astype(jnp.int32)
    segment = jnp.sum(after, axis=1)
    position = index - jnp.sum(after * lengths[None, :], axis=1)
    return (segment, position)


def gelu_tanh(value):
    return jax.nn.gelu(value, approximate=True)


def masked_scores(query_head, key_block, mask, scaling):
    raw = dot_last(query_head, key_block) * scaling
    return jnp.where(mask, raw, -1e30)

MESH = pl.DeviceIdType.MESH
LANES = 128
WAYS = 4


def vmem():
    return pl.BlockSpec(memory_space=pltpu.VMEM)


def greet(peers):
    barrier = pltpu.get_barrier_semaphore()
    for peer in peers:
        pl.semaphore_signal(barrier, inc=1, device_id=peer, device_id_type=MESH)
    pl.semaphore_wait(barrier, len(peers))


def params(number):
    return pltpu.CompilerParams(
        collective_id=number, has_side_effects=True, vmem_limit_bytes=56 * 1024 * 1024
    )


def send(src, dst, sems, where, peer):
    copy = pltpu.make_async_remote_copy(
        src_ref=src,
        dst_ref=dst,
        send_sem=sems[0].at[where],
        recv_sem=sems[1].at[where],
        device_id=peer,
        device_id_type=MESH,
    )
    copy.start()
    return copy


def place(n_ctx):
    shard, ctx, tp = (lax.axis_index("shard"), lax.axis_index("ctx"), lax.axis_index("tp"))
    core = lax.rem(ctx, 2)
    high = lax.rem(lax.div(ctx, 2), 2)
    return shard, ctx, tp, ctx + 1 - 2 * core, ctx + 2 - 4 * high


def columns(member, width):
    return pl.ds(pl.multiple_of(member * width, LANES), width)


def block_rows(index, count):
    return pl.ds(pl.multiple_of(index * count, 8), count)


def gather_kernel(n_shard, n_ctx, count, *refs):
    weights, unit, gain = (refs[:count], refs[count], refs[count + 1])
    refs = refs[count + 2 :]
    outs, row, gains = (refs[:count], refs[count], refs[count + 1])
    sems_a, sems_n, sems_f, sems_c, sems_x, sems_g, local = (
        refs[count + 2 : count + 4],
        refs[count + 4 : count + 6],
        refs[count + 6 : count + 8],
        refs[count + 8 : count + 10],
        refs[count + 10 : count + 12],
        refs[count + 12 : count + 14],
        refs[count + 14],
    )
    shard, ctx, tp, near, far = place(n_ctx)
    member = lax.rem(ctx, WAYS)
    rows = weights[0].shape[0]
    tokens = unit.shape[0]
    widths = [item.shape[1] // WAYS for item in weights]
    peers = [(lax.rem(shard + d, n_shard), ctx, tp) for d in range(1, n_shard)]
    mates = [(shard, lax.rem(ctx + d, n_ctx), tp) for d in range(1, n_ctx)]
    greet(peers + mates)
    started = []
    first = {}
    for d in range(1, n_shard):
        for a in range(count):
            cols = columns(member, widths[a])
            first[d, a] = send(
                weights[a].at[:, cols],
                outs[a].at[block_rows(shard, rows), cols],
                sems_a,
                (d - 1, a),
                peers[d - 1],
            )
        started.append(send(gain, gains.at[shard], sems_g, d - 1, peers[d - 1]))
    for d in range(1, n_ctx):
        started.append(
            send(unit, row.at[block_rows(ctx, tokens)], sems_x, d - 1, mates[d - 1])
        )
    own = [
        pltpu.make_async_copy(weights[a], outs[a].at[block_rows(shard, rows)], local.at[a])
        for a in range(count)
    ]
    own.append(pltpu.make_async_copy(unit, row.at[block_rows(ctx, tokens)], local.at[count]))
    own.append(pltpu.make_async_copy(gain, gains.at[shard], local.at[count + 1]))
    for item in own:
        item.start()
    across = {}
    other = lax.rem(far, WAYS)

    def relay(d):
        source = lax.rem(shard - d + n_shard, n_shard)
        for a in range(count):
            across[d, a].wait_recv()
            block = outs[a].at[block_rows(source, rows), columns(other, widths[a])]
            started.append(send(block, block, sems_c, (d - 1, a), (shard, near, tp)))

    for d in range(1, n_shard):
        source = lax.rem(shard - d + n_shard, n_shard)
        for a in range(count):
            first[d, a].wait_recv()
            block = outs[a].at[block_rows(source, rows), columns(member, widths[a])]
            across[d, a] = send(block, block, sems_f, (d - 1, a), (shard, far, tp))
            started.append(send(block, block, sems_n, (d - 1, a), (shard, near, tp)))
        if d > 1:
            relay(d - 1)
    relay(n_shard - 1)
    for item in started:
        item.wait()
    for item in list(first.values()) + list(across.values()):
        item.wait_send()
    for item in own:
        item.wait()


def gather_all(n_shard, n_ctx, weights, unit, gain):
    count = len(weights)
    grid = pltpu.SemaphoreType.DMA((n_shard - 1, count))
    return pl.pallas_call(
        functools.partial(gather_kernel, n_shard, n_ctx, count),
        out_shape=[
            jax.ShapeDtypeStruct((item.shape[0] * n_shard, item.shape[1]), item.dtype)
            for item in weights
        ]
        + [
            jax.ShapeDtypeStruct((unit.shape[0] * n_ctx, unit.shape[1]), unit.dtype),
            jax.ShapeDtypeStruct((n_shard,) + gain.shape, gain.dtype),
        ],
        in_specs=[vmem()] * (count + 2),
        out_specs=[vmem()] * (count + 2),
        scratch_shapes=[grid] * 8
        + [pltpu.SemaphoreType.DMA((n_ctx - 1,))] * 2
        + [pltpu.SemaphoreType.DMA((n_shard - 1,))] * 2
        + [pltpu.SemaphoreType.DMA((count + 2,))],
        compiler_params=params(0),
        name="gather_all",
    )(*weights, unit, gain)


def tp_kernel(n_tp, part, out, inbox, send_sem, recv_sem):
    shard, ctx, tp = (lax.axis_index("shard"), lax.axis_index("ctx"), lax.axis_index("tp"))
    peers = [(shard, ctx, lax.rem(tp + d, n_tp)) for d in range(1, n_tp)]
    greet(peers)
    copies = [
        send(part, inbox.at[d - 1], (send_sem, recv_sem), d - 1, peers[d - 1])
        for d in range(1, n_tp)
    ]
    total = part[...].astype(jnp.float32)
    for d in range(1, n_tp):
        copies[d - 1].wait_recv()
        total = total + inbox[d - 1].astype(jnp.float32)
    out[...] = total
    for copy in copies:
        copy.wait_send()


def tp_sum(value, n_tp, number):
    part = value.astype(jnp.bfloat16)
    return pl.pallas_call(
        functools.partial(tp_kernel, n_tp),
        out_shape=jax.ShapeDtypeStruct(part.shape, jnp.float32),
        in_specs=[vmem()],
        out_specs=vmem(),
        scratch_shapes=[
            pltpu.VMEM((n_tp - 1,) + part.shape, jnp.bfloat16),
            pltpu.SemaphoreType.DMA((n_tp - 1,)),
            pltpu.SemaphoreType.DMA((n_tp - 1,)),
        ],
        compiler_params=params(number),
        name=f"tp_sum{number}",
    )(part)


def tail_kernel(n_shard, n_ctx, n_tp, early, *refs):
    ready = refs[:early]
    (terms, dqp, qw, kvw, xn1_t, cosine, sine, kunit, rk, g_k, unit1, r1, g_ai, dh1, gain) = refs[
        early : early + 15
    ]
    refs = refs[early + 15 :]
    count = early + 2
    kv_at = count - 1
    outs, gain_out, input_grad = (refs[: count + 1], refs[count + 1], refs[count + 2])
    (late_q, late_kv, dkv_in, part, part_in) = refs[count + 3 : count + 8]
    (half, away, inbox, mine, arrived, done, kv_in, groups_in, shared) = refs[
        count + 8 : count + 17
    ]
    (g_own, g_near, g_far, g_mid, g_shard, g_group, g_tp) = refs[count + 17 : count + 24]
    sems = refs[count + 24 :]
    pair = [(sems[2 * k], sems[2 * k + 1]) for k in range(len(sems) // 2)]
    (
        s_core,
        s_far,
        s_shard,
        s_group,
        s_kv,
        s_share,
        s_gain,
        s_gz,
        s_gg,
        s_gt,
        s_dkv,
        s_part,
    ) = pair
    grads = list(ready) + [late_q, late_kv]
    shard, ctx, tp, near, far = place(n_ctx)
    n_groups = n_ctx // WAYS
    group = lax.div(ctx, WAYS)
    member, other = (lax.rem(ctx, WAYS), lax.rem(far, WAYS))
    beside = lax.rem(near, WAYS)
    opposite = beside + other - member
    rows = outs[0].shape[0]
    tokens = dqp.shape[0]
    widths = [item.shape[1] // WAYS for item in grads]
    starts = [sum(widths[:a]) for a in range(count)]
    batches = (list(range(early)), [early, early + 1])
    spans = (
        pl.ds(0, starts[early]),
        pl.ds(starts[early], widths[early] + widths[early + 1]),
    )
    near_id, far_id = ((shard, near, tp), (shard, far, tp))
    z_ids = [(lax.rem(shard + d, n_shard), ctx, tp) for d in range(1, n_shard)]
    c_ids = [(shard, lax.rem(ctx + d, n_ctx), tp) for d in range(1, n_ctx)]
    g_ids = [(shard, lax.rem(ctx + WAYS * d, n_ctx), tp) for d in range(1, n_groups)]
    t_ids = [(shard, ctx, lax.rem(tp + d, n_tp)) for d in range(1, n_tp)]
    greet(z_ids + c_ids + t_ids)

    ends = []
    core = {}
    over = {}
    along = {}
    order = list(range(1, n_shard)) + [0]
    targets = [lax.rem(shard + d, n_shard) for d in range(n_shard)]

    def start_core(batch):
        for slot, quarter in ((1, opposite), (0, beside)):
            for d in order:
                where = block_rows(targets[d], rows)
                for a in batches[batch]:
                    core[slot, a, d] = send(
                        grads[a].at[where, columns(quarter, widths[a])],
                        half.at[slot, where, pl.ds(starts[a], widths[a])],
                        s_core,
                        (slot, a, d),
                        near_id,
                    )

    def start_over(batch):
        for d in order:
            where = block_rows(targets[d], rows)
            for a in batches[batch]:
                core[1, a, d].wait_recv()
                cols = pl.ds(starts[a], widths[a])
                total = half[1, where, cols].astype(jnp.float32) + grads[a][
                    where, columns(other, widths[a])
                ].astype(jnp.float32)
                away[where, cols] = total.astype(jnp.bfloat16)
            over[batch, d] = send(
                away.at[where, spans[batch]],
                inbox.at[where, spans[batch]],
                s_far,
                (batch, d),
                far_id,
            )

    def start_along(batch):
        for d in order:
            where = block_rows(targets[d], rows)
            over[batch, d].wait_recv()
            for a in batches[batch]:
                core[0, a, d].wait_recv()
                cols = pl.ds(starts[a], widths[a])
                total = (
                    half[0, where, cols].astype(jnp.float32)
                    + grads[a][where, columns(member, widths[a])].astype(jnp.float32)
                    + inbox[where, cols].astype(jnp.float32)
                )
                mine[where, cols] = total.astype(jnp.bfloat16)
            if d:
                along[batch, d] = send(
                    mine.at[where, spans[batch]],
                    arrived.at[d - 1, :, spans[batch]],
                    s_shard,
                    (batch, d - 1),
                    z_ids[d - 1],
                )

    def finish(batch):
        span = spans[batch]
        total = mine[block_rows(shard, rows), span].astype(jnp.float32)
        for d in range(1, n_shard):
            along[batch, d].wait_recv()
            total = total + arrived[d - 1, :, span].astype(jnp.float32)
        if n_groups > 1:
            groups_in[group, :, span] = total.astype(jnp.bfloat16)
            piece = groups_in.at[group, :, span]
            moved = [
                send(piece, piece, s_group, (batch, d - 1), g_ids[d - 1])
                for d in range(1, n_groups)
            ]
            for item in moved:
                item.wait_recv()
            ends.extend(moved)
            total = groups_in[0, :, span].astype(jnp.float32)
            for g in range(1, n_groups):
                total = total + groups_in[g, :, span].astype(jnp.float32)
        return total.astype(jnp.bfloat16)

    def start_share(batch):
        piece = shared.at[member, :, spans[batch]]
        return (
            send(piece, piece, s_share, (batch, 0), far_id),
            send(piece, piece, s_share, (batch, 1), near_id),
        )

    def relay_share(batch, first):
        first[0].wait_recv()
        piece = shared.at[other, :, spans[batch]]
        return send(piece, piece, s_share, (batch, 2), near_id)

    scatter = [
        send(
            terms.at[block_rows(c_ids[d - 1][1], tokens)],
            dkv_in.at[d - 1],
            s_dkv,
            d - 1,
            c_ids[d - 1],
        )
        for d in range(1, n_ctx)
    ]
    start_core(0)
    late_q[...] = dot_plain(xn1_t[...], dqp[...]).astype(jnp.bfloat16)
    start_over(0)
    dxn1 = dot_last(dqp[...], qw[...])
    dkv = terms[block_rows(ctx, tokens), :].astype(jnp.float32)
    for d in range(1, n_ctx):
        scatter[d - 1].wait_recv()
        dkv = dkv + dkv_in[d - 1].astype(jnp.float32)
    dkn = unrotate(dkv[:, :HD], cosine[...], sine[...])
    dg_k = jnp.sum(dkn * kunit[...], axis=0, keepdims=True)
    dkp = norm_back(dkn * g_k[...], kunit[...], rk[...]).astype(jnp.bfloat16)
    dkvp = jnp.concatenate([dkp, dkv[:, HD:].astype(jnp.bfloat16)], axis=1)
    part[...] = (dxn1 + dot_last(dkvp, kvw[...])).astype(jnp.bfloat16)
    parts = [
        send(part, part_in.at[d - 1], s_part, d - 1, t_ids[d - 1]) for d in range(1, n_tp)
    ]
    late_kv[...] = dot_plain(xn1_t[...], dkvp).astype(jnp.bfloat16)
    start_core(1)
    dxn1 = part[...].astype(jnp.float32)
    for d in range(1, n_tp):
        parts[d - 1].wait_recv()
        dxn1 = dxn1 + part_in[d - 1].astype(jnp.float32)
    dg_ai = jnp.sum(dxn1 * unit1[...], axis=0, keepdims=True) * (1.0 / n_tp)
    input_grad[...] = dh1[...] + norm_back(dxn1 * g_ai[...], unit1[...], r1[...])
    g_own[...] = gain[...]
    at = 0
    for line in (dg_ai, dg_k):
        for k in range(line.shape[1] // LANES):
            g_own[pl.ds(at, 1), :] = line[:, k * LANES : (k + 1) * LANES]
            at = at + 1
    gain_near = send(g_own, g_near, s_gain, 0, near_id)
    start_over(1)
    gain_near.wait_recv()
    g_mid[0] = g_own[...] + g_near[...]
    gain_far = send(g_mid.at[0], g_far, s_gain, 1, far_id)

    start_along(0)
    gain_far.wait_recv()
    g_shard[shard] = g_mid[0] + g_far[...]
    gz = [
        send(g_shard.at[shard], g_shard.at[shard], s_gz, d - 1, z_ids[d - 1])
        for d in range(1, n_shard)
    ]
    start_along(1)
    shared[member, :, spans[0]] = finish(0)
    share0 = start_share(0)

    for item in gz:
        item.wait_recv()
    total = g_shard[0]
    for k in range(1, n_shard):
        total = total + g_shard[k]
    g_group[group] = total
    gg = [
        send(g_group.at[group], g_group.at[group], s_gg, d - 1, g_ids[d - 1])
        for d in range(1, n_groups)
    ]
    for item in gg:
        item.wait_recv()
    total = g_group[0]
    for k in range(1, n_groups):
        total = total + g_group[k]
    g_tp[tp] = total
    gt = [
        send(g_tp.at[tp], g_tp.at[tp], s_gt, d - 1, t_ids[d - 1]) for d in range(1, n_tp)
    ]

    done[...] = finish(1)
    kv_cols = pl.ds(widths[early], widths[kv_at])
    kvs = [
        send(done.at[:, kv_cols], kv_in.at[d - 1], s_kv, d - 1, t_ids[d - 1])
        for d in range(1, n_tp)
    ]
    relay0 = relay_share(0, share0)
    shared[member, :, pl.ds(starts[early], widths[early])] = done[:, pl.ds(0, widths[early])]
    total = done[:, kv_cols].astype(jnp.float32)
    for d in range(1, n_tp):
        kvs[d - 1].wait_recv()
        total = total + kv_in[d - 1].astype(jnp.float32)
    shared[member, :, pl.ds(starts[kv_at], widths[kv_at])] = total.astype(jnp.bfloat16)
    share1 = start_share(1)
    for item in gt:
        item.wait_recv()
    total = g_tp[0]
    for k in range(1, n_tp):
        total = total + g_tp[k]
    gain_out[...] = total

    def write(batch):
        for q in range(WAYS):
            for a in batches[batch]:
                value = shared[q, :, pl.ds(starts[a], widths[a])]
                if a == kv_at:
                    out = outs[a] if q < WAYS // 2 else outs[count]
                    out[:, pl.ds((q % (WAYS // 2)) * widths[a], widths[a])] = value
                else:
                    outs[a][:, pl.ds(q * widths[a], widths[a])] = value

    share0[1].wait_recv()
    relay0.wait_recv()
    write(0)
    relay1 = relay_share(1, share1)
    share1[1].wait_recv()
    relay1.wait_recv()
    write(1)
    ends.extend(scatter + parts + list(core.values()) + list(over.values()))
    ends.extend(list(along.values()) + kvs + gz + gg + gt + [gain_near, gain_far])
    ends.extend(list(share0) + list(share1) + [relay0, relay1])
    for item in ends:
        item.wait_send()


def run_tail(n_shard, n_ctx, n_tp, ready, terms, dqp, qw, kvw, xn1_t, small, dh1, gain):
    deep = qw.shape[0]
    tokens = dqp.shape[0]
    rows = deep // n_shard
    n_groups = n_ctx // WAYS
    early = len(ready)
    count = early + 2
    late = (qw.shape[1], kvw.shape[1])
    wide = sum([item.shape[1] // WAYS for item in ready]) + sum(late) // WAYS
    out_widths = [item.shape[1] for item in ready] + [late[0], late[1] // 2, late[1] // 2]
    low, full = (jnp.bfloat16, jnp.float32)
    operands = (*ready, terms, dqp, qw, kvw, xn1_t, *small, dh1, gain)

    def dma(*shape):
        return [pltpu.SemaphoreType.DMA(shape)] * 2

    return pl.pallas_call(
        functools.partial(tail_kernel, n_shard, n_ctx, n_tp, early),
        out_shape=[jax.ShapeDtypeStruct((rows, item), low) for item in out_widths]
        + [jax.ShapeDtypeStruct(gain.shape, full), jax.ShapeDtypeStruct(dh1.shape, full)],
        in_specs=[vmem()] * len(operands),
        out_specs=[vmem()] * (count + 3),
        scratch_shapes=[
            pltpu.VMEM((deep, late[0]), low),
            pltpu.VMEM((deep, late[1]), low),
            pltpu.VMEM((n_ctx - 1, tokens, terms.shape[1]), low),
            pltpu.VMEM((tokens, deep), low),
            pltpu.VMEM((n_tp - 1, tokens, deep), low),
            pltpu.VMEM((2, deep, wide), low),
            pltpu.VMEM((deep, wide), low),
            pltpu.VMEM((deep, wide), low),
            pltpu.VMEM((deep, wide), low),
            pltpu.VMEM((n_shard - 1, rows, wide), low),
            pltpu.VMEM((rows, sum(late) // WAYS), low),
            pltpu.VMEM((n_tp - 1, rows, late[1] // WAYS), low),
            pltpu.VMEM((n_groups, rows, wide), low),
            pltpu.VMEM((WAYS, rows, wide), low),
            pltpu.VMEM(gain.shape, full),
            pltpu.VMEM(gain.shape, full),
            pltpu.VMEM(gain.shape, full),
            pltpu.VMEM((1,) + gain.shape, full),
            pltpu.VMEM((n_shard,) + gain.shape, full),
            pltpu.VMEM((n_groups,) + gain.shape, full),
            pltpu.VMEM((n_tp,) + gain.shape, full),
        ]
        + dma(2, count, n_shard)
        + dma(2, n_shard)
        + dma(2, n_shard - 1)
        + dma(2, max(n_groups - 1, 1))
        + dma(n_tp - 1)
        + dma(2, 3)
        + dma(2)
        + dma(n_shard - 1)
        + dma(max(n_groups - 1, 1))
        + dma(n_tp - 1)
        + dma(n_ctx - 1)
        + dma(n_tp - 1),
        compiler_params=params(6),
        name="tail",
    )(*operands)


def pack_lanes(items):
    flat = jnp.concatenate([item.astype(jnp.float32) for item in items])
    unit = 8 * LANES
    short = -flat.shape[0] % unit
    return jnp.pad(flat, (0, short)).reshape(-1, LANES)


def per_device(
    block_input,
    out_cotangent,
    seq_lengths,
    q_weight,
    k_weight,
    v_weight,
    o_weight,
    gate_weight,
    up_weight,
    down_weight,
    attn_in_gain,
    attn_out_gain,
    ffn_in_gain,
    ffn_out_gain,
    query_gain,
    key_gain,
):
    tokens = block_input.shape[0]
    width = block_input.shape[1]
    n_ctx = lax.axis_size("ctx")
    n_tp = lax.axis_size("tp")
    row_len = tokens * n_ctx
    n_shard = lax.axis_size("shard")
    my_start = lax.axis_index("ctx") * tokens
    scaling = HD ** (-0.5)
    segment, position = layout(seq_lengths[0], row_len)
    key_index = jnp.arange(row_len)
    query_index = my_start + jnp.arange(tokens)
    query_seg = lax.dynamic_slice_in_dim(segment, my_start, tokens)
    allowed = (query_seg[:, None] == segment[None, :]) & (
        key_index[None, :] <= query_index[:, None]
    )
    row_cosine, row_sine = rope_tables(position)
    cosine = lax.dynamic_slice_in_dim(row_cosine, my_start, tokens)
    sine = lax.dynamic_slice_in_dim(row_sine, my_start, tokens)
    unit1, r1 = norm_parts(block_input)
    gains = (attn_in_gain, attn_out_gain, ffn_in_gain, ffn_out_gain, query_gain, key_gain)
    qw, kvw, ow, gw, uw, dw, unit_row, packed = gather_all(
        n_shard,
        n_ctx,
        (
            q_weight,
            jnp.concatenate([k_weight, v_weight], axis=1),
            o_weight,
            gate_weight,
            up_weight,
            down_weight,
        ),
        unit1.astype(jnp.bfloat16),
        pack_lanes(gains),
    )
    packed = packed.reshape(n_shard, -1)
    split = []
    at = 0
    for item in gains:
        split.append(packed[:, at : at + item.shape[0]].reshape(-1))
        at = at + item.shape[0]
    g_ai, g_ao, g_fi, g_fo, g_q, g_k = split
    local_heads = qw.shape[1] // HD
    xn1 = (unit1 * g_ai).astype(jnp.bfloat16)
    qp = dot_plain(xn1, qw).reshape(tokens, local_heads, HD)
    qunit, rq = norm_parts(qp)
    queries = rotate(qunit * g_q, cosine[:, None, :], sine[:, None, :]).astype(jnp.bfloat16)
    xn1_row = (unit_row.astype(jnp.float32) * g_ai).astype(jnp.bfloat16)
    kvp = dot_plain(xn1_row, kvw)
    row_kunit, row_rk = norm_parts(kvp[:, :HD])
    row_keys = rotate(row_kunit * g_k, row_cosine, row_sine).astype(jnp.bfloat16)
    row_values = kvp[:, HD:].astype(jnp.bfloat16)
    kunit = lax.dynamic_slice_in_dim(row_kunit, my_start, tokens)
    rk = lax.dynamic_slice_in_dim(row_rk, my_start, tokens)
    head_outs = []
    lses = []
    for head in range(local_heads):
        logits = masked_scores(queries[:, head, :], row_keys, allowed, scaling)
        peak = jnp.max(logits, axis=1, keepdims=True)
        lse = peak + jnp.log(jnp.sum(jnp.exp(logits - peak), axis=1, keepdims=True))
        weights = jnp.exp(logits - lse).astype(jnp.bfloat16)
        head_outs.append(dot_plain(weights, row_values))
        lses.append(lse)
    attended = jnp.concatenate(head_outs, axis=1).astype(jnp.bfloat16)
    proj = tp_sum(dot_last(attended, ow), n_tp, 1)
    aunit, ra = norm_parts(proj)
    h1 = block_input + aunit * g_ao
    unit2, r2 = norm_parts(h1)
    xn2 = (unit2 * g_fi).astype(jnp.bfloat16)
    gate = dot_plain(xn2, gw)
    up = dot_plain(xn2, uw)
    act, gelu_back = jax.vjp(gelu_tanh, gate)
    hidden = (act * up).astype(jnp.bfloat16)
    ffn = tp_sum(dot_last(hidden, dw), n_tp, 2)
    funit, rf = norm_parts(ffn)
    block_output = h1 + funit * g_fo
    back_keys, back_values = (row_keys, row_values)
    dg_fo = jnp.sum(out_cotangent * funit, axis=0)
    dffn = norm_back(out_cotangent * g_fo, funit, rf).astype(jnp.bfloat16)
    dhid = dot_plain(dffn, dw)
    d_down = dot_first(dffn, hidden)
    dup = (dhid * act).astype(jnp.bfloat16)
    dgate = gelu_back(dhid * up)[0].astype(jnp.bfloat16)
    d_gate_w = dot_first(xn2, dgate)
    d_up_w = dot_first(xn2, dup)
    dxn2 = tp_sum(dot_last(dgate, gw) + dot_last(dup, uw), n_tp, 3)
    dg_fi = jnp.sum(dxn2 * unit2, axis=0)
    dh1 = out_cotangent + norm_back(dxn2 * g_fi, unit2, r2)
    dg_ao = jnp.sum(dh1 * aunit, axis=0)
    dproj = norm_back(dh1 * g_ao, aunit, ra).astype(jnp.bfloat16)
    d_o_w = dot_first(dproj, attended)
    dattended = dot_plain(dproj, ow).astype(jnp.bfloat16)
    win_keys, win_values, win_allowed = (back_keys, back_values, allowed)
    key_terms = jnp.zeros((row_len, HD), jnp.float32)
    value_terms = jnp.zeros((row_len, HD), jnp.float32)
    dq_parts = []
    for head in range(local_heads):
        query_head = queries[:, head, :]
        out_head = attended[:, head * HD : (head + 1) * HD]
        dout_head = dattended[:, head * HD : (head + 1) * HD]
        logits = masked_scores(query_head, win_keys, win_allowed, scaling)
        weights = jnp.exp(logits - lses[head])
        weights_low = weights.astype(jnp.bfloat16)
        delta = jnp.sum(
            dout_head.astype(jnp.float32) * out_head.astype(jnp.float32), axis=1, keepdims=True
        )
        dprob = dot_last(dout_head, win_values)
        dscore = (weights * (dprob - delta) * scaling).astype(jnp.bfloat16)
        dq_parts.append(dot_plain(dscore, win_keys))
        key_terms = key_terms + dot_first(dscore, query_head)
        value_terms = value_terms + dot_first(weights_low, dout_head)
    dq = jnp.stack(dq_parts, axis=1)
    dqn = unrotate(dq, cosine[:, None, :], sine[:, None, :])
    dg_q = jnp.sum(dqn * qunit, axis=(0, 1))
    dqp = norm_back(dqn * g_q, qunit, rq).reshape(tokens, local_heads * HD).astype(jnp.bfloat16)
    terms = jnp.concatenate([key_terms, value_terms], axis=1).astype(jnp.bfloat16)
    ready = [item.astype(jnp.bfloat16) for item in (d_o_w, d_gate_w, d_up_w, d_down)]
    share = 1.0 / n_tp
    late = (jnp.zeros((width,), jnp.float32), jnp.zeros((HD,), jnp.float32))
    sums = (*late, dg_ao * share, dg_fi * share, dg_fo * share, dg_q)
    outs = run_tail(
        n_shard,
        n_ctx,
        n_tp,
        ready,
        terms,
        dqp,
        qw,
        kvw,
        xn1.T,
        (cosine, sine, kunit, rk, g_k[None, :], unit1, r1, g_ai[None, :]),
        dh1,
        pack_lanes(sums),
    )
    o_out, gate_out, up_out, down_out, q_out, k_out, v_out = [
        item.astype(jnp.float32) for item in outs[:7]
    ]
    gain_sums, input_grad = outs[7:]
    flat = gain_sums.reshape(-1)
    gain_outs = []
    at = 0
    for term in sums:
        own = term.shape[0] // n_shard
        gain_outs.append(
            lax.dynamic_slice_in_dim(flat, at + lax.axis_index("shard") * own, own)
        )
        at = at + term.shape[0]
    dg_ai, dg_k, dg_ao, dg_fi, dg_fo, dg_q = gain_outs
    return (
        block_output,
        input_grad,
        q_out,
        k_out,
        v_out,
        o_out,
        gate_out,
        up_out,
        down_out,
        dg_ai,
        dg_ao,
        dg_fi,
        dg_fo,
        dg_q,
        dg_k,
    )


def solution(mesh):
    placed = (
        P(("shard", "ctx"), None),
        P(("shard", "ctx"), None),
        P("shard", None),
        P("shard", "tp"),
        P("shard", None),
        P("shard", None),
        P("shard", "tp"),
        P("shard", "tp"),
        P("shard", "tp"),
        P("shard", "tp"),
        P("shard"),
        P("shard"),
        P("shard"),
        P("shard"),
        P("shard"),
        P("shard"),
    )
    return jax.shard_map(
        per_device,
        mesh=mesh,
        in_specs=placed,
        out_specs=(
            P(("shard", "ctx"), None),
            P(("shard", "ctx"), None),
            P("shard", "tp"),
            P("shard", None),
            P("shard", None),
            P("shard", "tp"),
            P("shard", "tp"),
            P("shard", "tp"),
            P("shard", "tp"),
            P("shard"),
            P("shard"),
            P("shard"),
            P("shard"),
            P("shard"),
            P("shard"),
        ),
        check_vma=False,
    )
```

```python
import functools

import jax
import jax.numpy as jnp
import numpy as np
from jax import lax
from jax.experimental import pallas as pl
from jax.experimental.pallas import tpu as pltpu
from jax.sharding import PartitionSpec as P

HD = 256
MESH = pl.DeviceIdType.MESH
LANES = 128
WAYS = 4
TILE = 256
LOW, FULL = (jnp.bfloat16, jnp.float32)

eps = 1e-06
rope_base = 1000000.0
gelu_c = 0.7978845608028654
gelu_k = 0.044715


def dot_plain(left, right):
    return jnp.dot(left, right, preferred_element_type=FULL)


def dot_last(left, right):
    return lax.dot_general(
        left, right, (((1,), (1,)), ((), ())), preferred_element_type=FULL
    )


def dot_first(left, right):
    return lax.dot_general(
        left, right, (((0,), (0,)), ((), ())), preferred_element_type=FULL
    )


def norm_parts(value):
    scale = lax.rsqrt(jnp.mean(value * value, axis=-1, keepdims=True) + eps)
    return (value * scale, scale)


def norm_back(dnormed, unit, scale):
    return scale * (dnormed - unit * jnp.mean(dnormed * unit, axis=-1, keepdims=True))


def rotate(value, cosine, sine):
    half = value.shape[-1] // 2
    first, second = (value[..., :half], value[..., half:])
    return jnp.concatenate(
        [first * cosine - second * sine, second * cosine + first * sine], axis=-1
    )


def unrotate(value, cosine, sine):
    half = value.shape[-1] // 2
    first, second = (value[..., :half], value[..., half:])
    return jnp.concatenate(
        [first * cosine + second * sine, second * cosine - first * sine], axis=-1
    )


def greet(peers):
    barrier = pltpu.get_barrier_semaphore()
    for peer in peers:
        pl.semaphore_signal(barrier, inc=1, device_id=peer, device_id_type=MESH)
    pl.semaphore_wait(barrier, len(peers))


def send(src, dst, sems, where, peer):
    copy = pltpu.make_async_remote_copy(
        src_ref=src,
        dst_ref=dst,
        send_sem=sems[0].at[where],
        recv_sem=sems[1].at[where],
        device_id=peer,
        device_id_type=MESH,
    )
    copy.start()
    return copy


def columns(member, width):
    return pl.ds(pl.multiple_of(member * width, LANES), width)


def block_rows(index, count):
    return pl.ds(pl.multiple_of(index * count, 16), count)


class Sizes:
    def __init__(self, shard, ctx, tp, tokens, deep, qcols, ff, window):
        self.S, self.C, self.TP = (shard, ctx, tp)
        self.T, self.D, self.R = (tokens, deep, deep // shard)
        self.HQ, self.F, self.W = (qcols, ff, window)
        self.heads = qcols // HD
        self.groups = ctx // WAYS
        self.full = [qcols, 2 * HD, qcols, ff, ff, ff]
        self.width = [item // WAYS for item in self.full]
        self.order = [5, 3, 4, 2, 0, 1]
        self.at = {}
        total = 0
        for a in self.order:
            self.at[a] = total
            total = total + self.width[a]
        self.wide = total


class Named:
    def __init__(self, names, refs):
        for name, ref in zip(names, refs, strict=True):
            setattr(self, name, ref)


class Place:
    def __init__(self, c):
        shard, ctx, tp = (
            lax.axis_index("shard"),
            lax.axis_index("ctx"),
            lax.axis_index("tp"),
        )
        core = lax.rem(ctx, 2)
        high = lax.rem(lax.div(ctx, 2), 2)
        near, far = (ctx + 1 - 2 * core, ctx + 2 - 4 * high)
        self.shard, self.ctx, self.tp = (shard, ctx, tp)
        self.member, self.other = (lax.rem(ctx, WAYS), lax.rem(far, WAYS))
        self.beside = lax.rem(near, WAYS)
        self.opposite = self.beside + self.other - self.member
        self.group = lax.div(ctx, WAYS)
        self.near_id, self.far_id = ((shard, near, tp), (shard, far, tp))
        self.z_ids = [(lax.rem(shard + d, c.S), ctx, tp) for d in range(1, c.S)]
        self.up_ids = [(shard, lax.rem(ctx + d, c.C), tp) for d in range(1, c.C)]
        self.down_ids = [
            (shard, lax.rem(ctx - d + c.C, c.C), tp) for d in range(1, c.C)
        ]
        self.g_ids = [
            (shard, lax.rem(ctx + WAYS * d, c.C), tp) for d in range(1, c.groups)
        ]
        self.t_ids = [(shard, ctx, lax.rem(tp + d, c.TP)) for d in range(1, c.TP)]


class Gather:
    def __init__(self, c, p, k):
        self.c, self.p, self.k = (c, p, k)
        self.src = [k.q_in, None, k.o_in, k.gate_in, k.up_in, k.down_in]
        self.dst = [k.qw, k.kvw, k.ow, k.gw, k.uw, k.dw]
        self.first, self.across, self.sent, self.landing, self.own = (
            {},
            {},
            [],
            {},
            [],
        )

    def local(self, src, dst):
        copy = pltpu.make_async_copy(src, dst, self.k.local.at[len(self.own)])
        copy.start()
        self.own.append(copy)

    def start_own(self):
        c, p, k = (self.c, self.p, self.k)
        rows = block_rows(p.shard, c.R)
        self.local(k.k_in, k.kvw.at[rows, pl.ds(0, HD)])
        self.local(k.v_in, k.kvw.at[rows, pl.ds(HD, HD)])
        for a in (0, 2, 3, 4, 5):
            self.local(self.src[a], self.dst[a].at[rows])

    def start(self, a):
        c, p, k = (self.c, self.p, self.k)
        cols = columns(p.member, c.width[a])
        rows = block_rows(p.shard, c.R)
        src = self.dst[a].at[rows, cols] if a == 1 else self.src[a].at[:, cols]
        for d in range(1, c.S):
            self.first[d, a] = send(
                src,
                self.dst[a].at[rows, cols],
                (k.za_s, k.za_r),
                (d - 1, a),
                p.z_ids[d - 1],
            )

    def piece(self, d, a, member):
        c, p = (self.c, self.p)
        source = lax.rem(p.shard - d + c.S, c.S)
        return self.dst[a].at[block_rows(source, c.R), columns(member, c.width[a])]

    def relay(self, a):
        c, p, k = (self.c, self.p, self.k)
        for d in range(1, c.S):
            self.first[d, a].wait_recv()
            block = self.piece(d, a, p.member)
            self.across[d, a] = send(
                block, block, (k.fa_s, k.fa_r), (d - 1, a), p.far_id
            )
            self.landing.setdefault(a, []).append(
                send(block, block, (k.na_s, k.na_r), (d - 1, a), p.near_id)
            )

    def pass_on(self, a):
        c, p, k = (self.c, self.p, self.k)
        for d in range(1, c.S):
            self.across[d, a].wait_recv()
            block = self.piece(d, a, p.other)
            self.landing[a].append(
                send(block, block, (k.ca_s, k.ca_r), (d - 1, a), p.near_id)
            )

    def ready(self, a):
        for item in self.landing[a]:
            item.wait_recv()

    def end(self):
        for group in (self.first.values(), self.across.values(), *self.landing.values()):
            for item in group:
                item.wait_send()


class Reduce:
    def __init__(self, c, p, k):
        self.c, self.p, self.k = (c, p, k)
        self.grads = [k.g_q, k.g_kv, k.g_o, k.g_gate, k.g_up, k.g_down]
        self.outs = [k.o_q, k.o_kv, k.o_o, k.o_gate, k.o_up, k.o_down]
        self.near, self.over, self.along, self.shared, self.ends = ({}, {}, {}, {}, [])

    def span(self, a):
        return pl.ds(self.c.at[a], self.c.width[a])

    def start(self, a):
        c, p, k = (self.c, self.p, self.k)
        for slot, quarter in ((1, p.opposite), (0, p.beside)):
            self.near[slot, a] = send(
                self.grads[a].at[:, columns(quarter, c.width[a])],
                k.half.at[slot, :, self.span(a)],
                (k.gc_s, k.gc_r),
                (slot, a),
                p.near_id,
            )

    def cross(self, a):
        c, p, k = (self.c, self.p, self.k)
        self.near[1, a].wait_recv()
        total = k.half[1, :, self.span(a)].astype(FULL) + self.grads[a][
            :, columns(p.other, c.width[a])
        ].astype(FULL)
        k.away[:, self.span(a)] = total.astype(LOW)
        self.over[a] = send(
            k.away.at[:, self.span(a)],
            k.inbox.at[:, self.span(a)],
            (k.gf_s, k.gf_r),
            a,
            p.far_id,
        )

    def spread(self, a):
        c, p, k = (self.c, self.p, self.k)
        self.over[a].wait_recv()
        self.near[0, a].wait_recv()
        total = (
            k.half[0, :, self.span(a)].astype(FULL)
            + self.grads[a][:, columns(p.member, c.width[a])].astype(FULL)
            + k.inbox[:, self.span(a)].astype(FULL)
        )
        k.mine[:, self.span(a)] = total.astype(LOW)
        self.along[a] = [
            send(
                k.mine.at[block_rows(p.z_ids[d - 1][0], c.R), self.span(a)],
                k.arrived.at[d - 1, :, self.span(a)],
                (k.gz_s, k.gz_r),
                (d - 1, a),
                p.z_ids[d - 1],
            )
            for d in range(1, c.S)
        ]

    def collect(self, a):
        c, p, k = (self.c, self.p, self.k)
        span = self.span(a)
        total = k.mine[block_rows(p.shard, c.R), span].astype(FULL)
        for d in range(1, c.S):
            self.along[a][d - 1].wait_recv()
            total = total + k.arrived[d - 1, :, span].astype(FULL)
        if c.groups > 1:
            k.grouped[p.group, :, span] = total.astype(LOW)
            piece = k.grouped.at[p.group, :, span]
            moved = [
                send(piece, piece, (k.gg_s, k.gg_r), (d - 1, a), p.g_ids[d - 1])
                for d in range(1, c.groups)
            ]
            for item in moved:
                item.wait_recv()
            self.ends.extend(moved)
            total = k.grouped[0, :, span].astype(FULL)
            for g in range(1, c.groups):
                total = total + k.grouped[g, :, span].astype(FULL)
        return total

    def share(self, a, total):
        c, p, k = (self.c, self.p, self.k)
        cols = columns(p.member, c.width[a])
        self.outs[a][:, cols] = total.astype(LOW)
        piece = self.outs[a].at[:, cols]
        self.shared[a] = [
            send(piece, piece, (k.gs_s, k.gs_r), (0, a), p.far_id),
            send(piece, piece, (k.gs_s, k.gs_r), (1, a), p.near_id),
        ]

    def pass_on(self, a):
        c, p, k = (self.c, self.p, self.k)
        self.shared[a][0].wait_recv()
        piece = self.outs[a].at[:, columns(p.other, c.width[a])]
        self.shared[a].append(
            send(piece, piece, (k.gs_s, k.gs_r), (2, a), p.near_id)
        )

    def end(self):
        for a in self.c.order:
            self.shared[a][1].wait_recv()
            self.shared[a][2].wait_recv()
        for group in (
            self.near.values(),
            self.over.values(),
            *self.along.values(),
            *self.shared.values(),
            self.ends,
        ):
            for item in group:
                item.wait_send()


def block_kernel(c, names, *refs):
    k = Named(names, refs)
    p = Place(c)
    T, D, F, W, S, TP = (c.T, c.D, c.F, c.W, c.S, c.TP)
    scaling = HD ** (-0.5)
    sent = []

    def tp_start(slot, value):
        k.part[slot] = value.astype(LOW)
        copies = [
            send(
                k.part.at[slot],
                k.part_in.at[slot, d - 1],
                (k.tp_s, k.tp_r),
                (slot, d - 1),
                p.t_ids[d - 1],
            )
            for d in range(1, TP)
        ]
        sent.extend(copies)
        return copies

    def tp_total(slot, copies):
        total = k.part[slot].astype(FULL)
        for d in range(1, TP):
            copies[d - 1].wait_recv()
            total = total + k.part_in[slot, d - 1].astype(FULL)
        return total

    weights = Gather(c, p, k)
    weights.start_own()
    k.gains_at[p.shard] = k.gain_in[...]
    greet(p.z_ids + p.up_ids + p.t_ids)
    gain_copies = [
        send(
            k.gains_at.at[p.shard],
            k.gains_at.at[p.shard],
            (k.gn_s, k.gn_r),
            d - 1,
            p.z_ids[d - 1],
        )
        for d in range(1, S)
    ]
    sent.extend(gain_copies)
    weights.start(0)
    weights.own[0].wait()
    weights.own[1].wait()
    for a in range(1, 6):
        weights.start(a)
    unit1, r1 = norm_parts(k.x[...])
    k.unit1[...] = unit1
    k.r1[...] = r1
    k.unit_low[...] = unit1.astype(LOW)
    unit_copies = [
        send(
            k.unit_low,
            k.unit_win.at[pl.ds((d - 1) * T, T)],
            (k.un_s, k.un_r),
            d - 1,
            p.up_ids[d - 1],
        )
        for d in range(1, W)
    ]
    sent.extend(unit_copies)

    count = k.lengths.shape[1]
    lens = [k.lengths[0, j] for j in range(count)]
    ends = []
    for item in lens:
        ends.append(item if not ends else ends[-1] + item)

    def segment_of(index):
        return sum([(index >= end).astype(jnp.int32) for end in ends])

    def place_of(index):
        return index - sum([jnp.where(index >= e, n, 0) for e, n in zip(ends, lens)])

    q_index = p.ctx * T + lax.broadcasted_iota(jnp.int32, (T, T), 0)
    q_seg = segment_of(q_index)
    for d in range(W):
        base = lax.rem(p.ctx - d + c.C, c.C) * T
        k_index = base + lax.broadcasted_iota(jnp.int32, (T, T), 1)
        allowed = (q_seg == segment_of(k_index)) & (k_index <= q_index)
        k.mask[:, pl.ds(d * T, T)] = allowed.astype(FULL)
        rows = base + lax.broadcasted_iota(jnp.int32, (T, HD // 2), 0)
        angle = place_of(rows).astype(FULL) * k.freq[...]
        k.cosine[pl.ds(d * T, T)] = jnp.cos(angle)
        k.sine[pl.ds(d * T, T)] = jnp.sin(angle)

    for item in gain_copies:
        item.wait_recv()
    wide_gain = jnp.zeros((16, D), FULL)
    head_gain = jnp.zeros((16, HD), FULL)
    lanes = k.gain_in.shape[1]
    for s in range(S):
        part = k.gains_at[s]
        for total in ("wide", "head"):
            width = D if total == "wide" else HD
            row = lax.broadcasted_iota(jnp.int32, (lanes, width), 0)
            col = lax.broadcasted_iota(jnp.int32, (lanes, width), 1)
            pick = (col == row + s * (width // S)).astype(FULL).astype(LOW)
            if total == "wide":
                wide_gain = wide_gain + dot_plain(part, pick)
            else:
                head_gain = head_gain + dot_plain(part, pick)
    k.wide_gain[...] = wide_gain
    k.head_gain[...] = head_gain

    def gain(row):
        return k.wide_gain[row : row + 1, :]

    g_q, g_k = (lambda: k.head_gain[4:5, :]), (lambda: k.head_gain[5:6, :])

    k.xn1[...] = (k.unit1[...] * gain(0)).astype(LOW)
    weights.relay(0)
    weights.relay(1)
    weights.pass_on(0)
    weights.own[2].wait()
    weights.pass_on(1)
    weights.ready(0)

    qp = dot_plain(k.xn1[...], k.qw[...])
    cos0, sin0 = (k.cosine[pl.ds(0, T)], k.sine[pl.ds(0, T)])
    for h in range(c.heads):
        cols = pl.ds(h * HD, HD)
        unit, scale = norm_parts(qp[:, h * HD : (h + 1) * HD])
        k.qunit[:, cols] = unit
        k.rq[h] = scale
        k.queries[:, cols] = rotate(unit * g_q(), cos0, sin0).astype(LOW)
    weights.ready(1)
    weights.relay(2)
    for d in range(W):
        rows = pl.ds(d * T, T)
        if d == 0:
            xw = k.xn1[...]
        else:
            unit_copies[d - 1].wait_recv()
            xw = (k.unit_win[pl.ds((d - 1) * T, T)].astype(FULL) * gain(0)).astype(LOW)
        kvp = dot_plain(xw, k.kvw[...])
        unit, scale = norm_parts(kvp[:, :HD])
        if d == 0:
            k.kunit[...] = unit
            k.rk[...] = scale
        k.keys[rows] = rotate(unit * g_k(), k.cosine[rows], k.sine[rows]).astype(LOW)
        k.values[rows] = kvp[:, HD:].astype(LOW)
    weights.pass_on(2)

    for h in range(c.heads):
        cols = pl.ds(h * HD, HD)
        raw = dot_last(k.queries[:, cols], k.keys[...]) * scaling
        logits = jnp.where(k.mask[...] > 0.5, raw, -1e30)
        peak = jnp.max(logits, axis=1, keepdims=True)
        lifted = jnp.exp(logits - peak)
        w = lifted * (1.0 / jnp.sum(lifted, axis=1, keepdims=True))
        k.w[h] = w
        k.attended[:, cols] = dot_plain(w.astype(LOW), k.values[...]).astype(LOW)
        weights.relay(3 + h) if h < 2 else None
    weights.own[3].wait()
    weights.ready(2)
    for h in range(c.heads, 2):
        weights.relay(3 + h)
    proj_copies = tp_start(0, dot_last(k.attended[...], k.ow[...]))
    weights.pass_on(3)
    weights.pass_on(4)
    proj = tp_total(0, proj_copies)
    aunit, ra = norm_parts(proj)
    k.aunit[...] = aunit
    k.ra[...] = ra
    h1 = k.x[...] + aunit * gain(1)
    k.h1[...] = h1
    unit2, r2 = norm_parts(h1)
    k.unit2[...] = unit2
    k.r2[...] = r2
    k.xn2[...] = (unit2 * gain(2)).astype(LOW)
    weights.own[4].wait()
    weights.own[5].wait()
    weights.ready(3)
    weights.ready(4)
    weights.relay(5)

    for at in range(0, F, TILE):
        cols = pl.ds(at, TILE)
        gate = dot_plain(k.xn2[...], k.gw[:, cols])
        up = dot_plain(k.xn2[...], k.uw[:, cols])
        square = gate * gate
        bent = jnp.tanh(gelu_c * (gate + gelu_k * (square * gate)))
        half = 0.5 * (1.0 + bent)
        act = gate * half
        slope = half + 0.5 * gate * (1.0 - bent * bent) * (
            gelu_c * (1.0 + 3.0 * gelu_k * square)
        )
        k.act[:, cols] = act
        k.slope[:, cols] = up * slope
        k.hidden[:, cols] = (act * up).astype(LOW)
    weights.pass_on(5)
    weights.own[6].wait()
    weights.ready(5)
    ffn = tp_total(1, tp_start(1, dot_last(k.hidden[...], k.dw[...])))
    funit, rf = norm_parts(ffn)
    k.y[...] = k.h1[...] + funit * gain(3)

    grads = Reduce(c, p, k)
    share = 1.0 / TP
    dy = k.dy[...]
    k.gsum_own[...] = jnp.zeros(k.gsum_own.shape, FULL)
    k.gsum_own[3:4, :] = jnp.sum(dy * funit, axis=0, keepdims=True) * share
    dffn = norm_back(dy * gain(3), funit, rf).astype(LOW)
    k.dffn[...] = dffn

    def grad(a, left_t, right):
        for at in range(0, c.full[a], TILE):
            cols = pl.ds(at, TILE)
            grads.grads[a][:, cols] = dot_plain(left_t[...], right[:, cols]).astype(LOW)

    k.left_t[...] = jnp.transpose(dffn.astype(FULL)).astype(LOW)
    grad(5, k.left_t, k.hidden)
    grads.start(5)
    for at in range(0, F, TILE):
        cols = pl.ds(at, TILE)
        dhid = dot_plain(k.dffn[...], k.dw[:, cols])
        k.dup[:, cols] = (dhid * k.act[:, cols]).astype(LOW)
        k.dgate[:, cols] = (dhid * k.slope[:, cols]).astype(LOW)
    back = tp_start(
        2, dot_last(k.dgate[...], k.gw[...]) + dot_last(k.dup[...], k.uw[...])
    )
    k.left_t[...] = jnp.transpose(k.xn2[...].astype(FULL)).astype(LOW)
    grads.cross(5)
    grad(3, k.left_t, k.dgate)
    grads.start(3)
    grad(4, k.left_t, k.dup)
    grads.start(4)
    dxn2 = tp_total(2, back)
    unit2 = k.unit2[...]
    k.gsum_own[2:3, :] = jnp.sum(dxn2 * unit2, axis=0, keepdims=True) * share
    dh1 = k.dy[...] + norm_back(dxn2 * gain(2), unit2, k.r2[...])
    k.dh1[...] = dh1
    aunit = k.aunit[...]
    k.gsum_own[1:2, :] = jnp.sum(dh1 * aunit, axis=0, keepdims=True) * share
    dproj = norm_back(dh1 * gain(1), aunit, k.ra[...])
    k.left_t[...] = jnp.transpose(dproj).astype(LOW)
    k.dout[...] = dot_plain(dproj.astype(LOW), k.ow[...]).astype(LOW)
    grads.cross(3)
    grad(2, k.left_t, k.attended)
    grads.start(2)
    grads.cross(4)

    key_terms = jnp.zeros((W * T, HD), FULL)
    value_terms = jnp.zeros((W * T, HD), FULL)
    for h in range(c.heads):
        cols = pl.ds(h * HD, HD)
        w = k.w[h]
        dout = k.dout[:, cols]
        query = k.queries[:, cols]
        delta = jnp.sum(
            dout.astype(FULL) * k.attended[:, cols].astype(FULL), axis=1, keepdims=True
        )
        dprob = dot_last(dout, k.values[...])
        dscore = w * (dprob - delta) * scaling
        k.dq[:, cols] = dot_plain(dscore.astype(LOW), k.keys[...])
        key_terms = key_terms + dot_plain(jnp.transpose(dscore).astype(LOW), query)
        value_terms = value_terms + dot_plain(jnp.transpose(w).astype(LOW), dout)
    k.terms[:, pl.ds(0, HD)] = key_terms.astype(LOW)
    k.terms[:, pl.ds(HD, HD)] = value_terms.astype(LOW)
    scatter = [
        send(
            k.terms.at[pl.ds(d * T, T)],
            k.terms_in.at[d - 1],
            (k.sc_s, k.sc_r),
            d - 1,
            p.down_ids[d - 1],
        )
        for d in range(1, W)
    ]
    sent.extend(scatter)
    grads.cross(2)
    k.left_t[...] = jnp.transpose(k.xn1[...].astype(FULL)).astype(LOW)
    cos0, sin0 = (k.cosine[pl.ds(0, T)], k.sine[pl.ds(0, T)])
    dg_q = jnp.zeros((1, HD), FULL)
    for h in range(c.heads):
        cols = pl.ds(h * HD, HD)
        dqn = unrotate(k.dq[:, cols], cos0, sin0)
        unit = k.qunit[:, cols]
        dg_q = dg_q + jnp.sum(dqn * unit, axis=0, keepdims=True)
        k.dqp[:, cols] = norm_back(dqn * g_q(), unit, k.rq[h]).astype(LOW)
    k.gsum_own[4:5, pl.ds(0, HD)] = dg_q
    grad(0, k.left_t, k.dqp)
    grads.start(0)
    grads.spread(5)
    dxn1 = dot_last(k.dqp[...], k.qw[...])
    dkv = k.terms[pl.ds(0, T), :].astype(FULL)
    for d in range(1, W):
        scatter[d - 1].wait_recv()
        dkv = dkv + k.terms_in[d - 1].astype(FULL)
    dkn = unrotate(dkv[:, :HD], cos0, sin0)
    kunit = k.kunit[...]
    k.gsum_own[5:6, pl.ds(0, HD)] = jnp.sum(dkn * kunit, axis=0, keepdims=True)
    k.dkvp[:, pl.ds(0, HD)] = norm_back(dkn * g_k(), kunit, k.rk[...]).astype(LOW)
    k.dkvp[:, pl.ds(HD, HD)] = dkv[:, HD:].astype(LOW)
    last = tp_start(3, dxn1 + dot_last(k.dkvp[...], k.kvw[...]))
    grad(1, k.left_t, k.dkvp)
    grads.start(1)
    grads.cross(0)
    dxn1 = tp_total(3, last)
    unit1 = k.unit1[...]
    k.gsum_own[0:1, :] = jnp.sum(dxn1 * unit1, axis=0, keepdims=True) * share
    grads.cross(1)
    gain_near = send(k.gsum_own, k.gsum_in.at[0], (k.gr_s, k.gr_r), 0, p.near_id)
    k.xg[...] = k.dh1[...] + norm_back(dxn1 * gain(0), unit1, k.r1[...])
    gain_near.wait_recv()
    k.gsum_mid[0] = k.gsum_own[...] + k.gsum_in[0]
    gain_far = send(k.gsum_mid.at[0], k.gsum_in.at[1], (k.gr_s, k.gr_r), 1, p.far_id)
    sent.extend([gain_near, gain_far])
    grads.spread(3)
    gain_far.wait_recv()
    k.gsum_z[p.shard] = k.gsum_mid[0] + k.gsum_in[1]
    gains_z = [
        send(k.gsum_z.at[p.shard], k.gsum_z.at[p.shard], (k.gh_s, k.gh_r), d - 1, p.z_ids[d - 1])
        for d in range(1, S)
    ]
    sent.extend(gains_z)
    grads.share(5, grads.collect(5))
    grads.spread(4)
    for item in gains_z:
        item.wait_recv()
    total = k.gsum_z[0]
    for s in range(1, S):
        total = total + k.gsum_z[s]
    if c.groups > 1:
        k.gsum_g[p.group] = total
        moved = [
            send(k.gsum_g.at[p.group], k.gsum_g.at[p.group], (k.gi_s, k.gi_r), d - 1, p.g_ids[d - 1])
            for d in range(1, c.groups)
        ]
        sent.extend(moved)
        for item in moved:
            item.wait_recv()
        total = k.gsum_g[0]
        for g in range(1, c.groups):
            total = total + k.gsum_g[g]
    k.gsum_t[p.tp] = total
    gains_t = [
        send(k.gsum_t.at[p.tp], k.gsum_t.at[p.tp], (k.gj_s, k.gj_r), d - 1, p.t_ids[d - 1])
        for d in range(1, TP)
    ]
    sent.extend(gains_t)
    grads.spread(2)
    grads.share(3, grads.collect(3))
    grads.pass_on(5)
    grads.spread(0)
    grads.spread(1)
    grads.share(4, grads.collect(4))
    grads.pass_on(3)
    k.kv_done[...] = grads.collect(1).astype(LOW)
    kvs = [
        send(k.kv_done, k.kv_in.at[d - 1], (k.kt_s, k.kt_r), d - 1, p.t_ids[d - 1])
        for d in range(1, TP)
    ]
    sent.extend(kvs)
    grads.share(2, grads.collect(2))
    grads.share(0, grads.collect(0))
    for item in gains_t:
        item.wait_recv()
    total = k.gsum_t[0]
    for t in range(1, TP):
        total = total + k.gsum_t[t]
    k.gsum[...] = total
    grads.pass_on(4)
    total = k.kv_done[...].astype(FULL)
    for d in range(1, TP):
        kvs[d - 1].wait_recv()
        total = total + k.kv_in[d - 1].astype(FULL)
    grads.share(1, total)
    for a in (2, 0, 1):
        grads.pass_on(a)
    grads.end()
    weights.end()
    for item in sent:
        item.wait_send()


def run_block(c, lengths, freq, x, dy, gain_in, weights):
    T, D, R, S, W, F, HQ = (c.T, c.D, c.R, c.S, c.W, c.F, c.HQ)
    names, operands, in_specs = ([], [], [])
    vm, anywhere = (
        pl.BlockSpec(memory_space=pltpu.VMEM),
        pl.BlockSpec(memory_space=pl.ANY),
    )

    def operand(name, value, spec):
        names.append(name)
        operands.append(value)
        in_specs.append(spec)

    operand("lengths", lengths, pl.BlockSpec(memory_space=pltpu.SMEM))
    operand("freq", freq, vm)
    operand("x", x, vm)
    operand("dy", dy, vm)
    operand("gain_in", gain_in, vm)
    for name, value in zip(("q", "k", "v", "o", "gate", "up", "down"), weights):
        operand(name + "_in", value, anywhere)
    outs = [
        ("o_q", (R, HQ), LOW),
        ("o_kv", (R, 2 * HD), LOW),
        ("o_o", (R, HQ), LOW),
        ("o_gate", (R, F), LOW),
        ("o_up", (R, F), LOW),
        ("o_down", (R, F), LOW),
        ("y", (T, D), FULL),
        ("xg", (T, D), FULL),
        ("gsum", (8, D), FULL),
    ]
    names.extend([item[0] for item in outs])
    scratch = []

    def vmem(name, shape, dtype):
        names.append(name)
        scratch.append(pltpu.VMEM(shape, dtype))

    def sem(name, *shape):
        for end in ("_s", "_r"):
            names.append(name + end)
            scratch.append(pltpu.SemaphoreType.DMA(shape))

    for name, width in zip(("qw", "kvw", "ow", "gw", "uw", "dw"), c.full):
        vmem(name, (D, width), LOW)
    vmem("gains_at", (S,) + gain_in.shape, LOW)
    vmem("wide_gain", (16, D), FULL)
    vmem("head_gain", (16, HD), FULL)
    for name in ("unit1", "aunit", "h1", "unit2", "dh1"):
        vmem(name, (T, D), FULL)
    for name in ("r1", "ra", "r2", "rk"):
        vmem(name, (T, 1), FULL)
    for name in ("unit_low", "xn1", "xn2", "dffn"):
        vmem(name, (T, D), LOW)
    vmem("unit_win", (max(W - 1, 1) * T, D), LOW)
    vmem("left_t", (D, T), LOW)
    for name in ("cosine", "sine"):
        vmem(name, (W * T, HD // 2), FULL)
    vmem("mask", (T, W * T), FULL)
    vmem("qunit", (T, HQ), FULL)
    vmem("rq", (c.heads, T, 1), FULL)
    for name in ("queries", "attended", "dout", "dqp"):
        vmem(name, (T, HQ), LOW)
    vmem("dq", (T, HQ), FULL)
    vmem("dkvp", (T, 2 * HD), LOW)
    for name in ("keys", "values"):
        vmem(name, (W * T, HD), LOW)
    vmem("kunit", (T, HD), FULL)
    vmem("w", (c.heads, T, W * T), FULL)
    for name in ("act", "slope"):
        vmem(name, (T, F), FULL)
    for name in ("hidden", "dup", "dgate"):
        vmem(name, (T, F), LOW)
    vmem("part", (4, T, D), LOW)
    vmem("part_in", (4, max(c.TP - 1, 1), T, D), LOW)
    vmem("terms", (W * T, 2 * HD), LOW)
    vmem("terms_in", (max(W - 1, 1), T, 2 * HD), LOW)
    for name, width in zip(("g_q", "g_kv", "g_o", "g_gate", "g_up", "g_down"), c.full):
        vmem(name, (D, width), LOW)
    vmem("half", (2, D, c.wide), LOW)
    for name in ("away", "inbox", "mine"):
        vmem(name, (D, c.wide), LOW)
    vmem("arrived", (S - 1, R, c.wide), LOW)
    if c.groups > 1:
        vmem("grouped", (c.groups, R, c.wide), LOW)
        sem("gg", c.groups - 1, 6)
        vmem("gsum_g", (c.groups, 8, D), FULL)
        sem("gi", c.groups - 1)
    vmem("kv_done", (R, c.width[1]), LOW)
    vmem("kv_in", (max(c.TP - 1, 1), R, c.width[1]), LOW)
    vmem("gsum_own", (8, D), FULL)
    vmem("gsum_in", (2, 8, D), FULL)
    vmem("gsum_mid", (1, 8, D), FULL)
    vmem("gsum_z", (S, 8, D), FULL)
    vmem("gsum_t", (c.TP, 8, D), FULL)
    names.append("local")
    scratch.append(pltpu.SemaphoreType.DMA((7,)))
    for name in ("za", "fa", "na", "ca"):
        sem(name, S - 1, 6)
    sem("gn", S - 1)
    sem("un", max(W - 1, 1))
    sem("tp", 4, max(c.TP - 1, 1))
    sem("gc", 2, 6)
    sem("gf", 6)
    sem("gz", S - 1, 6)
    sem("gs", 3, 6)
    sem("sc", max(W - 1, 1))
    sem("gr", 2)
    sem("gh", S - 1)
    sem("gj", max(c.TP - 1, 1))
    sem("kt", max(c.TP - 1, 1))
    return pl.pallas_call(
        functools.partial(block_kernel, c, names),
        out_shape=[jax.ShapeDtypeStruct(shape, kind) for _, shape, kind in outs],
        in_specs=in_specs,
        out_specs=[vm] * len(outs),
        scratch_shapes=scratch,
        compiler_params=pltpu.CompilerParams(
            collective_id=0, has_side_effects=True, vmem_limit_bytes=58 * 1024 * 1024
        ),
        name="block",
    )(*operands)


def finish_kernel(c, *refs):
    lows, wholes = (refs[:6], refs[6:8])
    outs, ends, stage, sems = (refs[8:15], refs[15:17], refs[17:24], refs[24])
    copies = []

    def put(src, dst):
        copy = pltpu.make_async_copy(src, dst, sems.at[len(copies)])
        copy.start()
        copies.append(copy)

    for src, dst in zip(wholes, ends):
        put(src, dst)
    q, kv, o, gate, up, down = lows
    for src, buf, dst in zip(
        (gate, up, down, q, o), (stage[4], stage[5], stage[6], stage[0], stage[3]),
        (outs[4], outs[5], outs[6], outs[0], outs[3]),
    ):
        buf[...] = src[...].astype(FULL)
        put(buf, dst)
    stage[1][...] = kv[:, :HD].astype(FULL)
    put(stage[1], outs[1])
    stage[2][...] = kv[:, HD:].astype(FULL)
    put(stage[2], outs[2])
    for copy in copies:
        copy.wait()


def finish(c, lows, wholes):
    R = c.R
    widths = [c.HQ, HD, HD, c.HQ, c.F, c.F, c.F]
    vm, anywhere = (
        pl.BlockSpec(memory_space=pltpu.VMEM),
        pl.BlockSpec(memory_space=pl.ANY),
    )
    return pl.pallas_call(
        functools.partial(finish_kernel, c),
        out_shape=[jax.ShapeDtypeStruct((R, width), FULL) for width in widths]
        + [jax.ShapeDtypeStruct(item.shape, FULL) for item in wholes],
        in_specs=[vm] * 8,
        out_specs=[anywhere] * 9,
        scratch_shapes=[pltpu.VMEM((R, width), FULL) for width in widths]
        + [pltpu.SemaphoreType.DMA((9,))],
        compiler_params=pltpu.CompilerParams(vmem_limit_bytes=24 * 1024 * 1024),
        name="finish",
    )(*lows, *wholes)


def per_device(
    block_input,
    out_cotangent,
    seq_lengths,
    q_weight,
    k_weight,
    v_weight,
    o_weight,
    gate_weight,
    up_weight,
    down_weight,
    attn_in_gain,
    attn_out_gain,
    ffn_in_gain,
    ffn_out_gain,
    query_gain,
    key_gain,
):
    tokens, width = block_input.shape
    n_ctx = lax.axis_size("ctx")
    n_shard = lax.axis_size("shard")
    longest = tokens * n_ctx // 2
    window = min(n_ctx, -(-(longest - 1) // tokens) + 1)
    c = Sizes(
        n_shard,
        n_ctx,
        lax.axis_size("tp"),
        tokens,
        width,
        q_weight.shape[1],
        gate_weight.shape[1],
        window,
    )
    gains = (attn_in_gain, attn_out_gain, ffn_in_gain, ffn_out_gain, query_gain, key_gain)
    lanes = -(-c.R // LANES) * LANES
    packed = jnp.stack([jnp.pad(item, (0, lanes - item.shape[0])) for item in gains])
    packed = jnp.pad(packed, ((0, 16 - len(gains)), (0, 0)))
    freq = rope_base ** (-np.arange(HD // 2).astype(np.float32) * np.float32(2.0 / HD))
    outs = run_block(
        c,
        seq_lengths,
        jnp.asarray(freq.astype(np.float32)[None, :]),
        block_input,
        out_cotangent,
        packed,
        (q_weight, k_weight, v_weight, o_weight, gate_weight, up_weight, down_weight),
    )
    big = finish(c, outs[:6], outs[6:8])
    gsum = outs[8]
    shard = lax.axis_index("shard")
    small = []
    for row in range(6):
        own = (width if row < 4 else HD) // n_shard
        small.append(lax.dynamic_slice(gsum, (row, shard * own), (1, own))[0])
    return (big[7], big[8], *big[:7], *small)


def solution(mesh):
    rows = P(("shard", "ctx"), None)
    split = P("shard", "tp")
    whole = P("shard", None)
    line = P("shard")
    return jax.shard_map(
        per_device,
        mesh=mesh,
        in_specs=(rows, rows, whole, split, whole, whole) + (split,) * 4 + (line,) * 6,
        out_specs=(rows, rows, split, whole, whole) + (split,) * 4 + (line,) * 6,
        check_vma=False,
    )
```

```python
import functools

import jax
import jax.numpy as jnp
import numpy as np
from jax import lax
from jax.experimental import pallas as pl
from jax.experimental.pallas import tpu as pltpu
from jax.sharding import PartitionSpec as P

HD = 256
MESH = pl.DeviceIdType.MESH
LANES = 128
WAYS = 4
TILE = 256
LOW, FULL = (jnp.bfloat16, jnp.float32)
PARTS = ("q", "kv", "o", "gate", "up", "down")

eps = 1e-06
rope_base = 1000000.0
gelu_c = 0.7978845608028654
gelu_k = 0.044715


def dot_plain(left, right):
    return jnp.dot(left, right, preferred_element_type=FULL)


def dot_last(left, right):
    return lax.dot_general(
        left, right, (((1,), (1,)), ((), ())), preferred_element_type=FULL
    )


def dot_first(left, right):
    return lax.dot_general(
        left, right, (((0,), (0,)), ((), ())), preferred_element_type=FULL
    )


def norm_parts(value):
    scale = lax.rsqrt(jnp.mean(value * value, axis=-1, keepdims=True) + eps)
    return (value * scale, scale)


def norm_back(dnormed, unit, scale):
    return scale * (dnormed - unit * jnp.mean(dnormed * unit, axis=-1, keepdims=True))


def rotate(value, cosine, sine):
    half = value.shape[-1] // 2
    first, second = (value[..., :half], value[..., half:])
    return jnp.concatenate(
        [first * cosine - second * sine, second * cosine + first * sine], axis=-1
    )


def unrotate(value, cosine, sine):
    half = value.shape[-1] // 2
    first, second = (value[..., :half], value[..., half:])
    return jnp.concatenate(
        [first * cosine + second * sine, second * cosine - first * sine], axis=-1
    )


def greet(peers):
    barrier = pltpu.get_barrier_semaphore()
    for peer in peers:
        pl.semaphore_signal(barrier, inc=1, device_id=peer, device_id_type=MESH)
    pl.semaphore_wait(barrier, len(peers))


def remote(src, dst, send_sem, recv_sem, peer):
    return pltpu.make_async_remote_copy(
        src_ref=src,
        dst_ref=dst,
        send_sem=send_sem,
        recv_sem=recv_sem,
        device_id=peer,
        device_id_type=MESH,
    )


def send(src, dst, sems, where, peer):
    copy = remote(src, dst, sems[0].at[where], sems[1].at[where], peer)
    copy.start()
    return copy


def columns(member, width):
    return pl.ds(pl.multiple_of(member * width, LANES), width)


def block_rows(index, count):
    return pl.ds(pl.multiple_of(index * count, 16), count)


class Sizes:
    def __init__(self, shard, ctx, tp, tokens, deep, qcols, ff, window):
        self.S, self.C, self.TP = (shard, ctx, tp)
        self.T, self.D, self.R = (tokens, deep, deep // shard)
        self.HQ, self.F, self.W = (qcols, ff, window)
        self.heads = qcols // HD
        self.groups = ctx // WAYS
        self.full = [qcols, 2 * HD, qcols, ff, ff, ff]
        self.width = [item // WAYS for item in self.full]
        self.order = [5, 3, 4, 2, 0, 1]
        self.at = {}
        total = 0
        for a in self.order:
            self.at[a] = total
            total = total + self.width[a]
        self.wide = total


class Named:
    def __init__(self, names, refs):
        for name, ref in zip(names, refs, strict=True):
            setattr(self, name, ref)


class Place:
    def __init__(self, c):
        shard, ctx, tp = (
            lax.axis_index("shard"),
            lax.axis_index("ctx"),
            lax.axis_index("tp"),
        )
        core = lax.rem(ctx, 2)
        high = lax.rem(lax.div(ctx, 2), 2)
        near, far = (ctx + 1 - 2 * core, ctx + 2 - 4 * high)
        self.shard, self.ctx, self.tp = (shard, ctx, tp)
        self.member, self.other = (lax.rem(ctx, WAYS), lax.rem(far, WAYS))
        self.beside = lax.rem(near, WAYS)
        self.opposite = self.beside + self.other - self.member
        self.group = lax.div(ctx, WAYS)
        self.near_id, self.far_id = ((shard, near, tp), (shard, far, tp))
        left, right = (shard, c.S - 1 - shard)
        least = jnp.minimum(left, right)
        self.far_by = []
        for i in range(c.S - 1):
            hop = i // 2 + 1
            both = hop if i % 2 == 0 else c.S - hop
            alone = i - least + 1
            alone = jnp.where(left > right, alone, c.S - alone)
            self.far_by.append(jnp.where(i < 2 * least, both, alone))
        self.after_id = (jnp.minimum(shard + 1, c.S - 1), ctx, tp)
        self.before_id = (jnp.maximum(shard - 1, 0), ctx, tp)
        self.z_ids = [(lax.rem(shard + d, c.S), ctx, tp) for d in range(1, c.S)]
        self.up_ids = [(shard, lax.rem(ctx + d, c.C), tp) for d in range(1, c.C)]
        self.down_ids = [
            (shard, lax.rem(ctx - d + c.C, c.C), tp) for d in range(1, c.C)
        ]
        self.g_ids = [
            (shard, lax.rem(ctx + WAYS * d, c.C), tp) for d in range(1, c.groups)
        ]
        self.t_ids = [(shard, ctx, lax.rem(tp + d, c.TP)) for d in range(1, c.TP)]


class Gather:
    def __init__(self, c, p, k):
        self.c, self.p, self.k = (c, p, k)
        self.src = [k.q_in, None, k.o_in, k.gate_in, k.up_in, k.down_in]
        self.dst = [k.qw, k.kvw, k.ow, k.gw, k.uw, k.dw]
        self.first, self.across, self.landing, self.own = ([], {}, {}, [])

    def local(self, src, dst):
        copy = pltpu.make_async_copy(src, dst, self.k.local.at[len(self.own)])
        copy.start()
        self.own.append(copy)

    def start_own(self):
        c, p, k = (self.c, self.p, self.k)
        rows = block_rows(p.shard, c.R)
        self.local(k.k_in, k.kvw.at[rows, pl.ds(0, HD)])
        self.local(k.v_in, k.kvw.at[rows, pl.ds(HD, HD)])
        for a in (0, 2, 3, 4, 5):
            self.local(self.src[a], self.dst[a].at[rows])

    def start(self, a):
        c, p, k = (self.c, self.p, self.k)
        cols = columns(p.member, c.width[a])
        rows = block_rows(p.shard, c.R)
        src = self.dst[a].at[rows, cols] if a == 1 else self.src[a].at[:, cols]
        for side, ok, peer, at in (
            (0, p.shard < c.S - 1, p.after_id, 0),
            (1, p.shard > 0, p.before_id, c.S - 2),
        ):
            copy = remote(
                src,
                self.dst[a].at[rows, cols],
                k.zo_s.at[side, a],
                k.za_r.at[at, a],
                peer,
            )
            pl.when(ok)(copy.start)
            self.first.append((ok, copy))

    def piece(self, i, a, member):
        c, p = (self.c, self.p)
        source = lax.rem(p.shard - p.far_by[i] + c.S, c.S)
        return self.dst[a].at[block_rows(source, c.R), columns(member, c.width[a])]

    def relay(self, a, i):
        c, p, k = (self.c, self.p, self.k)
        middle = (p.shard > 0) & (p.shard < c.S - 1)
        d = p.far_by[i]
        block = self.piece(i, a, p.member)
        up = d <= p.shard
        target = jnp.where(up, p.shard + 1, p.shard - 1)
        target = jnp.clip(target, 0, c.S - 1)
        there = jnp.clip(jnp.where(up, d, d - 2), 0, c.S - 2)
        copy = remote(
            block,
            block,
            k.zf_s.at[i, a],
            k.za_r.at[there, a],
            (target, p.ctx, p.tp),
        )
        remote(block, block, k.zf_s.at[i, a], k.za_r.at[d - 1, a], p.far_id).wait_recv()
        pl.when(middle)(copy.start)
        self.first.append((middle, copy))
        self.across[i, a] = send(block, block, (k.fa_s, k.fa_r), (i, a), p.far_id)
        self.landing.setdefault(a, []).append(
            send(block, block, (k.na_s, k.na_r), (i, a), p.near_id)
        )

    def pass_on(self, a, i):
        p, k = (self.p, self.k)
        self.across[i, a].wait_recv()
        block = self.piece(i, a, p.other)
        self.landing[a].append(send(block, block, (k.ca_s, k.ca_r), (i, a), p.near_id))

    def ready(self, a):
        for item in self.landing[a]:
            item.wait_recv()

    def end(self):
        for ok, copy in self.first:
            pl.when(ok)(copy.wait_send)
        for group in (self.across.values(), *self.landing.values()):
            for item in group:
                item.wait_send()


class Reduce:
    def __init__(self, c, p, k):
        self.c, self.p, self.k = (c, p, k)
        self.grads = [k.g_q, k.g_kv, k.g_o, k.g_gate, k.g_up, k.g_down]
        self.outs = [k.o_q, k.o_kv, k.o_o, k.o_gate, k.o_up, k.o_down]
        self.near, self.over, self.along, self.shared, self.ends = ({}, {}, {}, {}, [])

    def span(self, a):
        return pl.ds(self.c.at[a], self.c.width[a])

    def start(self, a):
        c, p, k = (self.c, self.p, self.k)
        for slot, quarter in ((1, p.opposite), (0, p.beside)):
            self.near[slot, a] = send(
                self.grads[a].at[:, columns(quarter, c.width[a])],
                k.half.at[slot, :, self.span(a)],
                (k.gc_s, k.gc_r),
                (slot, a),
                p.near_id,
            )

    def cross(self, a):
        c, p, k = (self.c, self.p, self.k)
        self.near[1, a].wait_recv()
        total = k.half[1, :, self.span(a)].astype(FULL) + self.grads[a][
            :, columns(p.other, c.width[a])
        ].astype(FULL)
        k.away[:, self.span(a)] = total.astype(LOW)
        self.over[a] = send(
            k.away.at[:, self.span(a)],
            k.inbox.at[:, self.span(a)],
            (k.gf_s, k.gf_r),
            a,
            p.far_id,
        )

    def spread(self, a):
        c, p, k = (self.c, self.p, self.k)
        self.over[a].wait_recv()
        self.near[0, a].wait_recv()
        total = (
            k.half[0, :, self.span(a)].astype(FULL)
            + self.grads[a][:, columns(p.member, c.width[a])].astype(FULL)
            + k.inbox[:, self.span(a)].astype(FULL)
        )
        k.mine[:, self.span(a)] = total.astype(LOW)
        self.along[a] = [
            send(
                k.mine.at[block_rows(p.z_ids[d - 1][0], c.R), self.span(a)],
                k.arrived.at[d - 1, :, self.span(a)],
                (k.gz_s, k.gz_r),
                (d - 1, a),
                p.z_ids[d - 1],
            )
            for d in range(1, c.S)
        ]

    def collect(self, a):
        c, p, k = (self.c, self.p, self.k)
        span = self.span(a)
        total = k.mine[block_rows(p.shard, c.R), span].astype(FULL)
        for d in range(1, c.S):
            self.along[a][d - 1].wait_recv()
            total = total + k.arrived[d - 1, :, span].astype(FULL)
        if c.groups > 1:
            k.grouped[p.group, :, span] = total.astype(LOW)
            piece = k.grouped.at[p.group, :, span]
            moved = [
                send(piece, piece, (k.gg_s, k.gg_r), (d - 1, a), p.g_ids[d - 1])
                for d in range(1, c.groups)
            ]
            for item in moved:
                item.wait_recv()
            self.ends.extend(moved)
            total = k.grouped[0, :, span].astype(FULL)
            for g in range(1, c.groups):
                total = total + k.grouped[g, :, span].astype(FULL)
        return total

    def share(self, a, total):
        c, p, k = (self.c, self.p, self.k)
        cols = columns(p.member, c.width[a])
        self.outs[a][:, cols] = total.astype(LOW)
        piece = self.outs[a].at[:, cols]
        self.shared[a] = [
            send(piece, piece, (k.gs_s, k.gs_r), (0, a), p.far_id),
            send(piece, piece, (k.gs_s, k.gs_r), (1, a), p.near_id),
        ]

    def pass_on(self, a):
        c, p, k = (self.c, self.p, self.k)
        self.shared[a][0].wait_recv()
        piece = self.outs[a].at[:, columns(p.other, c.width[a])]
        self.shared[a].append(
            send(piece, piece, (k.gs_s, k.gs_r), (2, a), p.near_id)
        )

    def arrived(self, a):
        self.shared[a][1].wait_recv()
        self.shared[a][2].wait_recv()

    def end(self):
        for group in (
            self.near.values(),
            self.over.values(),
            *self.along.values(),
            *self.shared.values(),
            self.ends,
        ):
            for item in group:
                item.wait_send()


def block_kernel(c, names, *refs):
    k = Named(names, refs)
    p = Place(c)
    T, D, F, W, S, TP = (c.T, c.D, c.F, c.W, c.S, c.TP)
    scaling = HD ** (-0.5)
    sent = []
    left = []

    def leave(src, dst):
        copy = pltpu.make_async_copy(src, dst, k.leave.at[len(left)])
        copy.start()
        left.append(copy)

    def tp_start(slot, value):
        k.part[slot] = value.astype(LOW)
        copies = [
            send(
                k.part.at[slot],
                k.part_in.at[slot, d - 1],
                (k.tp_s, k.tp_r),
                (slot, d - 1),
                p.t_ids[d - 1],
            )
            for d in range(1, TP)
        ]
        sent.extend(copies)
        return copies

    def tp_total(slot, copies):
        total = k.part[slot].astype(FULL)
        for d in range(1, TP):
            copies[d - 1].wait_recv()
            total = total + k.part_in[slot, d - 1].astype(FULL)
        return total

    weights = Gather(c, p, k)
    weights.start_own()
    k.gains_at[p.shard] = k.gain_in[...]
    greet(p.z_ids + p.up_ids + p.t_ids)
    gain_copies = [
        send(
            k.gains_at.at[p.shard],
            k.gains_at.at[p.shard],
            (k.gn_s, k.gn_r),
            d - 1,
            p.z_ids[d - 1],
        )
        for d in range(1, S)
    ]
    sent.extend(gain_copies)
    weights.start(0)
    weights.own[0].wait()
    weights.own[1].wait()
    for a in range(1, 6):
        weights.start(a)
    unit1, r1 = norm_parts(k.x[...])
    k.unit1[...] = unit1
    k.r1[...] = r1
    k.unit_low[...] = unit1.astype(LOW)
    unit_copies = [
        send(
            k.unit_low,
            k.unit_win.at[pl.ds((d - 1) * T, T)],
            (k.un_s, k.un_r),
            d - 1,
            p.up_ids[d - 1],
        )
        for d in range(1, W)
    ]
    sent.extend(unit_copies)

    count = k.lengths.shape[1]
    lens = [k.lengths[0, j] for j in range(count)]
    ends = []
    for item in lens:
        ends.append(item if not ends else ends[-1] + item)

    def segment_of(index):
        return sum([(index >= end).astype(jnp.int32) for end in ends])

    def place_of(index):
        return index - sum([jnp.where(index >= e, n, 0) for e, n in zip(ends, lens)])

    q_index = p.ctx * T + lax.broadcasted_iota(jnp.int32, (T, T), 0)
    q_seg = segment_of(q_index)
    for d in range(W):
        base = lax.rem(p.ctx - d + c.C, c.C) * T
        k_index = base + lax.broadcasted_iota(jnp.int32, (T, T), 1)
        allowed = (q_seg == segment_of(k_index)) & (k_index <= q_index)
        k.mask[:, pl.ds(d * T, T)] = allowed.astype(FULL)
        rows = base + lax.broadcasted_iota(jnp.int32, (T, HD // 2), 0)
        angle = place_of(rows).astype(FULL) * k.freq[...]
        k.cosine[pl.ds(d * T, T)] = jnp.cos(angle)
        k.sine[pl.ds(d * T, T)] = jnp.sin(angle)

    for item in gain_copies:
        item.wait_recv()
    wide_gain = jnp.zeros((8, D), FULL)
    head_gain = jnp.zeros((8, HD), FULL)
    lanes = k.gain_in.shape[1]
    for s in range(S):
        part = k.gains_at[s].astype(LOW)
        for total in ("wide", "head"):
            width = D if total == "wide" else HD
            row = lax.broadcasted_iota(jnp.int32, (lanes, width), 0)
            col = lax.broadcasted_iota(jnp.int32, (lanes, width), 1)
            pick = (col == row + s * (width // S)).astype(FULL).astype(LOW)
            if total == "wide":
                wide_gain = wide_gain + dot_plain(part, pick)
            else:
                head_gain = head_gain + dot_plain(part, pick)
    k.wide_gain[...] = wide_gain
    k.head_gain[...] = head_gain

    def gain(row):
        return k.wide_gain[row : row + 1, :]

    g_q, g_k = (lambda: k.head_gain[4:5, :]), (lambda: k.head_gain[5:6, :])

    k.xn1[...] = (k.unit1[...] * gain(0)).astype(LOW)
    for item in weights.own[2:]:
        item.wait()

    def project():
        weights.ready(0)
        qp = dot_plain(k.xn1[...], k.qw[...])
        cos0, sin0 = (k.cosine[pl.ds(0, T)], k.sine[pl.ds(0, T)])
        for h in range(c.heads):
            cols = pl.ds(h * HD, HD)
            unit, scale = norm_parts(qp[:, h * HD : (h + 1) * HD])
            k.qunit[:, cols] = unit
            k.rq[h] = scale
            k.queries[:, cols] = rotate(unit * g_q(), cos0, sin0).astype(LOW)
        weights.ready(1)
        for d in range(W):
            rows = pl.ds(d * T, T)
            if d == 0:
                xw = k.xn1[...]
            else:
                unit_copies[d - 1].wait_recv()
                low = k.unit_win[pl.ds((d - 1) * T, T)]
                xw = (low.astype(FULL) * gain(0)).astype(LOW)
            kvp = dot_plain(xw, k.kvw[...])
            unit, scale = norm_parts(kvp[:, :HD])
            if d == 0:
                k.kunit[...] = unit
                k.rk[...] = scale
            k.keys[rows] = rotate(unit * g_k(), k.cosine[rows], k.sine[rows]).astype(LOW)
            k.values[rows] = kvp[:, HD:].astype(LOW)

    def attend(h):
        cols = pl.ds(h * HD, HD)
        raw = dot_last(k.queries[:, cols], k.keys[...]) * scaling
        logits = jnp.where(k.mask[...] > 0.5, raw, -1e30)
        peak = jnp.max(logits, axis=1, keepdims=True)
        lifted = jnp.exp(logits - peak)
        w = lifted * (1.0 / jnp.sum(lifted, axis=1, keepdims=True))
        k.w[h] = w
        k.attended[:, cols] = dot_plain(w.astype(LOW), k.values[...]).astype(LOW)

    proj_copies = []

    def output():
        weights.ready(2)
        proj_copies.extend(tp_start(0, dot_last(k.attended[...], k.ow[...])))

    steps = []
    reach = 0.0
    for a in range(6):
        reach = reach + c.width[a] / LANES
        for i in range(S - 1):
            steps.append((reach + 3.5 * i, len(steps), functools.partial(weights.relay, a, i)))
            steps.append((reach + 3.5 * i + 4.0, len(steps), functools.partial(weights.pass_on, a, i)))
    ready = 2.0 + 3.5 * (S - 2) + 4.0
    steps.append((ready + 0.3, len(steps), project))
    for h in range(c.heads):
        steps.append((ready + 0.6 + 0.3 * h, len(steps), functools.partial(attend, h)))
    steps.append((max(ready + 0.6 + 0.3 * c.heads, ready + 1.5), len(steps), output))
    for _, _, step in sorted(steps, key=lambda item: item[:2]):
        step()
    proj = tp_total(0, proj_copies)
    aunit, ra = norm_parts(proj)
    k.aunit[...] = aunit
    k.ra[...] = ra
    h1 = k.x[...] + aunit * gain(1)
    k.h1[...] = h1
    unit2, r2 = norm_parts(h1)
    k.unit2[...] = unit2
    k.r2[...] = r2
    k.xn2[...] = (unit2 * gain(2)).astype(LOW)
    weights.ready(3)
    weights.ready(4)

    for at in range(0, F, TILE):
        cols = pl.ds(at, TILE)
        gate = dot_plain(k.xn2[...], k.gw[:, cols])
        up = dot_plain(k.xn2[...], k.uw[:, cols])
        square = gate * gate
        bent = jnp.tanh(gelu_c * (gate + gelu_k * (square * gate)))
        half = 0.5 * (1.0 + bent)
        act = gate * half
        slope = half + 0.5 * gate * (1.0 - bent * bent) * (
            gelu_c * (1.0 + 3.0 * gelu_k * square)
        )
        k.act[:, cols] = act
        k.slope[:, cols] = up * slope
        k.hidden[:, cols] = (act * up).astype(LOW)
    weights.ready(5)
    ffn = tp_total(1, tp_start(1, dot_last(k.hidden[...], k.dw[...])))
    funit, rf = norm_parts(ffn)
    k.y[...] = k.h1[...] + funit * gain(3)
    leave(k.y, k.h_y)

    grads = Reduce(c, p, k)
    share = 1.0 / TP
    dy = k.dy[...]
    k.gsum_own[...] = jnp.zeros(k.gsum_own.shape, FULL)
    k.gsum_own[3:4, :] = jnp.sum(dy * funit, axis=0, keepdims=True) * share
    dffn = norm_back(dy * gain(3), funit, rf).astype(LOW)
    k.dffn[...] = dffn

    def grad(a, left_t, right):
        for at in range(0, c.full[a], TILE):
            cols = pl.ds(at, TILE)
            grads.grads[a][:, cols] = dot_plain(left_t[...], right[:, cols]).astype(LOW)

    k.left_t[...] = jnp.transpose(dffn.astype(FULL)).astype(LOW)
    grad(5, k.left_t, k.hidden)
    grads.start(5)
    for at in range(0, F, TILE):
        cols = pl.ds(at, TILE)
        dhid = dot_plain(k.dffn[...], k.dw[:, cols])
        k.dup[:, cols] = (dhid * k.act[:, cols]).astype(LOW)
        k.dgate[:, cols] = (dhid * k.slope[:, cols]).astype(LOW)
    back = tp_start(
        2, dot_last(k.dgate[...], k.gw[...]) + dot_last(k.dup[...], k.uw[...])
    )
    k.left_t[...] = jnp.transpose(k.xn2[...].astype(FULL)).astype(LOW)
    grads.cross(5)
    grad(3, k.left_t, k.dgate)
    grads.start(3)
    grad(4, k.left_t, k.dup)
    grads.start(4)
    grads.cross(3)
    dxn2 = tp_total(2, back)
    unit2 = k.unit2[...]
    k.gsum_own[2:3, :] = jnp.sum(dxn2 * unit2, axis=0, keepdims=True) * share
    dh1 = k.dy[...] + norm_back(dxn2 * gain(2), unit2, k.r2[...])
    k.dh1[...] = dh1
    aunit = k.aunit[...]
    k.gsum_own[1:2, :] = jnp.sum(dh1 * aunit, axis=0, keepdims=True) * share
    dproj = norm_back(dh1 * gain(1), aunit, k.ra[...])
    k.left_t[...] = jnp.transpose(dproj).astype(LOW)
    k.dout[...] = dot_plain(dproj.astype(LOW), k.ow[...]).astype(LOW)
    grad(2, k.left_t, k.attended)
    grads.start(2)

    key_terms = jnp.zeros((W * T, HD), FULL)
    value_terms = jnp.zeros((W * T, HD), FULL)
    for h in range(c.heads):
        cols = pl.ds(h * HD, HD)
        w = k.w[h]
        dout = k.dout[:, cols]
        query = k.queries[:, cols]
        delta = jnp.sum(
            dout.astype(FULL) * k.attended[:, cols].astype(FULL), axis=1, keepdims=True
        )
        dprob = dot_last(dout, k.values[...])
        dscore = w * (dprob - delta) * scaling
        k.dq[:, cols] = dot_plain(dscore.astype(LOW), k.keys[...])
        key_terms = key_terms + dot_plain(jnp.transpose(dscore).astype(LOW), query)
        value_terms = value_terms + dot_plain(jnp.transpose(w).astype(LOW), dout)
    k.terms[:, pl.ds(0, HD)] = key_terms.astype(LOW)
    k.terms[:, pl.ds(HD, HD)] = value_terms.astype(LOW)
    scatter = [
        send(
            k.terms.at[pl.ds(d * T, T)],
            k.terms_in.at[d - 1],
            (k.sc_s, k.sc_r),
            d - 1,
            p.down_ids[d - 1],
        )
        for d in range(1, W)
    ]
    sent.extend(scatter)
    grads.spread(5)
    grads.cross(4)
    k.left_t[...] = jnp.transpose(k.xn1[...].astype(FULL)).astype(LOW)
    cos0, sin0 = (k.cosine[pl.ds(0, T)], k.sine[pl.ds(0, T)])
    dg_q = jnp.zeros((1, HD), FULL)
    for h in range(c.heads):
        cols = pl.ds(h * HD, HD)
        dqn = unrotate(k.dq[:, cols], cos0, sin0)
        unit = k.qunit[:, cols]
        dg_q = dg_q + jnp.sum(dqn * unit, axis=0, keepdims=True)
        k.dqp[:, cols] = norm_back(dqn * g_q(), unit, k.rq[h]).astype(LOW)
    k.gsum_own[4:5, pl.ds(0, HD)] = dg_q
    grad(0, k.left_t, k.dqp)
    grads.start(0)
    dxn1 = dot_last(k.dqp[...], k.qw[...])
    dkv = k.terms[pl.ds(0, T), :].astype(FULL)
    for d in range(1, W):
        scatter[d - 1].wait_recv()
        dkv = dkv + k.terms_in[d - 1].astype(FULL)
    dkn = unrotate(dkv[:, :HD], cos0, sin0)
    kunit = k.kunit[...]
    k.gsum_own[5:6, pl.ds(0, HD)] = jnp.sum(dkn * kunit, axis=0, keepdims=True)
    k.dkvp[:, pl.ds(0, HD)] = norm_back(dkn * g_k(), kunit, k.rk[...]).astype(LOW)
    k.dkvp[:, pl.ds(HD, HD)] = dkv[:, HD:].astype(LOW)
    last = tp_start(3, dxn1 + dot_last(k.dkvp[...], k.kvw[...]))
    grad(1, k.left_t, k.dkvp)
    grads.start(1)
    grads.cross(2)
    grads.spread(3)
    dxn1 = tp_total(3, last)
    unit1 = k.unit1[...]
    k.gsum_own[0:1, :] = jnp.sum(dxn1 * unit1, axis=0, keepdims=True) * share
    grads.cross(0)
    gain_near = send(k.gsum_own, k.gsum_in.at[0], (k.gr_s, k.gr_r), 0, p.near_id)
    k.xg[...] = k.dh1[...] + norm_back(dxn1 * gain(0), unit1, k.r1[...])
    leave(k.xg, k.h_xg)
    gain_near.wait_recv()
    k.gsum_mid[0] = k.gsum_own[...] + k.gsum_in[0]
    gain_far = send(k.gsum_mid.at[0], k.gsum_in.at[1], (k.gr_s, k.gr_r), 1, p.far_id)
    sent.extend([gain_near, gain_far])
    grads.share(5, grads.collect(5))
    grads.spread(4)
    grads.cross(1)
    gain_far.wait_recv()
    k.gsum_z[p.shard] = k.gsum_mid[0] + k.gsum_in[1]
    gains_z = [
        send(k.gsum_z.at[p.shard], k.gsum_z.at[p.shard], (k.gh_s, k.gh_r), d - 1, p.z_ids[d - 1])
        for d in range(1, S)
    ]
    sent.extend(gains_z)
    grads.share(3, grads.collect(3))
    grads.pass_on(5)
    grads.spread(2)
    for item in gains_z:
        item.wait_recv()
    total = k.gsum_z[0]
    for s in range(1, S):
        total = total + k.gsum_z[s]
    if c.groups > 1:
        k.gsum_g[p.group] = total
        moved = [
            send(k.gsum_g.at[p.group], k.gsum_g.at[p.group], (k.gi_s, k.gi_r), d - 1, p.g_ids[d - 1])
            for d in range(1, c.groups)
        ]
        sent.extend(moved)
        for item in moved:
            item.wait_recv()
        total = k.gsum_g[0]
        for g in range(1, c.groups):
            total = total + k.gsum_g[g]
    k.gsum_t[p.tp] = total
    gains_t = [
        send(k.gsum_t.at[p.tp], k.gsum_t.at[p.tp], (k.gj_s, k.gj_r), d - 1, p.t_ids[d - 1])
        for d in range(1, TP)
    ]
    sent.extend(gains_t)
    grads.spread(0)
    grads.share(4, grads.collect(4))
    grads.pass_on(3)
    grads.spread(1)
    grads.share(2, grads.collect(2))
    grads.pass_on(4)
    k.kv_done[...] = grads.collect(1).astype(LOW)
    kvs = [
        send(k.kv_done, k.kv_in.at[d - 1], (k.kt_s, k.kt_r), d - 1, p.t_ids[d - 1])
        for d in range(1, TP)
    ]
    sent.extend(kvs)
    grads.share(0, grads.collect(0))
    for item in gains_t:
        item.wait_recv()
    total = k.gsum_t[0]
    for t in range(1, TP):
        total = total + k.gsum_t[t]
    k.gsum[...] = total
    total = k.kv_done[...].astype(FULL)
    for d in range(1, TP):
        kvs[d - 1].wait_recv()
        total = total + k.kv_in[d - 1].astype(FULL)
    grads.share(1, total)
    for a in (2, 0, 1):
        grads.pass_on(a)
    hbm = [k.h_q, k.h_kv, k.h_o, k.h_gate, k.h_up, k.h_down]
    for a in c.order:
        grads.arrived(a)
        leave(grads.outs[a], hbm[a])
    grads.end()
    weights.end()
    for item in left:
        item.wait()
    for item in sent:
        item.wait_send()


def run_block(c, lengths, freq, x, dy, gain_in, weights):
    T, D, R, S, W, F, HQ = (c.T, c.D, c.R, c.S, c.W, c.F, c.HQ)
    names, operands, in_specs = ([], [], [])
    vm, anywhere = (
        pl.BlockSpec(memory_space=pltpu.VMEM),
        pl.BlockSpec(memory_space=pl.ANY),
    )

    def operand(name, value, spec):
        names.append(name)
        operands.append(value)
        in_specs.append(spec)

    operand("lengths", lengths, pl.BlockSpec(memory_space=pltpu.SMEM))
    operand("freq", freq, vm)
    operand("x", x, vm)
    operand("dy", dy, vm)
    operand("gain_in", gain_in, vm)
    for name, value in zip(("q", "k", "v", "o", "gate", "up", "down"), weights):
        operand(name + "_in", value, anywhere)
    outs = [(f"h_{name}", (R, width), LOW) for name, width in zip(PARTS, c.full)]
    outs.extend([("h_y", (T, D), FULL), ("h_xg", (T, D), FULL), ("gsum", (8, D), FULL)])
    names.extend([item[0] for item in outs])
    scratch = []

    def vmem(name, shape, dtype):
        names.append(name)
        scratch.append(pltpu.VMEM(shape, dtype))

    def sem(name, *shape):
        for end in ("_s", "_r"):
            names.append(name + end)
            scratch.append(pltpu.SemaphoreType.DMA(shape))

    for name, width in zip(PARTS, c.full):
        vmem("o_" + name, (R, width), LOW)
    vmem("y", (T, D), FULL)
    vmem("xg", (T, D), FULL)
    names.append("leave")
    scratch.append(pltpu.SemaphoreType.DMA((8,)))
    for name, width in zip(("qw", "kvw", "ow", "gw", "uw", "dw"), c.full):
        vmem(name, (D, width), LOW)
    vmem("gains_at", (S,) + gain_in.shape, FULL)
    vmem("wide_gain", (8, D), FULL)
    vmem("head_gain", (8, HD), FULL)
    for name in ("unit1", "aunit", "h1", "unit2", "dh1"):
        vmem(name, (T, D), FULL)
    for name in ("r1", "ra", "r2", "rk"):
        vmem(name, (T, 1), FULL)
    for name in ("unit_low", "xn1", "xn2", "dffn"):
        vmem(name, (T, D), LOW)
    vmem("unit_win", (max(W - 1, 1) * T, D), LOW)
    vmem("left_t", (D, T), LOW)
    for name in ("cosine", "sine"):
        vmem(name, (W * T, HD // 2), FULL)
    vmem("mask", (T, W * T), FULL)
    vmem("qunit", (T, HQ), FULL)
    vmem("rq", (c.heads, T, 1), FULL)
    for name in ("queries", "attended", "dout", "dqp"):
        vmem(name, (T, HQ), LOW)
    vmem("dq", (T, HQ), FULL)
    vmem("dkvp", (T, 2 * HD), LOW)
    for name in ("keys", "values"):
        vmem(name, (W * T, HD), LOW)
    vmem("kunit", (T, HD), FULL)
    vmem("w", (c.heads, T, W * T), FULL)
    for name in ("act", "slope"):
        vmem(name, (T, F), FULL)
    for name in ("hidden", "dup", "dgate"):
        vmem(name, (T, F), LOW)
    vmem("part", (4, T, D), LOW)
    vmem("part_in", (4, max(c.TP - 1, 1), T, D), LOW)
    vmem("terms", (W * T, 2 * HD), LOW)
    vmem("terms_in", (max(W - 1, 1), T, 2 * HD), LOW)
    for name, width in zip(("g_q", "g_kv", "g_o", "g_gate", "g_up", "g_down"), c.full):
        vmem(name, (D, width), LOW)
    vmem("half", (2, D, c.wide), LOW)
    for name in ("away", "inbox", "mine"):
        vmem(name, (D, c.wide), LOW)
    vmem("arrived", (S - 1, R, c.wide), LOW)
    if c.groups > 1:
        vmem("grouped", (c.groups, R, c.wide), LOW)
        sem("gg", c.groups - 1, 6)
        vmem("gsum_g", (c.groups, 8, D), FULL)
        sem("gi", c.groups - 1)
    vmem("kv_done", (R, c.width[1]), LOW)
    vmem("kv_in", (max(c.TP - 1, 1), R, c.width[1]), LOW)
    vmem("gsum_own", (8, D), FULL)
    vmem("gsum_in", (2, 8, D), FULL)
    vmem("gsum_mid", (1, 8, D), FULL)
    vmem("gsum_z", (S, 8, D), FULL)
    vmem("gsum_t", (c.TP, 8, D), FULL)
    names.append("local")
    scratch.append(pltpu.SemaphoreType.DMA((7,)))
    for name in ("za", "fa", "na", "ca"):
        sem(name, S - 1, 6)
    sem("zo", 2, 6)
    sem("zf", S - 1, 6)
    sem("gn", S - 1)
    sem("un", max(W - 1, 1))
    sem("tp", 4, max(c.TP - 1, 1))
    sem("gc", 2, 6)
    sem("gf", 6)
    sem("gz", S - 1, 6)
    sem("gs", 3, 6)
    sem("sc", max(W - 1, 1))
    sem("gr", 2)
    sem("gh", S - 1)
    sem("gj", max(c.TP - 1, 1))
    sem("kt", max(c.TP - 1, 1))
    return pl.pallas_call(
        functools.partial(block_kernel, c, names),
        out_shape=[jax.ShapeDtypeStruct(shape, kind) for _, shape, kind in outs],
        in_specs=in_specs,
        out_specs=[anywhere] * 8 + [vm],
        scratch_shapes=scratch,
        compiler_params=pltpu.CompilerParams(
            collective_id=0, has_side_effects=True, vmem_limit_bytes=58 * 1024 * 1024
        ),
        name="block",
    )(*operands)


def finish_kernel(c, *refs):
    ins, gsum, outs, small, stage, lows, through, sems, own_sems = (
        refs[:8],
        refs[8],
        refs[9:18],
        refs[18],
        refs[19:26],
        refs[26:32],
        refs[32],
        refs[33],
        refs[34],
    )
    copies = []

    def put(src, dst):
        copy = pltpu.make_async_copy(src, dst, sems.at[len(copies)])
        copy.start()
        copies.append(copy)

    taken = []
    for a in (5, 3, 4, 0, 2, 1):
        copy = pltpu.make_async_copy(ins[a], lows[a], own_sems.at[a])
        copy.start()
        taken.append((a, copy))
    for a in (6, 7):
        copy = pltpu.make_async_copy(ins[a], through.at[a - 6], own_sems.at[a])
        copy.start()
        taken.append((a, copy))
    shard = lax.axis_index("shard")
    for row, width in ((0, c.D), (4, HD)):
        part = gsum[...] if width == c.D else gsum[:, :HD]
        moved = pltpu.roll(part, lax.rem(width - shard * (width // c.S), width), 1)
        if row == 0:
            small[0:4, :] = moved[0:4, : small.shape[1]]
        else:
            small[4:8, :] = moved[4:8, : small.shape[1]]
    at = {0: (0,), 1: (1, 2), 2: (3,), 3: (4,), 4: (5,), 5: (6,)}
    for a, copy in taken:
        copy.wait()
        if a >= 6:
            put(through.at[a - 6], outs[a + 1])
            continue
        for j, slot in enumerate(at[a]):
            width = stage[slot].shape[1]
            stage[slot][...] = lows[a][:, j * width : (j + 1) * width].astype(FULL)
            put(stage[slot], outs[slot])
    for copy in copies:
        copy.wait()


def finish(c, parts, gsum):
    R = c.R
    widths = [c.HQ, HD, HD, c.HQ, c.F, c.F, c.F]
    vm, anywhere = (
        pl.BlockSpec(memory_space=pltpu.VMEM),
        pl.BlockSpec(memory_space=pl.ANY),
    )
    lanes = max(-(-c.R // LANES) * LANES, LANES)
    return pl.pallas_call(
        functools.partial(finish_kernel, c),
        out_shape=[jax.ShapeDtypeStruct((R, width), FULL) for width in widths]
        + [jax.ShapeDtypeStruct(item.shape, FULL) for item in parts[6:]]
        + [jax.ShapeDtypeStruct((8, lanes), FULL)],
        in_specs=[anywhere] * 8 + [vm],
        out_specs=[anywhere] * 9 + [vm],
        scratch_shapes=[pltpu.VMEM((R, width), FULL) for width in widths]
        + [pltpu.VMEM((R, width), LOW) for width in c.full]
        + [pltpu.VMEM((2,) + parts[6].shape, FULL)]
        + [pltpu.SemaphoreType.DMA((9,)), pltpu.SemaphoreType.DMA((8,))],
        compiler_params=pltpu.CompilerParams(vmem_limit_bytes=58 * 1024 * 1024),
        name="finish",
    )(*parts, gsum)


def per_device(
    block_input,
    out_cotangent,
    seq_lengths,
    q_weight,
    k_weight,
    v_weight,
    o_weight,
    gate_weight,
    up_weight,
    down_weight,
    attn_in_gain,
    attn_out_gain,
    ffn_in_gain,
    ffn_out_gain,
    query_gain,
    key_gain,
):
    tokens, width = block_input.shape
    n_ctx = lax.axis_size("ctx")
    n_shard = lax.axis_size("shard")
    longest = tokens * n_ctx // 2
    window = min(n_ctx, -(-(longest - 1) // tokens) + 1)
    c = Sizes(
        n_shard,
        n_ctx,
        lax.axis_size("tp"),
        tokens,
        width,
        q_weight.shape[1],
        gate_weight.shape[1],
        window,
    )
    gains = (attn_in_gain, attn_out_gain, ffn_in_gain, ffn_out_gain, query_gain, key_gain)
    lanes = -(-c.R // LANES) * LANES
    packed = jnp.zeros((8 * lanes,), FULL)
    for row, item in enumerate(gains):
        behind = (8 - row) * lanes - item.shape[0]
        packed = packed + jnp.pad(item.astype(FULL), (row * lanes, behind))
    packed = packed.reshape(8, lanes)
    freq = rope_base ** (-np.arange(HD // 2).astype(np.float32) * np.float32(2.0 / HD))
    outs = run_block(
        c,
        seq_lengths,
        jnp.asarray(freq.astype(np.float32)[None, :]),
        block_input,
        out_cotangent,
        packed,
        (q_weight, k_weight, v_weight, o_weight, gate_weight, up_weight, down_weight),
    )
    big = finish(c, outs[:8], outs[8])
    small = [
        big[9][row, : (width if row < 4 else HD) // n_shard] for row in range(len(gains))
    ]
    return (big[7], big[8], *big[:7], *small)


def solution(mesh):
    rows = P(("shard", "ctx"), None)
    split = P("shard", "tp")
    whole = P("shard", None)
    line = P("shard")
    return jax.shard_map(
        per_device,
        mesh=mesh,
        in_specs=(rows, rows, whole, split, whole, whole) + (split,) * 4 + (line,) * 6,
        out_specs=(rows, rows, split, whole, whole) + (split,) * 4 + (line,) * 6,
        check_vma=False,
    )
```

```python
import functools

import jax
import jax.numpy as jnp
import numpy as np
from jax import lax
from jax.experimental import pallas as pl
from jax.experimental.pallas import tpu as pltpu
from jax.sharding import PartitionSpec as P

HD = 256
MESH = pl.DeviceIdType.MESH
LANES = 128
WAYS = 4
TILE = 256
LOW, FULL = (jnp.bfloat16, jnp.float32)
PAIRS = ("xn1", "xn2", "dffn", "dproj", "attended", "hidden", "dgate", "dup", "dqp", "dkvp")
PARTS = ("q", "kv", "o", "gate", "up", "down")

eps = 1e-06
rope_base = 1000000.0
gelu_c = 0.7978845608028654
gelu_k = 0.044715


def dot_plain(left, right):
    return jnp.dot(left, right, preferred_element_type=FULL)


def dot_last(left, right):
    return lax.dot_general(
        left, right, (((1,), (1,)), ((), ())), preferred_element_type=FULL
    )


def dot_first(left, right):
    return lax.dot_general(
        left, right, (((0,), (0,)), ((), ())), preferred_element_type=FULL
    )


def norm_parts(value):
    scale = lax.rsqrt(jnp.mean(value * value, axis=-1, keepdims=True) + eps)
    return (value * scale, scale)


def norm_back(dnormed, unit, scale):
    return scale * (dnormed - unit * jnp.mean(dnormed * unit, axis=-1, keepdims=True))


def rotate(value, cosine, sine):
    half = value.shape[-1] // 2
    first, second = (value[..., :half], value[..., half:])
    return jnp.concatenate(
        [first * cosine - second * sine, second * cosine + first * sine], axis=-1
    )


def unrotate(value, cosine, sine):
    half = value.shape[-1] // 2
    first, second = (value[..., :half], value[..., half:])
    return jnp.concatenate(
        [first * cosine + second * sine, second * cosine - first * sine], axis=-1
    )


def greet(peers):
    barrier = pltpu.get_barrier_semaphore()
    for peer in peers:
        pl.semaphore_signal(barrier, inc=1, device_id=peer, device_id_type=MESH)
    pl.semaphore_wait(barrier, len(peers))


def remote(src, dst, send_sem, recv_sem, peer):
    return pltpu.make_async_remote_copy(
        src_ref=src,
        dst_ref=dst,
        send_sem=send_sem,
        recv_sem=recv_sem,
        device_id=peer,
        device_id_type=MESH,
    )


def send(src, dst, sems, where, peer):
    copy = remote(src, dst, sems[0].at[where], sems[1].at[where], peer)
    copy.start()
    return copy


def columns(member, width):
    return pl.ds(pl.multiple_of(member * width, LANES), width)


def block_rows(index, count):
    return pl.ds(pl.multiple_of(index * count, 16), count)


class Sizes:
    def __init__(self, shard, ctx, tp, tokens, deep, qcols, ff, window):
        self.S, self.C, self.TP = (shard, ctx, tp)
        self.T, self.D, self.R = (tokens, deep, deep // shard)
        self.HQ, self.F, self.W = (qcols, ff, window)
        self.heads = qcols // HD
        self.groups = ctx // WAYS
        self.full = [qcols, 2 * HD, qcols, ff, ff, ff]
        self.width = [item // WAYS for item in self.full]
        self.order = [5, 3, 4, 2, 0, 1]
        self.at = {}
        total = 0
        for a in self.order:
            self.at[a] = total
            total = total + self.width[a]
        self.wide = total


class Named:
    def __init__(self, names, refs):
        for name, ref in zip(names, refs, strict=True):
            setattr(self, name, ref)


class Place:
    def __init__(self, c):
        shard, ctx, tp = (
            lax.axis_index("shard"),
            lax.axis_index("ctx"),
            lax.axis_index("tp"),
        )
        core = lax.rem(ctx, 2)
        high = lax.rem(lax.div(ctx, 2), 2)
        near, far = (ctx + 1 - 2 * core, ctx + 2 - 4 * high)
        self.shard, self.ctx, self.tp = (shard, ctx, tp)
        self.member, self.other = (lax.rem(ctx, WAYS), lax.rem(far, WAYS))
        self.core, self.high = (core, high)
        self.group = lax.div(ctx, WAYS)
        self.near_id, self.far_id = ((shard, near, tp), (shard, far, tp))
        self.diag_id = (shard, near + far - ctx, tp)
        left, right = (shard, c.S - 1 - shard)
        least = jnp.minimum(left, right)
        self.far_by = []
        for i in range(c.S - 1):
            hop = i // 2 + 1
            both = hop if i % 2 == 0 else c.S - hop
            alone = i - least + 1
            alone = jnp.where(left > right, alone, c.S - alone)
            self.far_by.append(jnp.where(i < 2 * least, both, alone))
        self.after_id = (jnp.minimum(shard + 1, c.S - 1), ctx, tp)
        self.before_id = (jnp.maximum(shard - 1, 0), ctx, tp)
        self.z_ids = [(lax.rem(shard + d, c.S), ctx, tp) for d in range(1, c.S)]
        self.up_ids = [(shard, lax.rem(ctx + d, c.C), tp) for d in range(1, c.C)]
        self.down_ids = [
            (shard, lax.rem(ctx - d + c.C, c.C), tp) for d in range(1, c.C)
        ]
        self.g_ids = [
            (shard, lax.rem(ctx + WAYS * d, c.C), tp) for d in range(1, c.groups)
        ]
        self.t_ids = [(shard, ctx, lax.rem(tp + d, c.TP)) for d in range(1, c.TP)]


class Gather:
    def __init__(self, c, p, k):
        self.c, self.p, self.k = (c, p, k)
        self.src = [k.q_in, None, k.o_in, k.gate_in, k.up_in, k.down_in]
        self.dst = [k.qw, k.kvw, k.ow, k.gw, k.uw, k.dw]
        self.first, self.across, self.landing, self.own = ([], {}, {}, [])

    def local(self, src, dst):
        copy = pltpu.make_async_copy(src, dst, self.k.local.at[len(self.own)])
        copy.start()
        self.own.append(copy)

    def start_own(self):
        c, p, k = (self.c, self.p, self.k)
        rows = block_rows(p.shard, c.R)
        self.local(k.k_in, k.kvw.at[rows, pl.ds(0, HD)])
        self.local(k.v_in, k.kvw.at[rows, pl.ds(HD, HD)])
        for a in (0, 2, 3, 4, 5):
            self.local(self.src[a], self.dst[a].at[rows])

    def start(self, a):
        c, p, k = (self.c, self.p, self.k)
        cols = columns(p.member, c.width[a])
        rows = block_rows(p.shard, c.R)
        src = self.dst[a].at[rows, cols] if a == 1 else self.src[a].at[:, cols]
        for side, ok, peer, at in (
            (0, p.shard < c.S - 1, p.after_id, 0),
            (1, p.shard > 0, p.before_id, c.S - 2),
        ):
            copy = remote(
                src,
                self.dst[a].at[rows, cols],
                k.zo_s.at[side, a],
                k.za_r.at[at, a],
                peer,
            )
            pl.when(ok)(copy.start)
            self.first.append((ok, copy))

    def piece(self, i, a, member):
        c, p = (self.c, self.p)
        source = lax.rem(p.shard - p.far_by[i] + c.S, c.S)
        return self.dst[a].at[block_rows(source, c.R), columns(member, c.width[a])]

    def relay(self, a, i):
        c, p, k = (self.c, self.p, self.k)
        middle = (p.shard > 0) & (p.shard < c.S - 1)
        d = p.far_by[i]
        block = self.piece(i, a, p.member)
        up = d <= p.shard
        target = jnp.where(up, p.shard + 1, p.shard - 1)
        target = jnp.clip(target, 0, c.S - 1)
        there = jnp.clip(jnp.where(up, d, d - 2), 0, c.S - 2)
        copy = remote(
            block,
            block,
            k.zf_s.at[i, a],
            k.za_r.at[there, a],
            (target, p.ctx, p.tp),
        )
        remote(block, block, k.zf_s.at[i, a], k.za_r.at[d - 1, a], p.far_id).wait_recv()
        pl.when(middle)(copy.start)
        self.first.append((middle, copy))
        self.across[i, a] = send(block, block, (k.fa_s, k.fa_r), (i, a), p.far_id)
        self.landing.setdefault(a, []).append(
            send(block, block, (k.na_s, k.na_r), (i, a), p.near_id)
        )

    def pass_on(self, a, i):
        p, k = (self.p, self.k)
        self.across[i, a].wait_recv()
        block = self.piece(i, a, p.other)
        self.landing[a].append(send(block, block, (k.ca_s, k.ca_r), (i, a), p.near_id))

    def ready(self, a):
        for item in self.landing[a]:
            item.wait_recv()

    def end(self):
        for ok, copy in self.first:
            pl.when(ok)(copy.wait_send)
        for group in (self.across.values(), *self.landing.values()):
            for item in group:
                item.wait_send()


class Reduce:
    def __init__(self, c, p, k):
        self.c, self.p, self.k = (c, p, k)
        self.grads = [k.g_q, k.g_kv, k.g_o, k.g_gate, k.g_up, k.g_down]
        self.outs = [k.o_q, k.o_kv, k.o_o, k.o_gate, k.o_up, k.o_down]
        self.near, self.along, self.shared, self.ends = ({}, {}, {}, [])

    def span(self, a):
        return pl.ds(self.c.at[a], self.c.width[a])

    def start(self, a):
        c, p, k = (self.c, self.p, self.k)
        self.near[a] = send(
            self.grads[a].at[:, columns(1 - p.core, c.width[a])],
            k.half.at[:, self.span(a)],
            (k.gc_s, k.gc_r),
            a,
            p.near_id,
        )

    def summed(self, a):
        c, p, k = (self.c, self.p, self.k)
        self.near[a].wait_recv()
        return k.half[:, self.span(a)].astype(FULL) + self.grads[a][
            :, columns(p.core, c.width[a])
        ].astype(FULL)

    def spread(self, a, total=None):
        c, p, k = (self.c, self.p, self.k)
        total = self.summed(a) if total is None else total
        k.mine[:, self.span(a)] = total.astype(LOW)
        self.along[a] = [
            send(
                k.mine.at[block_rows(p.z_ids[d - 1][0], c.R), self.span(a)],
                k.arrived.at[d - 1, :, self.span(a)],
                (k.gz_s, k.gz_r),
                (d - 1, a),
                p.z_ids[d - 1],
            )
            for d in range(1, c.S)
        ]

    def collect(self, a):
        c, p, k = (self.c, self.p, self.k)
        span = self.span(a)
        total = k.mine[block_rows(p.shard, c.R), span].astype(FULL)
        for d in range(1, c.S):
            self.along[a][d - 1].wait_recv()
            total = total + k.arrived[d - 1, :, span].astype(FULL)
        if c.groups > 1:
            k.grouped[p.group, :, span] = total.astype(LOW)
            piece = k.grouped.at[p.group, :, span]
            moved = [
                send(piece, piece, (k.gg_s, k.gg_r), (d - 1, a), p.g_ids[d - 1])
                for d in range(1, c.groups)
            ]
            for item in moved:
                item.wait_recv()
            self.ends.extend(moved)
            total = k.grouped[0, :, span].astype(FULL)
            for g in range(1, c.groups):
                total = total + k.grouped[g, :, span].astype(FULL)
        return total

    def share(self, a, total):
        c, p, k = (self.c, self.p, self.k)
        cols = columns(p.member, c.width[a])
        self.outs[a][:, cols] = total.astype(LOW)
        piece = self.outs[a].at[:, cols]
        self.shared[a] = [
            send(piece, piece, (k.gs_s, k.gs_r), (at, a), peer)
            for at, peer in enumerate((p.far_id, p.near_id, p.diag_id))
        ]

    def arrived(self, a):
        for item in self.shared[a]:
            item.wait_recv()

    def end(self):
        for group in (
            self.near.values(),
            *self.along.values(),
            *self.shared.values(),
            self.ends,
        ):
            for item in group:
                item.wait_send()


def block_kernel(c, names, *refs):
    k = Named(names, refs)
    p = Place(c)
    T, D, F, W, S, TP = (c.T, c.D, c.F, c.W, c.S, c.TP)
    scaling = HD ** (-0.5)
    sent = []
    left = []

    def leave(src, dst):
        copy = pltpu.make_async_copy(src, dst, k.leave.at[len(left)])
        copy.start()
        left.append(copy)

    def tp_start(slot, value):
        k.part[slot] = value.astype(LOW)
        copies = [
            send(
                k.part.at[slot],
                k.part_in.at[slot, d - 1],
                (k.tp_s, k.tp_r),
                (slot, d - 1),
                p.t_ids[d - 1],
            )
            for d in range(1, TP)
        ]
        sent.extend(copies)
        return copies

    def tp_total(slot, copies):
        total = k.part[slot].astype(FULL)
        for d in range(1, TP):
            copies[d - 1].wait_recv()
            total = total + k.part_in[slot, d - 1].astype(FULL)
        return total

    paired = {}

    def pair(name, value, half=False):
        width = value.shape[1] // 2
        src = value.at[:, columns(1 - p.high, width)] if half else value
        order = PAIRS.index(name)
        paired[name] = send(
            src, getattr(k, "far_" + name), (k.px_s, k.px_r), order, p.far_id
        )
        sent.append(paired[name])

    weights = Gather(c, p, k)
    weights.start_own()
    k.gains_at[p.shard] = k.gain_in[...]
    greet(p.z_ids + p.up_ids + p.t_ids)
    gain_copies = [
        send(
            k.gains_at.at[p.shard],
            k.gains_at.at[p.shard],
            (k.gn_s, k.gn_r),
            d - 1,
            p.z_ids[d - 1],
        )
        for d in range(1, S)
    ]
    sent.extend(gain_copies)
    weights.start(0)
    weights.own[0].wait()
    weights.own[1].wait()
    for a in range(1, 6):
        weights.start(a)
    unit1, r1 = norm_parts(k.x[...])
    k.unit1[...] = unit1
    k.r1[...] = r1
    k.unit_low[...] = unit1.astype(LOW)
    unit_copies = [
        send(
            k.unit_low,
            k.unit_win.at[pl.ds((d - 1) * T, T)],
            (k.un_s, k.un_r),
            d - 1,
            p.up_ids[d - 1],
        )
        for d in range(1, W)
    ]
    sent.extend(unit_copies)

    count = k.lengths.shape[1]
    lens = [k.lengths[0, j] for j in range(count)]
    ends = []
    for item in lens:
        ends.append(item if not ends else ends[-1] + item)

    def segment_of(index):
        return sum([(index >= end).astype(jnp.int32) for end in ends])

    def place_of(index):
        return index - sum([jnp.where(index >= e, n, 0) for e, n in zip(ends, lens)])

    q_index = p.ctx * T + lax.broadcasted_iota(jnp.int32, (T, T), 0)
    q_seg = segment_of(q_index)
    for d in range(W):
        base = lax.rem(p.ctx - d + c.C, c.C) * T
        k_index = base + lax.broadcasted_iota(jnp.int32, (T, T), 1)
        allowed = (q_seg == segment_of(k_index)) & (k_index <= q_index)
        k.mask[:, pl.ds(d * T, T)] = allowed.astype(FULL)
        rows = base + lax.broadcasted_iota(jnp.int32, (T, HD // 2), 0)
        angle = place_of(rows).astype(FULL) * k.freq[...]
        k.cosine[pl.ds(d * T, T)] = jnp.cos(angle)
        k.sine[pl.ds(d * T, T)] = jnp.sin(angle)

    for item in gain_copies:
        item.wait_recv()
    wide_gain = jnp.zeros((8, D), FULL)
    head_gain = jnp.zeros((8, HD), FULL)
    lanes = k.gain_in.shape[1]
    for s in range(S):
        part = k.gains_at[s].astype(LOW)
        for total in ("wide", "head"):
            width = D if total == "wide" else HD
            row = lax.broadcasted_iota(jnp.int32, (lanes, width), 0)
            col = lax.broadcasted_iota(jnp.int32, (lanes, width), 1)
            pick = (col == row + s * (width // S)).astype(FULL).astype(LOW)
            if total == "wide":
                wide_gain = wide_gain + dot_plain(part, pick)
            else:
                head_gain = head_gain + dot_plain(part, pick)
    k.wide_gain[...] = wide_gain
    k.head_gain[...] = head_gain

    def gain(row):
        return k.wide_gain[row : row + 1, :]

    g_q, g_k = (lambda: k.head_gain[4:5, :]), (lambda: k.head_gain[5:6, :])

    k.xn1[...] = (k.unit1[...] * gain(0)).astype(LOW)
    pair("xn1", k.xn1)
    for item in weights.own[2:]:
        item.wait()

    def project():
        weights.ready(0)
        qp = dot_plain(k.xn1[...], k.qw[...])
        cos0, sin0 = (k.cosine[pl.ds(0, T)], k.sine[pl.ds(0, T)])
        for h in range(c.heads):
            cols = pl.ds(h * HD, HD)
            unit, scale = norm_parts(qp[:, h * HD : (h + 1) * HD])
            k.qunit[:, cols] = unit
            k.rq[h] = scale
            k.queries[:, cols] = rotate(unit * g_q(), cos0, sin0).astype(LOW)
        weights.ready(1)
        for d in range(W):
            rows = pl.ds(d * T, T)
            if d == 0:
                xw = k.xn1[...]
            else:
                unit_copies[d - 1].wait_recv()
                low = k.unit_win[pl.ds((d - 1) * T, T)]
                xw = (low.astype(FULL) * gain(0)).astype(LOW)
            kvp = dot_plain(xw, k.kvw[...])
            unit, scale = norm_parts(kvp[:, :HD])
            if d == 0:
                k.kunit[...] = unit
                k.rk[...] = scale
            k.keys[rows] = rotate(unit * g_k(), k.cosine[rows], k.sine[rows]).astype(LOW)
            k.values[rows] = kvp[:, HD:].astype(LOW)

    def attend(h):
        cols = pl.ds(h * HD, HD)
        raw = dot_last(k.queries[:, cols], k.keys[...]) * scaling
        logits = jnp.where(k.mask[...] > 0.5, raw, -1e30)
        peak = jnp.max(logits, axis=1, keepdims=True)
        lifted = jnp.exp(logits - peak)
        w = lifted * (1.0 / jnp.sum(lifted, axis=1, keepdims=True))
        k.w[h] = w
        k.attended[:, cols] = dot_plain(w.astype(LOW), k.values[...]).astype(LOW)

    proj_copies = []

    def output():
        weights.ready(2)
        proj_copies.extend(tp_start(0, dot_last(k.attended[...], k.ow[...])))

    steps = []
    reach = 0.0
    for a in range(6):
        reach = reach + c.width[a] / LANES
        for i in range(S - 1):
            steps.append((reach + 3.5 * i, len(steps), functools.partial(weights.relay, a, i)))
            steps.append((reach + 3.5 * i + 4.0, len(steps), functools.partial(weights.pass_on, a, i)))
    ready = 2.0 + 3.5 * (S - 2) + 4.0
    steps.append((ready + 0.3, len(steps), project))
    for h in range(c.heads):
        steps.append((ready + 0.6 + 0.3 * h, len(steps), functools.partial(attend, h)))
    steps.append((max(ready + 0.6 + 0.3 * c.heads, ready + 1.5), len(steps), output))
    for _, _, step in sorted(steps, key=lambda item: item[:2]):
        step()
    proj = tp_total(0, proj_copies)
    aunit, ra = norm_parts(proj)
    k.aunit[...] = aunit
    k.ra[...] = ra
    h1 = k.x[...] + aunit * gain(1)
    k.h1[...] = h1
    unit2, r2 = norm_parts(h1)
    k.unit2[...] = unit2
    k.r2[...] = r2
    k.xn2[...] = (unit2 * gain(2)).astype(LOW)
    pair("xn2", k.xn2)
    pair("attended", k.attended, True)
    weights.ready(3)
    weights.ready(4)

    for at in range(0, F, TILE):
        cols = pl.ds(at, TILE)
        gate = dot_plain(k.xn2[...], k.gw[:, cols])
        up = dot_plain(k.xn2[...], k.uw[:, cols])
        square = gate * gate
        bent = jnp.tanh(gelu_c * (gate + gelu_k * (square * gate)))
        half = 0.5 * (1.0 + bent)
        act = gate * half
        slope = half + 0.5 * gate * (1.0 - bent * bent) * (
            gelu_c * (1.0 + 3.0 * gelu_k * square)
        )
        k.act[:, cols] = act
        k.slope[:, cols] = up * slope
        k.hidden[:, cols] = (act * up).astype(LOW)
    pair("hidden", k.hidden, True)
    weights.ready(5)
    ffn = tp_total(1, tp_start(1, dot_last(k.hidden[...], k.dw[...])))
    funit, rf = norm_parts(ffn)
    k.y[...] = k.h1[...] + funit * gain(3)
    leave(k.y, k.h_y)

    grads = Reduce(c, p, k)
    share = 1.0 / TP
    dy = k.dy[...]
    k.gsum_own[...] = jnp.zeros(k.gsum_own.shape, FULL)
    k.gsum_own[3:4, :] = jnp.sum(dy * funit, axis=0, keepdims=True) * share
    dffn = norm_back(dy * gain(3), funit, rf).astype(LOW)
    k.dffn[...] = dffn

    pair("dffn", k.dffn)

    def transposed(name, own):
        paired[name].wait_recv()
        k.left_t[:, pl.ds(0, T)] = jnp.transpose(own[...].astype(FULL)).astype(LOW)
        far = getattr(k, "far_" + name)
        k.left_t[:, pl.ds(T, T)] = jnp.transpose(far[...].astype(FULL)).astype(LOW)

    def grad(a, name, own):
        paired[name].wait_recv()
        half = c.full[a] // 2
        k.right[pl.ds(0, T), pl.ds(0, half)] = own[:, columns(p.high, half)]
        k.right[pl.ds(T, T), pl.ds(0, half)] = getattr(k, "far_" + name)[...]
        for at in range(0, half, TILE):
            cols = pl.ds(at, TILE)
            grads.grads[a][:, cols] = dot_plain(k.left_t[...], k.right[:, cols]).astype(LOW)
        grads.start(a)

    for at in range(0, F, TILE):
        cols = pl.ds(at, TILE)
        dhid = dot_plain(k.dffn[...], k.dw[:, cols])
        k.dup[:, cols] = (dhid * k.act[:, cols]).astype(LOW)
        k.dgate[:, cols] = (dhid * k.slope[:, cols]).astype(LOW)
    pair("dgate", k.dgate, True)
    pair("dup", k.dup, True)
    back = tp_start(
        2, dot_last(k.dgate[...], k.gw[...]) + dot_last(k.dup[...], k.uw[...])
    )
    transposed("dffn", k.dffn)
    grad(5, "hidden", k.hidden)
    dxn2 = tp_total(2, back)
    unit2 = k.unit2[...]
    k.gsum_own[2:3, :] = jnp.sum(dxn2 * unit2, axis=0, keepdims=True) * share
    dh1 = k.dy[...] + norm_back(dxn2 * gain(2), unit2, k.r2[...])
    k.dh1[...] = dh1
    aunit = k.aunit[...]
    k.gsum_own[1:2, :] = jnp.sum(dh1 * aunit, axis=0, keepdims=True) * share
    k.dproj[...] = norm_back(dh1 * gain(1), aunit, k.ra[...]).astype(LOW)
    pair("dproj", k.dproj)
    k.dout[...] = dot_plain(k.dproj[...], k.ow[...]).astype(LOW)
    grads.spread(5)

    key_terms = jnp.zeros((W * T, HD), FULL)
    value_terms = jnp.zeros((W * T, HD), FULL)
    for h in range(c.heads):
        cols = pl.ds(h * HD, HD)
        w = k.w[h]
        dout = k.dout[:, cols]
        query = k.queries[:, cols]
        delta = jnp.sum(
            dout.astype(FULL) * k.attended[:, cols].astype(FULL), axis=1, keepdims=True
        )
        dprob = dot_last(dout, k.values[...])
        dscore = w * (dprob - delta) * scaling
        k.dq[:, cols] = dot_plain(dscore.astype(LOW), k.keys[...])
        key_terms = key_terms + dot_plain(jnp.transpose(dscore).astype(LOW), query)
        value_terms = value_terms + dot_plain(jnp.transpose(w).astype(LOW), dout)
    k.terms[:, pl.ds(0, HD)] = key_terms.astype(LOW)
    k.terms[:, pl.ds(HD, HD)] = value_terms.astype(LOW)
    scatter = [
        send(
            k.terms.at[pl.ds(d * T, T)],
            k.terms_in.at[d - 1],
            (k.sc_s, k.sc_r),
            d - 1,
            p.down_ids[d - 1],
        )
        for d in range(1, W)
    ]
    sent.extend(scatter)
    cos0, sin0 = (k.cosine[pl.ds(0, T)], k.sine[pl.ds(0, T)])
    dg_q = jnp.zeros((1, HD), FULL)
    for h in range(c.heads):
        cols = pl.ds(h * HD, HD)
        dqn = unrotate(k.dq[:, cols], cos0, sin0)
        unit = k.qunit[:, cols]
        dg_q = dg_q + jnp.sum(dqn * unit, axis=0, keepdims=True)
        k.dqp[:, cols] = norm_back(dqn * g_q(), unit, k.rq[h]).astype(LOW)
    k.gsum_own[4:5, pl.ds(0, HD)] = dg_q
    pair("dqp", k.dqp, True)
    transposed("xn2", k.xn2)
    grad(3, "dgate", k.dgate)
    grad(4, "dup", k.dup)
    dxn1 = dot_last(k.dqp[...], k.qw[...])
    grads.spread(3)
    dkv = k.terms[pl.ds(0, T), :].astype(FULL)
    for d in range(1, W):
        scatter[d - 1].wait_recv()
        dkv = dkv + k.terms_in[d - 1].astype(FULL)
    dkn = unrotate(dkv[:, :HD], cos0, sin0)
    kunit = k.kunit[...]
    k.gsum_own[5:6, pl.ds(0, HD)] = jnp.sum(dkn * kunit, axis=0, keepdims=True)
    k.dkvp[:, pl.ds(0, HD)] = norm_back(dkn * g_k(), kunit, k.rk[...]).astype(LOW)
    k.dkvp[:, pl.ds(HD, HD)] = dkv[:, HD:].astype(LOW)
    pair("dkvp", k.dkvp, True)
    last = tp_start(3, dxn1 + dot_last(k.dkvp[...], k.kvw[...]))
    grads.spread(4)
    transposed("dproj", k.dproj)
    grad(2, "attended", k.attended)
    transposed("xn1", k.xn1)
    grad(0, "dqp", k.dqp)
    grads.share(5, grads.collect(5))
    grads.spread(2)
    dxn1 = tp_total(3, last)
    unit1 = k.unit1[...]
    k.gsum_own[0:1, :] = jnp.sum(dxn1 * unit1, axis=0, keepdims=True) * share
    grad(1, "dkvp", k.dkvp)
    grads.spread(0)
    k.kv_done[...] = grads.summed(1).astype(LOW)
    kvs = [
        send(k.kv_done, k.kv_in.at[d - 1], (k.kt_s, k.kt_r), d - 1, p.t_ids[d - 1])
        for d in range(1, TP)
    ]
    sent.extend(kvs)
    gain_near = send(k.gsum_own, k.gsum_in.at[0], (k.gr_s, k.gr_r), 0, p.near_id)
    k.xg[...] = k.dh1[...] + norm_back(dxn1 * gain(0), unit1, k.r1[...])
    leave(k.xg, k.h_xg)
    grads.share(3, grads.collect(3))
    gain_near.wait_recv()
    k.gsum_mid[0] = k.gsum_own[...] + k.gsum_in[0]
    gain_far = send(k.gsum_mid.at[0], k.gsum_in.at[1], (k.gr_s, k.gr_r), 1, p.far_id)
    sent.extend([gain_near, gain_far])
    total = k.kv_done[...].astype(FULL)
    for d in range(1, TP):
        kvs[d - 1].wait_recv()
        total = total + k.kv_in[d - 1].astype(FULL)
    grads.spread(1, total)
    grads.share(4, grads.collect(4))
    gain_far.wait_recv()
    k.gsum_z[p.shard] = k.gsum_mid[0] + k.gsum_in[1]
    gains_z = [
        send(k.gsum_z.at[p.shard], k.gsum_z.at[p.shard], (k.gh_s, k.gh_r), d - 1, p.z_ids[d - 1])
        for d in range(1, S)
    ]
    sent.extend(gains_z)
    grads.share(2, grads.collect(2))
    for item in gains_z:
        item.wait_recv()
    total = k.gsum_z[0]
    for s in range(1, S):
        total = total + k.gsum_z[s]
    if c.groups > 1:
        k.gsum_g[p.group] = total
        moved = [
            send(k.gsum_g.at[p.group], k.gsum_g.at[p.group], (k.gi_s, k.gi_r), d - 1, p.g_ids[d - 1])
            for d in range(1, c.groups)
        ]
        sent.extend(moved)
        for item in moved:
            item.wait_recv()
        total = k.gsum_g[0]
        for g in range(1, c.groups):
            total = total + k.gsum_g[g]
    k.gsum_t[p.tp] = total
    gains_t = [
        send(k.gsum_t.at[p.tp], k.gsum_t.at[p.tp], (k.gj_s, k.gj_r), d - 1, p.t_ids[d - 1])
        for d in range(1, TP)
    ]
    sent.extend(gains_t)
    grads.share(0, grads.collect(0))
    grads.share(1, grads.collect(1))
    for item in gains_t:
        item.wait_recv()
    total = k.gsum_t[0]
    for t in range(1, TP):
        total = total + k.gsum_t[t]
    k.gsum[...] = total
    hbm = [k.h_q, k.h_kv, k.h_o, k.h_gate, k.h_up, k.h_down]
    for a in c.order:
        grads.arrived(a)
        leave(grads.outs[a], hbm[a])
    grads.end()
    weights.end()
    for item in left:
        item.wait()
    for item in sent:
        item.wait_send()


def run_block(c, lengths, freq, x, dy, gain_in, weights):
    T, D, R, S, W, F, HQ = (c.T, c.D, c.R, c.S, c.W, c.F, c.HQ)
    names, operands, in_specs = ([], [], [])
    vm, anywhere = (
        pl.BlockSpec(memory_space=pltpu.VMEM),
        pl.BlockSpec(memory_space=pl.ANY),
    )

    def operand(name, value, spec):
        names.append(name)
        operands.append(value)
        in_specs.append(spec)

    operand("lengths", lengths, pl.BlockSpec(memory_space=pltpu.SMEM))
    operand("freq", freq, vm)
    operand("x", x, vm)
    operand("dy", dy, vm)
    operand("gain_in", gain_in, vm)
    for name, value in zip(("q", "k", "v", "o", "gate", "up", "down"), weights):
        operand(name + "_in", value, anywhere)
    outs = [(f"h_{name}", (R, width), LOW) for name, width in zip(PARTS, c.full)]
    outs.extend([("h_y", (T, D), FULL), ("h_xg", (T, D), FULL), ("gsum", (8, D), FULL)])
    names.extend([item[0] for item in outs])
    scratch = []

    def vmem(name, shape, dtype):
        names.append(name)
        scratch.append(pltpu.VMEM(shape, dtype))

    def sem(name, *shape):
        for end in ("_s", "_r"):
            names.append(name + end)
            scratch.append(pltpu.SemaphoreType.DMA(shape))

    for name, width in zip(PARTS, c.full):
        vmem("o_" + name, (R, width), LOW)
    vmem("y", (T, D), FULL)
    vmem("xg", (T, D), FULL)
    names.append("leave")
    scratch.append(pltpu.SemaphoreType.DMA((8,)))
    for name, width in zip(("qw", "kvw", "ow", "gw", "uw", "dw"), c.full):
        vmem(name, (D, width), LOW)
    vmem("gains_at", (S,) + gain_in.shape, FULL)
    vmem("wide_gain", (8, D), FULL)
    vmem("head_gain", (8, HD), FULL)
    for name in ("unit1", "aunit", "h1", "unit2", "dh1"):
        vmem(name, (T, D), FULL)
    for name in ("r1", "ra", "r2", "rk"):
        vmem(name, (T, 1), FULL)
    for name in ("unit_low", "xn1", "xn2", "dffn"):
        vmem(name, (T, D), LOW)
    vmem("unit_win", (max(W - 1, 1) * T, D), LOW)
    vmem("left_t", (D, 2 * T), LOW)
    for name in ("cosine", "sine"):
        vmem(name, (W * T, HD // 2), FULL)
    vmem("mask", (T, W * T), FULL)
    vmem("qunit", (T, HQ), FULL)
    vmem("rq", (c.heads, T, 1), FULL)
    for name in ("queries", "attended", "dout", "dqp"):
        vmem(name, (T, HQ), LOW)
    vmem("dq", (T, HQ), FULL)
    vmem("dkvp", (T, 2 * HD), LOW)
    for name in ("keys", "values"):
        vmem(name, (W * T, HD), LOW)
    vmem("kunit", (T, HD), FULL)
    vmem("w", (c.heads, T, W * T), FULL)
    for name in ("act", "slope"):
        vmem(name, (T, F), FULL)
    for name in ("hidden", "dup", "dgate"):
        vmem(name, (T, F), LOW)
    vmem("part", (4, T, D), LOW)
    vmem("part_in", (4, max(c.TP - 1, 1), T, D), LOW)
    vmem("terms", (W * T, 2 * HD), LOW)
    vmem("terms_in", (max(W - 1, 1), T, 2 * HD), LOW)
    for name, width in zip(("g_q", "g_kv", "g_o", "g_gate", "g_up", "g_down"), c.full):
        vmem(name, (D, width // 2), LOW)
    for name in ("half", "mine"):
        vmem(name, (D, c.wide), LOW)
    vmem("right", (2 * T, max(c.full) // 2), LOW)
    for name in PAIRS[:4]:
        vmem("far_" + name, (T, D), LOW)
    for name, width in zip(PAIRS[4:], (HQ, F, F, F, HQ, 2 * HD), strict=True):
        vmem("far_" + name, (T, width // 2), LOW)
    vmem("dproj", (T, D), LOW)
    sem("px", len(PAIRS))
    vmem("arrived", (S - 1, R, c.wide), LOW)
    if c.groups > 1:
        vmem("grouped", (c.groups, R, c.wide), LOW)
        sem("gg", c.groups - 1, 6)
        vmem("gsum_g", (c.groups, 8, D), FULL)
        sem("gi", c.groups - 1)
    vmem("kv_done", (D, c.width[1]), LOW)
    vmem("kv_in", (max(c.TP - 1, 1), D, c.width[1]), LOW)
    vmem("gsum_own", (8, D), FULL)
    vmem("gsum_in", (2, 8, D), FULL)
    vmem("gsum_mid", (1, 8, D), FULL)
    vmem("gsum_z", (S, 8, D), FULL)
    vmem("gsum_t", (c.TP, 8, D), FULL)
    names.append("local")
    scratch.append(pltpu.SemaphoreType.DMA((7,)))
    for name in ("za", "fa", "na", "ca"):
        sem(name, S - 1, 6)
    sem("zo", 2, 6)
    sem("zf", S - 1, 6)
    sem("gn", S - 1)
    sem("un", max(W - 1, 1))
    sem("tp", 4, max(c.TP - 1, 1))
    sem("gc", 6)
    sem("gz", S - 1, 6)
    sem("gs", 3, 6)
    sem("sc", max(W - 1, 1))
    sem("gr", 2)
    sem("gh", S - 1)
    sem("gj", max(c.TP - 1, 1))
    sem("kt", max(c.TP - 1, 1))
    return pl.pallas_call(
        functools.partial(block_kernel, c, names),
        out_shape=[jax.ShapeDtypeStruct(shape, kind) for _, shape, kind in outs],
        in_specs=in_specs,
        out_specs=[anywhere] * 8 + [vm],
        scratch_shapes=scratch,
        compiler_params=pltpu.CompilerParams(
            collective_id=0, has_side_effects=True, vmem_limit_bytes=58 * 1024 * 1024
        ),
        name="block",
    )(*operands)


def finish_kernel(c, *refs):
    ins, gsum, outs, small, stage, lows, through, sems, own_sems = (
        refs[:8],
        refs[8],
        refs[9:18],
        refs[18],
        refs[19:26],
        refs[26:32],
        refs[32],
        refs[33],
        refs[34],
    )
    copies = []

    def put(src, dst):
        copy = pltpu.make_async_copy(src, dst, sems.at[len(copies)])
        copy.start()
        copies.append(copy)

    taken = []
    for a in (5, 3, 4, 0, 2, 1):
        copy = pltpu.make_async_copy(ins[a], lows[a], own_sems.at[a])
        copy.start()
        taken.append((a, copy))
    for a in (6, 7):
        copy = pltpu.make_async_copy(ins[a], through.at[a - 6], own_sems.at[a])
        copy.start()
        taken.append((a, copy))
    shard = lax.axis_index("shard")
    for row, width in ((0, c.D), (4, HD)):
        part = gsum[...] if width == c.D else gsum[:, :HD]
        moved = pltpu.roll(part, lax.rem(width - shard * (width // c.S), width), 1)
        if row == 0:
            small[0:4, :] = moved[0:4, : small.shape[1]]
        else:
            small[4:8, :] = moved[4:8, : small.shape[1]]
    at = {0: (0,), 1: (1, 2), 2: (3,), 3: (4,), 4: (5,), 5: (6,)}
    for a, copy in taken:
        copy.wait()
        if a >= 6:
            put(through.at[a - 6], outs[a + 1])
            continue
        for j, slot in enumerate(at[a]):
            width = stage[slot].shape[1]
            stage[slot][...] = lows[a][:, j * width : (j + 1) * width].astype(FULL)
            put(stage[slot], outs[slot])
    for copy in copies:
        copy.wait()


def finish(c, parts, gsum):
    R = c.R
    widths = [c.HQ, HD, HD, c.HQ, c.F, c.F, c.F]
    vm, anywhere = (
        pl.BlockSpec(memory_space=pltpu.VMEM),
        pl.BlockSpec(memory_space=pl.ANY),
    )
    lanes = max(-(-c.R // LANES) * LANES, LANES)
    return pl.pallas_call(
        functools.partial(finish_kernel, c),
        out_shape=[jax.ShapeDtypeStruct((R, width), FULL) for width in widths]
        + [jax.ShapeDtypeStruct(item.shape, FULL) for item in parts[6:]]
        + [jax.ShapeDtypeStruct((8, lanes), FULL)],
        in_specs=[anywhere] * 8 + [vm],
        out_specs=[anywhere] * 9 + [vm],
        scratch_shapes=[pltpu.VMEM((R, width), FULL) for width in widths]
        + [pltpu.VMEM((R, width), LOW) for width in c.full]
        + [pltpu.VMEM((2,) + parts[6].shape, FULL)]
        + [pltpu.SemaphoreType.DMA((9,)), pltpu.SemaphoreType.DMA((8,))],
        compiler_params=pltpu.CompilerParams(vmem_limit_bytes=58 * 1024 * 1024),
        name="finish",
    )(*parts, gsum)


def per_device(
    block_input,
    out_cotangent,
    seq_lengths,
    q_weight,
    k_weight,
    v_weight,
    o_weight,
    gate_weight,
    up_weight,
    down_weight,
    attn_in_gain,
    attn_out_gain,
    ffn_in_gain,
    ffn_out_gain,
    query_gain,
    key_gain,
):
    tokens, width = block_input.shape
    n_ctx = lax.axis_size("ctx")
    n_shard = lax.axis_size("shard")
    longest = tokens * n_ctx // 2
    window = min(n_ctx, -(-(longest - 1) // tokens) + 1)
    c = Sizes(
        n_shard,
        n_ctx,
        lax.axis_size("tp"),
        tokens,
        width,
        q_weight.shape[1],
        gate_weight.shape[1],
        window,
    )
    gains = (attn_in_gain, attn_out_gain, ffn_in_gain, ffn_out_gain, query_gain, key_gain)
    lanes = -(-c.R // LANES) * LANES
    packed = jnp.zeros((8 * lanes,), FULL)
    for row, item in enumerate(gains):
        behind = (8 - row) * lanes - item.shape[0]
        packed = packed + jnp.pad(item.astype(FULL), (row * lanes, behind))
    packed = packed.reshape(8, lanes)
    freq = rope_base ** (-np.arange(HD // 2).astype(np.float32) * np.float32(2.0 / HD))
    outs = run_block(
        c,
        seq_lengths,
        jnp.asarray(freq.astype(np.float32)[None, :]),
        block_input,
        out_cotangent,
        packed,
        (q_weight, k_weight, v_weight, o_weight, gate_weight, up_weight, down_weight),
    )
    big = finish(c, outs[:8], outs[8])
    small = [
        big[9][row, : (width if row < 4 else HD) // n_shard] for row in range(len(gains))
    ]
    return (big[7], big[8], *big[:7], *small)


def solution(mesh):
    rows = P(("shard", "ctx"), None)
    split = P("shard", "tp")
    whole = P("shard", None)
    line = P("shard")
    return jax.shard_map(
        per_device,
        mesh=mesh,
        in_specs=(rows, rows, whole, split, whole, whole) + (split,) * 4 + (line,) * 6,
        out_specs=(rows, rows, split, whole, whole) + (split,) * 4 + (line,) * 6,
        check_vma=False,
    )
```

```python
import functools

import jax
import jax.numpy as jnp
import numpy as np
from jax import lax
from jax.experimental import pallas as pl
from jax.experimental.pallas import tpu as pltpu
from jax.sharding import PartitionSpec as P

HD = 256
MESH = pl.DeviceIdType.MESH
LANES = 128
WAYS = 4
TILE = 256
LOW, FULL = (jnp.bfloat16, jnp.float32)
PAIRS = ("xn1", "xn2", "dffn", "dproj", "attended", "hidden", "dgate", "dup", "dqp", "dkvp")
PARTS = ("q", "kv", "o", "gate", "up", "down")

eps = 1e-06
rope_base = 1000000.0
gelu_c = 0.7978845608028654
gelu_k = 0.044715


def dot_plain(left, right):
    return jnp.dot(left, right, preferred_element_type=FULL)


def dot_last(left, right):
    return lax.dot_general(
        left, right, (((1,), (1,)), ((), ())), preferred_element_type=FULL
    )


def dot_first(left, right):
    return lax.dot_general(
        left, right, (((0,), (0,)), ((), ())), preferred_element_type=FULL
    )


def norm_parts(value):
    scale = lax.rsqrt(jnp.mean(value * value, axis=-1, keepdims=True) + eps)
    return (value * scale, scale)


def norm_back(dnormed, unit, scale):
    return scale * (dnormed - unit * jnp.mean(dnormed * unit, axis=-1, keepdims=True))


def rotate(value, cosine, sine):
    half = value.shape[-1] // 2
    first, second = (value[..., :half], value[..., half:])
    return jnp.concatenate(
        [first * cosine - second * sine, second * cosine + first * sine], axis=-1
    )


def unrotate(value, cosine, sine):
    half = value.shape[-1] // 2
    first, second = (value[..., :half], value[..., half:])
    return jnp.concatenate(
        [first * cosine + second * sine, second * cosine - first * sine], axis=-1
    )


def greet(peers):
    barrier = pltpu.get_barrier_semaphore()
    for peer in peers:
        pl.semaphore_signal(barrier, inc=1, device_id=peer, device_id_type=MESH)
    pl.semaphore_wait(barrier, len(peers))


def remote(src, dst, send_sem, recv_sem, peer):
    return pltpu.make_async_remote_copy(
        src_ref=src,
        dst_ref=dst,
        send_sem=send_sem,
        recv_sem=recv_sem,
        device_id=peer,
        device_id_type=MESH,
    )


def send(src, dst, sems, where, peer):
    copy = remote(src, dst, sems[0].at[where], sems[1].at[where], peer)
    copy.start()
    return copy


def columns(member, width):
    return pl.ds(pl.multiple_of(member * width, LANES), width)


def block_rows(index, count):
    return pl.ds(pl.multiple_of(index * count, 16), count)


class Sizes:
    def __init__(self, shard, ctx, tp, tokens, deep, qcols, ff, window):
        self.S, self.C, self.TP = (shard, ctx, tp)
        self.T, self.D, self.R = (tokens, deep, deep // shard)
        self.HQ, self.F, self.W = (qcols, ff, window)
        self.heads = qcols // HD
        self.groups = ctx // WAYS
        self.full = [qcols, 2 * HD, qcols, ff, ff, ff]
        self.width = [item // WAYS for item in self.full]
        self.order = [5, 3, 4, 2, 0, 1]
        self.at = {}
        total = 0
        for a in self.order:
            self.at[a] = total
            total = total + self.width[a]
        self.wide = total


class Named:
    def __init__(self, names, refs):
        for name, ref in zip(names, refs, strict=True):
            setattr(self, name, ref)


class Place:
    def __init__(self, c):
        shard, ctx, tp = (
            lax.axis_index("shard"),
            lax.axis_index("ctx"),
            lax.axis_index("tp"),
        )
        core = lax.rem(ctx, 2)
        high = lax.rem(lax.div(ctx, 2), 2)
        near, far = (ctx + 1 - 2 * core, ctx + 2 - 4 * high)
        self.shard, self.ctx, self.tp = (shard, ctx, tp)
        self.member, self.other = (lax.rem(ctx, WAYS), lax.rem(far, WAYS))
        self.core, self.high = (core, high)
        self.group = lax.div(ctx, WAYS)
        self.near_id, self.far_id = ((shard, near, tp), (shard, far, tp))
        self.diag_id = (shard, near + far - ctx, tp)
        left, right = (shard, c.S - 1 - shard)
        least = jnp.minimum(left, right)
        self.far_by = []
        for i in range(c.S - 1):
            hop = i // 2 + 1
            both = hop if i % 2 == 0 else c.S - hop
            alone = i - least + 1
            alone = jnp.where(left > right, alone, c.S - alone)
            self.far_by.append(jnp.where(i < 2 * least, both, alone))
        self.last = c.S - 1
        self.at_end = (shard == 0) | (shard == c.S - 1)
        self.next_to_end = (shard == 1) | (shard == c.S - 2)
        self.after_id = (jnp.minimum(shard + 1, c.S - 1), ctx, tp)
        self.before_id = (jnp.maximum(shard - 1, 0), ctx, tp)
        self.z_ids = [(lax.rem(shard + d, c.S), ctx, tp) for d in range(1, c.S)]
        self.up_ids = [(shard, lax.rem(ctx + d, c.C), tp) for d in range(1, c.C)]
        self.down_ids = [
            (shard, lax.rem(ctx - d + c.C, c.C), tp) for d in range(1, c.C)
        ]
        self.g_ids = [
            (shard, lax.rem(ctx + WAYS * d, c.C), tp) for d in range(1, c.groups)
        ]
        self.t_ids = [(shard, ctx, lax.rem(tp + d, c.TP)) for d in range(1, c.TP)]


    def by_early(self, d):
        last = self.last
        first_end = (self.shard == 0) & (d == last)
        return first_end | ((self.shard == last) & (d == 1))

    def joined(self, d):
        last = self.last
        low = (self.shard == 1) & (d == last - 1)
        return low | ((self.shard == last - 1) & (d == 2))

    def not_from(self, d):
        last = self.last
        return ((self.shard == last) & (d == last)) | ((self.shard == 0) & (d == 1))


class Gather:
    def __init__(self, c, p, k):
        self.c, self.p, self.k = (c, p, k)
        self.src = [k.q_in, None, k.o_in, k.gate_in, k.up_in, k.down_in]
        self.dst = [k.qw, k.kvw, k.ow, k.gw, k.uw, k.dw]
        self.first, self.across, self.landing, self.own = ([], {}, {}, [])

    def local(self, src, dst):
        copy = pltpu.make_async_copy(src, dst, self.k.local.at[len(self.own)])
        copy.start()
        self.own.append(copy)

    def start_own(self):
        c, p, k = (self.c, self.p, self.k)
        rows = block_rows(p.shard, c.R)
        self.local(k.k_in, k.kvw.at[rows, pl.ds(0, HD)])
        self.local(k.v_in, k.kvw.at[rows, pl.ds(HD, HD)])
        for a in (0, 2, 3, 4, 5):
            self.local(self.src[a], self.dst[a].at[rows])

    def start(self, a):
        c, p, k = (self.c, self.p, self.k)
        cols = columns(p.member, c.width[a])
        rows = block_rows(p.shard, c.R)
        src = self.dst[a].at[rows, cols] if a == 1 else self.src[a].at[:, cols]
        for side, ok, peer, at in (
            (0, p.shard < c.S - 1, p.after_id, 0),
            (1, p.shard > 0, p.before_id, c.S - 2),
        ):
            copy = remote(
                src,
                self.dst[a].at[rows, cols],
                k.zo_s.at[side, a],
                k.za_r.at[at, a],
                peer,
            )
            pl.when(ok)(copy.start)
            self.first.append((ok, copy))

    def piece(self, i, a, member):
        c, p = (self.c, self.p)
        source = lax.rem(p.shard - p.far_by[i] + c.S, c.S)
        return self.dst[a].at[block_rows(source, c.R), columns(member, c.width[a])]

    def relay(self, a, i):
        c, p, k = (self.c, self.p, self.k)
        middle = (p.shard > 0) & (p.shard < c.S - 1)
        d = p.far_by[i]
        block = self.piece(i, a, p.member)
        up = d <= p.shard
        target = jnp.where(up, p.shard + 1, p.shard - 1)
        target = jnp.clip(target, 0, c.S - 1)
        there = jnp.clip(jnp.where(up, d, d - 2), 0, c.S - 2)
        copy = remote(
            block,
            block,
            k.zf_s.at[i, a],
            k.za_r.at[there, a],
            (target, p.ctx, p.tp),
        )
        remote(block, block, k.zf_s.at[i, a], k.za_r.at[d - 1, a], p.far_id).wait_recv()
        pl.when(middle)(copy.start)
        self.first.append((middle, copy))
        self.across[i, a] = send(block, block, (k.fa_s, k.fa_r), (i, a), p.far_id)
        self.landing.setdefault(a, []).append(
            send(block, block, (k.na_s, k.na_r), (i, a), p.near_id)
        )

    def pass_on(self, a, i):
        p, k = (self.p, self.k)
        self.across[i, a].wait_recv()
        block = self.piece(i, a, p.other)
        self.landing[a].append(send(block, block, (k.ca_s, k.ca_r), (i, a), p.near_id))

    def ready(self, a):
        for item in self.landing[a]:
            item.wait_recv()

    def end(self):
        for ok, copy in self.first:
            pl.when(ok)(copy.wait_send)
        for group in (self.across.values(), *self.landing.values()):
            for item in group:
                item.wait_send()


class Reduce:
    def __init__(self, c, p, k):
        self.c, self.p, self.k = (c, p, k)
        self.grads = [k.g_q, k.g_kv, k.g_o, k.g_gate, k.g_up, k.g_down]
        self.outs = [k.o_q, k.o_kv, k.o_o, k.o_gate, k.o_up, k.o_down]
        self.near, self.along, self.early, self.shared, self.ends = ({}, {}, {}, {}, [])

    def span(self, a):
        return pl.ds(self.c.at[a], self.c.width[a])

    def start(self, a):
        c, p, k = (self.c, self.p, self.k)
        self.near[a] = send(
            self.grads[a].at[:, columns(1 - p.core, c.width[a])],
            k.half.at[:, self.span(a)],
            (k.gc_s, k.gc_r),
            a,
            p.near_id,
        )

    def summed(self, a):
        c, p, k = (self.c, self.p, self.k)
        self.near[a].wait_recv()
        return k.half[:, self.span(a)].astype(FULL) + self.grads[a][
            :, columns(p.core, c.width[a])
        ].astype(FULL)

    def spread(self, a, total=None):
        c, p, k = (self.c, self.p, self.k)
        total = self.summed(a) if total is None else total
        k.mine[:, self.span(a)] = total.astype(LOW)
        span = self.span(a)
        self.along[a] = [
            remote(
                k.mine.at[block_rows(p.z_ids[d - 1][0], c.R), span],
                k.arrived.at[d - 1, :, span],
                k.gz_s.at[d - 1, a],
                k.gz_r.at[d - 1, a],
                p.z_ids[d - 1],
            )
            for d in range(1, c.S)
        ]
        opposite = block_rows(c.S - 1 - p.shard, c.R)
        self.early[a] = remote(
            k.mine.at[opposite, span],
            k.early.at[:, span],
            k.ge_s.at[a],
            k.ge_r.at[a],
            (jnp.where(p.shard == 0, 1, c.S - 2), p.ctx, p.tp),
        )
        pl.when(p.at_end)(self.early[a].start)
        for d in range(1, c.S):
            ok = jnp.logical_not(p.by_early(d) | p.joined(d))
            pl.when(ok)(self.along[a][d - 1].start)

    def forward(self, a):
        c, p, k = (self.c, self.p, self.k)
        span = self.span(a)

        @pl.when(p.next_to_end)
        def _():
            self.early[a].wait_recv()
            rows = block_rows(jnp.where(p.shard == 1, c.S - 1, 0), c.R)
            total = k.mine[rows, span].astype(FULL) + k.early[:, span].astype(FULL)
            k.mine[rows, span] = total.astype(LOW)

        for d in sorted({2, c.S - 2}):
            pl.when(p.joined(d))(self.along[a][d - 1].start)

    def collect(self, a):
        c, p, k = (self.c, self.p, self.k)
        span = self.span(a)
        k.total[:, span] = k.mine[block_rows(p.shard, c.R), span].astype(FULL)
        for d in range(1, c.S):
            ok = jnp.logical_not(p.not_from(d))

            @pl.when(ok)
            def _(d=d):
                self.along[a][d - 1].wait_recv()
                k.total[:, span] = k.total[:, span] + k.arrived[d - 1, :, span].astype(FULL)

        total = k.total[:, span]
        if c.groups > 1:
            k.grouped[p.group, :, span] = total.astype(LOW)
            piece = k.grouped.at[p.group, :, span]
            moved = [
                send(piece, piece, (k.gg_s, k.gg_r), (d - 1, a), p.g_ids[d - 1])
                for d in range(1, c.groups)
            ]
            for item in moved:
                item.wait_recv()
            self.ends.extend(moved)
            total = k.grouped[0, :, span].astype(FULL)
            for g in range(1, c.groups):
                total = total + k.grouped[g, :, span].astype(FULL)
        return total

    def share(self, a, total):
        c, p, k = (self.c, self.p, self.k)
        cols = columns(p.member, c.width[a])
        self.outs[a][:, cols] = total.astype(LOW)
        piece = self.outs[a].at[:, cols]
        peers = (p.far_id, p.near_id) if a > 2 else (p.far_id, p.near_id, p.diag_id)
        self.shared[a] = [
            send(piece, piece, (k.gs_s, k.gs_r), (at, a), peer)
            for at, peer in enumerate(peers)
        ]

    def pass_on(self, a):
        c, p, k = (self.c, self.p, self.k)
        self.shared[a][0].wait_recv()
        piece = self.outs[a].at[:, columns(p.other, c.width[a])]
        self.shared[a].append(send(piece, piece, (k.gs_s, k.gs_r), (2, a), p.near_id))

    def arrived(self, a):
        for item in self.shared[a][1 if a > 2 else 0 :]:
            item.wait_recv()

    def end(self):
        for a in self.c.order:
            pl.when(self.p.at_end)(self.early[a].wait_send)
            for d in range(1, self.c.S):
                ok = jnp.logical_not(self.p.by_early(d))
                pl.when(ok)(self.along[a][d - 1].wait_send)
        for group in (
            self.near.values(),
            *self.shared.values(),
            self.ends,
        ):
            for item in group:
                item.wait_send()


def block_kernel(c, names, *refs):
    k = Named(names, refs)
    p = Place(c)
    T, D, F, W, S, TP = (c.T, c.D, c.F, c.W, c.S, c.TP)
    scaling = HD ** (-0.5)
    sent = []
    left = []

    def leave(src, dst):
        copy = pltpu.make_async_copy(src, dst, k.leave.at[len(left)])
        copy.start()
        left.append(copy)

    def tp_start(slot, value):
        k.part[slot] = value.astype(LOW)
        copies = [
            send(
                k.part.at[slot],
                k.part_in.at[slot, d - 1],
                (k.tp_s, k.tp_r),
                (slot, d - 1),
                p.t_ids[d - 1],
            )
            for d in range(1, TP)
        ]
        sent.extend(copies)
        return copies

    def tp_total(slot, copies):
        total = k.part[slot].astype(FULL)
        for d in range(1, TP):
            copies[d - 1].wait_recv()
            total = total + k.part_in[slot, d - 1].astype(FULL)
        return total

    paired = {}
    held = c.C == WAYS and W > 2

    def pair(name, value, half=False):
        width = value.shape[1] // 2
        src = value.at[:, columns(1 - p.high, width)] if half else value
        order = PAIRS.index(name)
        paired[name] = send(
            src, getattr(k, "far_" + name), (k.px_s, k.px_r), order, p.far_id
        )
        sent.append(paired[name])

    weights = Gather(c, p, k)
    weights.start_own()
    k.gains_at[p.shard] = k.gain_in[...]
    greet(p.z_ids + p.up_ids + p.t_ids)
    gain_copies = [
        send(
            k.gains_at.at[p.shard],
            k.gains_at.at[p.shard],
            (k.gn_s, k.gn_r),
            d - 1,
            p.z_ids[d - 1],
        )
        for d in range(1, S)
    ]
    sent.extend(gain_copies)
    weights.start(0)
    weights.own[0].wait()
    weights.own[1].wait()
    for a in range(1, 6):
        weights.start(a)
    unit1, r1 = norm_parts(k.x[...])
    k.unit1[...] = unit1
    k.r1[...] = r1
    k.unit_low[...] = unit1.astype(LOW)
    unit_copies = [
        send(
            k.unit_low,
            k.unit_win.at[pl.ds((d - 1) * T, T)],
            (k.un_s, k.un_r),
            d - 1,
            p.up_ids[d - 1],
        )
        for d in range(1, W)
    ]
    sent.extend(unit_copies)

    count = k.lengths.shape[1]
    lens = [k.lengths[0, j] for j in range(count)]
    ends = []
    for item in lens:
        ends.append(item if not ends else ends[-1] + item)

    def segment_of(index):
        return sum([(index >= end).astype(jnp.int32) for end in ends])

    def place_of(index):
        return index - sum([jnp.where(index >= e, n, 0) for e, n in zip(ends, lens)])

    q_index = p.ctx * T + lax.broadcasted_iota(jnp.int32, (T, T), 0)
    q_seg = segment_of(q_index)
    for d in range(W):
        base = lax.rem(p.ctx - d + c.C, c.C) * T
        k_index = base + lax.broadcasted_iota(jnp.int32, (T, T), 1)
        allowed = (q_seg == segment_of(k_index)) & (k_index <= q_index)
        k.mask[:, pl.ds(d * T, T)] = allowed.astype(FULL)
        rows = base + lax.broadcasted_iota(jnp.int32, (T, HD // 2), 0)
        angle = place_of(rows).astype(FULL) * k.freq[...]
        k.cosine[pl.ds(d * T, T)] = jnp.cos(angle)
        k.sine[pl.ds(d * T, T)] = jnp.sin(angle)

    for item in gain_copies:
        item.wait_recv()
    wide_gain = jnp.zeros((8, D), FULL)
    head_gain = jnp.zeros((8, HD), FULL)
    lanes = k.gain_in.shape[1]
    for s in range(S):
        part = k.gains_at[s].astype(LOW)
        for total in ("wide", "head"):
            width = D if total == "wide" else HD
            row = lax.broadcasted_iota(jnp.int32, (lanes, width), 0)
            col = lax.broadcasted_iota(jnp.int32, (lanes, width), 1)
            pick = (col == row + s * (width // S)).astype(FULL).astype(LOW)
            if total == "wide":
                wide_gain = wide_gain + dot_plain(part, pick)
            else:
                head_gain = head_gain + dot_plain(part, pick)
    k.wide_gain[...] = wide_gain
    k.head_gain[...] = head_gain

    def gain(row):
        return k.wide_gain[row : row + 1, :]

    g_q, g_k = (lambda: k.head_gain[4:5, :]), (lambda: k.head_gain[5:6, :])

    k.xn1[...] = (k.unit1[...] * gain(0)).astype(LOW)
    for item in weights.own[2:]:
        item.wait()

    def project():
        weights.ready(0)
        qp = dot_plain(k.xn1[...], k.qw[...])
        cos0, sin0 = (k.cosine[pl.ds(0, T)], k.sine[pl.ds(0, T)])
        for h in range(c.heads):
            cols = pl.ds(h * HD, HD)
            unit, scale = norm_parts(qp[:, h * HD : (h + 1) * HD])
            k.qunit[:, cols] = unit
            k.rq[h] = scale
            k.queries[:, cols] = rotate(unit * g_q(), cos0, sin0).astype(LOW)
        weights.ready(1)
        for d in range(W):
            rows = pl.ds(d * T, T)
            if d == 0:
                xw = k.xn1[...]
            else:
                unit_copies[d - 1].wait_recv()
                low = k.unit_win[pl.ds((d - 1) * T, T)]
                xw = (low.astype(FULL) * gain(0)).astype(LOW)
            kvp = dot_plain(xw, k.kvw[...])
            unit, scale = norm_parts(kvp[:, :HD])
            if d == 0:
                k.kunit[...] = unit
                k.rk[...] = scale
            k.keys[rows] = rotate(unit * g_k(), k.cosine[rows], k.sine[rows]).astype(LOW)
            k.values[rows] = kvp[:, HD:].astype(LOW)

    def attend(h):
        cols = pl.ds(h * HD, HD)
        raw = dot_last(k.queries[:, cols], k.keys[...]) * scaling
        logits = jnp.where(k.mask[...] > 0.5, raw, -1e30)
        peak = jnp.max(logits, axis=1, keepdims=True)
        lifted = jnp.exp(logits - peak)
        w = lifted * (1.0 / jnp.sum(lifted, axis=1, keepdims=True))
        k.w[h] = w
        k.attended[:, cols] = dot_plain(w.astype(LOW), k.values[...]).astype(LOW)

    proj_copies = []

    def output():
        weights.ready(2)
        proj_copies.extend(tp_start(0, dot_last(k.attended[...], k.ow[...])))

    steps = []
    reach = 0.0
    for a in range(6):
        reach = reach + c.width[a] / LANES
        for i in range(S - 1):
            steps.append((reach + 3.5 * i, len(steps), functools.partial(weights.relay, a, i)))
            steps.append((reach + 3.5 * i + 4.0, len(steps), functools.partial(weights.pass_on, a, i)))
    ready = 2.0 + 3.5 * (S - 2) + 4.0
    steps.append((ready + 0.3, len(steps), project))
    for h in range(c.heads):
        steps.append((ready + 0.6 + 0.3 * h, len(steps), functools.partial(attend, h)))
    steps.append((max(ready + 0.6 + 0.3 * c.heads, ready + 1.5), len(steps), output))
    for _, _, step in sorted(steps, key=lambda item: item[:2]):
        step()
    proj = tp_total(0, proj_copies)
    aunit, ra = norm_parts(proj)
    k.aunit[...] = aunit
    k.ra[...] = ra
    h1 = k.x[...] + aunit * gain(1)
    k.h1[...] = h1
    unit2, r2 = norm_parts(h1)
    k.unit2[...] = unit2
    k.r2[...] = r2
    k.xn2[...] = (unit2 * gain(2)).astype(LOW)
    pair("xn2", k.xn2)
    pair("attended", k.attended, True)
    weights.ready(3)
    weights.ready(4)

    for at in range(0, F, TILE):
        cols = pl.ds(at, TILE)
        gate = dot_plain(k.xn2[...], k.gw[:, cols])
        up = dot_plain(k.xn2[...], k.uw[:, cols])
        square = gate * gate
        bent = jnp.tanh(gelu_c * (gate + gelu_k * (square * gate)))
        half = 0.5 * (1.0 + bent)
        act = gate * half
        slope = half + 0.5 * gate * (1.0 - bent * bent) * (
            gelu_c * (1.0 + 3.0 * gelu_k * square)
        )
        k.act[:, cols] = act
        k.slope[:, cols] = up * slope
        k.hidden[:, cols] = (act * up).astype(LOW)
    pair("hidden", k.hidden, True)
    weights.ready(5)
    ffn = tp_total(1, tp_start(1, dot_last(k.hidden[...], k.dw[...])))
    funit, rf = norm_parts(ffn)
    k.y[...] = k.h1[...] + funit * gain(3)
    leave(k.y, k.h_y)

    grads = Reduce(c, p, k)
    share = 1.0 / TP
    dy = k.dy[...]
    k.gsum_own[...] = jnp.zeros(k.gsum_own.shape, FULL)
    k.gsum_own[3:4, :] = jnp.sum(dy * funit, axis=0, keepdims=True) * share
    dffn = norm_back(dy * gain(3), funit, rf).astype(LOW)
    k.dffn[...] = dffn

    pair("dffn", k.dffn)

    def transposed(name, own):
        if name == "xn1" and held:
            low = k.unit_win[pl.ds(T, T)]
            k.far_xn1[...] = (low.astype(FULL) * gain(0)).astype(LOW)
        else:
            paired[name].wait_recv()
        k.left_t[:, pl.ds(0, T)] = jnp.transpose(own[...].astype(FULL)).astype(LOW)
        far = getattr(k, "far_" + name)
        k.left_t[:, pl.ds(T, T)] = jnp.transpose(far[...].astype(FULL)).astype(LOW)

    def grad(a, name, own):
        paired[name].wait_recv()
        half = c.full[a] // 2
        k.right[pl.ds(0, T), pl.ds(0, half)] = own[:, columns(p.high, half)]
        k.right[pl.ds(T, T), pl.ds(0, half)] = getattr(k, "far_" + name)[...]
        for at in range(0, half, TILE):
            cols = pl.ds(at, TILE)
            grads.grads[a][:, cols] = dot_plain(k.left_t[...], k.right[:, cols]).astype(LOW)
        grads.start(a)

    for at in range(0, F, TILE):
        cols = pl.ds(at, TILE)
        dhid = dot_plain(k.dffn[...], k.dw[:, cols])
        k.dup[:, cols] = (dhid * k.act[:, cols]).astype(LOW)
        k.dgate[:, cols] = (dhid * k.slope[:, cols]).astype(LOW)
    pair("dgate", k.dgate, True)
    pair("dup", k.dup, True)
    if not held:
        pair("xn1", k.xn1)
    back = tp_start(
        2, dot_last(k.dgate[...], k.gw[...]) + dot_last(k.dup[...], k.uw[...])
    )
    transposed("dffn", k.dffn)
    grad(5, "hidden", k.hidden)
    dxn2 = tp_total(2, back)
    unit2 = k.unit2[...]
    k.gsum_own[2:3, :] = jnp.sum(dxn2 * unit2, axis=0, keepdims=True) * share
    dh1 = k.dy[...] + norm_back(dxn2 * gain(2), unit2, k.r2[...])
    k.dh1[...] = dh1
    aunit = k.aunit[...]
    k.gsum_own[1:2, :] = jnp.sum(dh1 * aunit, axis=0, keepdims=True) * share
    k.dproj[...] = norm_back(dh1 * gain(1), aunit, k.ra[...]).astype(LOW)
    pair("dproj", k.dproj)
    k.dout[...] = dot_plain(k.dproj[...], k.ow[...]).astype(LOW)
    grads.spread(5)

    key_terms = jnp.zeros((W * T, HD), FULL)
    value_terms = jnp.zeros((W * T, HD), FULL)
    for h in range(c.heads):
        cols = pl.ds(h * HD, HD)
        w = k.w[h]
        dout = k.dout[:, cols]
        query = k.queries[:, cols]
        delta = jnp.sum(
            dout.astype(FULL) * k.attended[:, cols].astype(FULL), axis=1, keepdims=True
        )
        dprob = dot_last(dout, k.values[...])
        dscore = w * (dprob - delta) * scaling
        k.dq[:, cols] = dot_plain(dscore.astype(LOW), k.keys[...])
        key_terms = key_terms + dot_plain(jnp.transpose(dscore).astype(LOW), query)
        value_terms = value_terms + dot_plain(jnp.transpose(w).astype(LOW), dout)
    k.terms[:, pl.ds(0, HD)] = key_terms.astype(LOW)
    k.terms[:, pl.ds(HD, HD)] = value_terms.astype(LOW)
    scatter = [
        send(
            k.terms.at[pl.ds(d * T, T)],
            k.terms_in.at[d - 1],
            (k.sc_s, k.sc_r),
            d - 1,
            p.down_ids[d - 1],
        )
        for d in range(1, W)
    ]
    sent.extend(scatter)
    grads.forward(5)
    cos0, sin0 = (k.cosine[pl.ds(0, T)], k.sine[pl.ds(0, T)])
    dg_q = jnp.zeros((1, HD), FULL)
    for h in range(c.heads):
        cols = pl.ds(h * HD, HD)
        dqn = unrotate(k.dq[:, cols], cos0, sin0)
        unit = k.qunit[:, cols]
        dg_q = dg_q + jnp.sum(dqn * unit, axis=0, keepdims=True)
        k.dqp[:, cols] = norm_back(dqn * g_q(), unit, k.rq[h]).astype(LOW)
    k.gsum_own[4:5, pl.ds(0, HD)] = dg_q
    pair("dqp", k.dqp, True)
    transposed("xn2", k.xn2)
    grad(3, "dgate", k.dgate)
    grad(4, "dup", k.dup)
    dxn1 = dot_last(k.dqp[...], k.qw[...])
    grads.spread(3)
    dkv = k.terms[pl.ds(0, T), :].astype(FULL)
    for d in range(1, W):
        scatter[d - 1].wait_recv()
        dkv = dkv + k.terms_in[d - 1].astype(FULL)
    dkn = unrotate(dkv[:, :HD], cos0, sin0)
    kunit = k.kunit[...]
    k.gsum_own[5:6, pl.ds(0, HD)] = jnp.sum(dkn * kunit, axis=0, keepdims=True)
    k.dkvp[:, pl.ds(0, HD)] = norm_back(dkn * g_k(), kunit, k.rk[...]).astype(LOW)
    k.dkvp[:, pl.ds(HD, HD)] = dkv[:, HD:].astype(LOW)
    pair("dkvp", k.dkvp, True)
    last = tp_start(3, dxn1 + dot_last(k.dkvp[...], k.kvw[...]))
    grads.forward(3)
    grads.spread(4)
    transposed("dproj", k.dproj)
    grad(2, "attended", k.attended)
    grads.share(5, grads.collect(5))
    transposed("xn1", k.xn1)
    grad(0, "dqp", k.dqp)
    grads.forward(4)
    grads.spread(2)
    dxn1 = tp_total(3, last)
    unit1 = k.unit1[...]
    k.gsum_own[0:1, :] = jnp.sum(dxn1 * unit1, axis=0, keepdims=True) * share
    grad(1, "dkvp", k.dkvp)
    grads.forward(2)
    grads.spread(0)
    k.kv_done[...] = grads.summed(1).astype(LOW)
    kvs = [
        send(k.kv_done, k.kv_in.at[d - 1], (k.kt_s, k.kt_r), d - 1, p.t_ids[d - 1])
        for d in range(1, TP)
    ]
    sent.extend(kvs)
    gain_near = send(k.gsum_own, k.gsum_in.at[0], (k.gr_s, k.gr_r), 0, p.near_id)
    k.xg[...] = k.dh1[...] + norm_back(dxn1 * gain(0), unit1, k.r1[...])
    leave(k.xg, k.h_xg)
    grads.share(3, grads.collect(3))
    grads.pass_on(5)
    gain_near.wait_recv()
    k.gsum_mid[0] = k.gsum_own[...] + k.gsum_in[0]
    gain_far = send(k.gsum_mid.at[0], k.gsum_in.at[1], (k.gr_s, k.gr_r), 1, p.far_id)
    sent.extend([gain_near, gain_far])
    total = k.kv_done[...].astype(FULL)
    for d in range(1, TP):
        kvs[d - 1].wait_recv()
        total = total + k.kv_in[d - 1].astype(FULL)
    grads.spread(1, total)
    grads.forward(0)
    grads.share(4, grads.collect(4))
    grads.pass_on(3)
    gain_far.wait_recv()
    k.gsum_z[p.shard] = k.gsum_mid[0] + k.gsum_in[1]
    gains_z = [
        send(k.gsum_z.at[p.shard], k.gsum_z.at[p.shard], (k.gh_s, k.gh_r), d - 1, p.z_ids[d - 1])
        for d in range(1, S)
    ]
    sent.extend(gains_z)
    grads.forward(1)
    grads.share(2, grads.collect(2))
    grads.pass_on(4)
    for item in gains_z:
        item.wait_recv()
    total = k.gsum_z[0]
    for s in range(1, S):
        total = total + k.gsum_z[s]
    if c.groups > 1:
        k.gsum_g[p.group] = total
        moved = [
            send(k.gsum_g.at[p.group], k.gsum_g.at[p.group], (k.gi_s, k.gi_r), d - 1, p.g_ids[d - 1])
            for d in range(1, c.groups)
        ]
        sent.extend(moved)
        for item in moved:
            item.wait_recv()
        total = k.gsum_g[0]
        for g in range(1, c.groups):
            total = total + k.gsum_g[g]
    k.gsum_t[p.tp] = total
    gains_t = [
        send(k.gsum_t.at[p.tp], k.gsum_t.at[p.tp], (k.gj_s, k.gj_r), d - 1, p.t_ids[d - 1])
        for d in range(1, TP)
    ]
    sent.extend(gains_t)
    grads.share(0, grads.collect(0))
    grads.share(1, grads.collect(1))
    for item in gains_t:
        item.wait_recv()
    total = k.gsum_t[0]
    for t in range(1, TP):
        total = total + k.gsum_t[t]
    k.gsum[...] = total
    hbm = [k.h_q, k.h_kv, k.h_o, k.h_gate, k.h_up, k.h_down]
    for a in c.order:
        grads.arrived(a)
        leave(grads.outs[a], hbm[a])
    grads.end()
    weights.end()
    for item in left:
        item.wait()
    for item in sent:
        item.wait_send()


def run_block(c, lengths, freq, x, dy, gain_in, weights):
    T, D, R, S, W, F, HQ = (c.T, c.D, c.R, c.S, c.W, c.F, c.HQ)
    names, operands, in_specs = ([], [], [])
    vm, anywhere = (
        pl.BlockSpec(memory_space=pltpu.VMEM),
        pl.BlockSpec(memory_space=pl.ANY),
    )

    def operand(name, value, spec):
        names.append(name)
        operands.append(value)
        in_specs.append(spec)

    operand("lengths", lengths, pl.BlockSpec(memory_space=pltpu.SMEM))
    operand("freq", freq, vm)
    operand("x", x, vm)
    operand("dy", dy, vm)
    operand("gain_in", gain_in, vm)
    for name, value in zip(("q", "k", "v", "o", "gate", "up", "down"), weights):
        operand(name + "_in", value, anywhere)
    outs = [(f"h_{name}", (R, width), LOW) for name, width in zip(PARTS, c.full)]
    outs.extend([("h_y", (T, D), FULL), ("h_xg", (T, D), FULL), ("gsum", (8, D), FULL)])
    names.extend([item[0] for item in outs])
    scratch = []

    def vmem(name, shape, dtype):
        names.append(name)
        scratch.append(pltpu.VMEM(shape, dtype))

    def sem(name, *shape):
        for end in ("_s", "_r"):
            names.append(name + end)
            scratch.append(pltpu.SemaphoreType.DMA(shape))

    for name, width in zip(PARTS, c.full):
        vmem("o_" + name, (R, width), LOW)
    vmem("y", (T, D), FULL)
    vmem("xg", (T, D), FULL)
    names.append("leave")
    scratch.append(pltpu.SemaphoreType.DMA((8,)))
    for name, width in zip(("qw", "kvw", "ow", "gw", "uw", "dw"), c.full):
        vmem(name, (D, width), LOW)
    vmem("gains_at", (S,) + gain_in.shape, FULL)
    vmem("wide_gain", (8, D), FULL)
    vmem("head_gain", (8, HD), FULL)
    for name in ("unit1", "aunit", "h1", "unit2", "dh1"):
        vmem(name, (T, D), FULL)
    for name in ("r1", "ra", "r2", "rk"):
        vmem(name, (T, 1), FULL)
    for name in ("unit_low", "xn1", "xn2", "dffn"):
        vmem(name, (T, D), LOW)
    vmem("unit_win", (max(W - 1, 1) * T, D), LOW)
    vmem("left_t", (D, 2 * T), LOW)
    for name in ("cosine", "sine"):
        vmem(name, (W * T, HD // 2), FULL)
    vmem("mask", (T, W * T), FULL)
    vmem("qunit", (T, HQ), FULL)
    vmem("rq", (c.heads, T, 1), FULL)
    for name in ("queries", "attended", "dout", "dqp"):
        vmem(name, (T, HQ), LOW)
    vmem("dq", (T, HQ), FULL)
    vmem("dkvp", (T, 2 * HD), LOW)
    for name in ("keys", "values"):
        vmem(name, (W * T, HD), LOW)
    vmem("kunit", (T, HD), FULL)
    vmem("w", (c.heads, T, W * T), FULL)
    for name in ("act", "slope"):
        vmem(name, (T, F), FULL)
    for name in ("hidden", "dup", "dgate"):
        vmem(name, (T, F), LOW)
    vmem("part", (4, T, D), LOW)
    vmem("part_in", (4, max(c.TP - 1, 1), T, D), LOW)
    vmem("terms", (W * T, 2 * HD), LOW)
    vmem("terms_in", (max(W - 1, 1), T, 2 * HD), LOW)
    for name, width in zip(("g_q", "g_kv", "g_o", "g_gate", "g_up", "g_down"), c.full):
        vmem(name, (D, width // 2), LOW)
    for name in ("half", "mine"):
        vmem(name, (D, c.wide), LOW)
    vmem("right", (2 * T, max(c.full) // 2), LOW)
    for name in PAIRS[:4]:
        vmem("far_" + name, (T, D), LOW)
    for name, width in zip(PAIRS[4:], (HQ, F, F, F, HQ, 2 * HD), strict=True):
        vmem("far_" + name, (T, width // 2), LOW)
    vmem("dproj", (T, D), LOW)
    sem("px", len(PAIRS))
    vmem("arrived", (S - 1, R, c.wide), LOW)
    vmem("early", (R, c.wide), LOW)
    vmem("total", (R, c.wide), FULL)
    sem("ge", 6)
    if c.groups > 1:
        vmem("grouped", (c.groups, R, c.wide), LOW)
        sem("gg", c.groups - 1, 6)
        vmem("gsum_g", (c.groups, 8, D), FULL)
        sem("gi", c.groups - 1)
    vmem("kv_done", (D, c.width[1]), LOW)
    vmem("kv_in", (max(c.TP - 1, 1), D, c.width[1]), LOW)
    vmem("gsum_own", (8, D), FULL)
    vmem("gsum_in", (2, 8, D), FULL)
    vmem("gsum_mid", (1, 8, D), FULL)
    vmem("gsum_z", (S, 8, D), FULL)
    vmem("gsum_t", (c.TP, 8, D), FULL)
    names.append("local")
    scratch.append(pltpu.SemaphoreType.DMA((7,)))
    for name in ("za", "fa", "na", "ca"):
        sem(name, S - 1, 6)
    sem("zo", 2, 6)
    sem("zf", S - 1, 6)
    sem("gn", S - 1)
    sem("un", max(W - 1, 1))
    sem("tp", 4, max(c.TP - 1, 1))
    sem("gc", 6)
    sem("gz", S - 1, 6)
    sem("gs", 3, 6)
    sem("sc", max(W - 1, 1))
    sem("gr", 2)
    sem("gh", S - 1)
    sem("gj", max(c.TP - 1, 1))
    sem("kt", max(c.TP - 1, 1))
    return pl.pallas_call(
        functools.partial(block_kernel, c, names),
        out_shape=[jax.ShapeDtypeStruct(shape, kind) for _, shape, kind in outs],
        in_specs=in_specs,
        out_specs=[anywhere] * 8 + [vm],
        scratch_shapes=scratch,
        compiler_params=pltpu.CompilerParams(
            collective_id=0, has_side_effects=True, vmem_limit_bytes=58 * 1024 * 1024
        ),
        name="block",
    )(*operands)


def finish_kernel(c, *refs):
    ins, gsum, outs, small, stage, lows, through, sems, own_sems = (
        refs[:8],
        refs[8],
        refs[9:18],
        refs[18],
        refs[19:26],
        refs[26:32],
        refs[32],
        refs[33],
        refs[34],
    )
    copies = []

    def put(src, dst):
        copy = pltpu.make_async_copy(src, dst, sems.at[len(copies)])
        copy.start()
        copies.append(copy)

    taken = []
    for a in (5, 3, 4, 0, 2, 1):
        copy = pltpu.make_async_copy(ins[a], lows[a], own_sems.at[a])
        copy.start()
        taken.append((a, copy))
    for a in (6, 7):
        copy = pltpu.make_async_copy(ins[a], through.at[a - 6], own_sems.at[a])
        copy.start()
        taken.append((a, copy))
    shard = lax.axis_index("shard")
    for row, width in ((0, c.D), (4, HD)):
        part = gsum[...] if width == c.D else gsum[:, :HD]
        moved = pltpu.roll(part, lax.rem(width - shard * (width // c.S), width), 1)
        if row == 0:
            small[0:4, :] = moved[0:4, : small.shape[1]]
        else:
            small[4:8, :] = moved[4:8, : small.shape[1]]
    at = {0: (0,), 1: (1, 2), 2: (3,), 3: (4,), 4: (5,), 5: (6,)}
    for a, copy in taken:
        copy.wait()
        if a >= 6:
            put(through.at[a - 6], outs[a + 1])
            continue
        for j, slot in enumerate(at[a]):
            width = stage[slot].shape[1]
            stage[slot][...] = lows[a][:, j * width : (j + 1) * width].astype(FULL)
            put(stage[slot], outs[slot])
    for copy in copies:
        copy.wait()


def finish(c, parts, gsum):
    R = c.R
    widths = [c.HQ, HD, HD, c.HQ, c.F, c.F, c.F]
    vm, anywhere = (
        pl.BlockSpec(memory_space=pltpu.VMEM),
        pl.BlockSpec(memory_space=pl.ANY),
    )
    lanes = max(-(-c.R // LANES) * LANES, LANES)
    return pl.pallas_call(
        functools.partial(finish_kernel, c),
        out_shape=[jax.ShapeDtypeStruct((R, width), FULL) for width in widths]
        + [jax.ShapeDtypeStruct(item.shape, FULL) for item in parts[6:]]
        + [jax.ShapeDtypeStruct((8, lanes), FULL)],
        in_specs=[anywhere] * 8 + [vm],
        out_specs=[anywhere] * 9 + [vm],
        scratch_shapes=[pltpu.VMEM((R, width), FULL) for width in widths]
        + [pltpu.VMEM((R, width), LOW) for width in c.full]
        + [pltpu.VMEM((2,) + parts[6].shape, FULL)]
        + [pltpu.SemaphoreType.DMA((9,)), pltpu.SemaphoreType.DMA((8,))],
        compiler_params=pltpu.CompilerParams(vmem_limit_bytes=58 * 1024 * 1024),
        name="finish",
    )(*parts, gsum)


def per_device(
    block_input,
    out_cotangent,
    seq_lengths,
    q_weight,
    k_weight,
    v_weight,
    o_weight,
    gate_weight,
    up_weight,
    down_weight,
    attn_in_gain,
    attn_out_gain,
    ffn_in_gain,
    ffn_out_gain,
    query_gain,
    key_gain,
):
    tokens, width = block_input.shape
    n_ctx = lax.axis_size("ctx")
    n_shard = lax.axis_size("shard")
    longest = tokens * n_ctx // 2
    window = min(n_ctx, -(-(longest - 1) // tokens) + 1)
    c = Sizes(
        n_shard,
        n_ctx,
        lax.axis_size("tp"),
        tokens,
        width,
        q_weight.shape[1],
        gate_weight.shape[1],
        window,
    )
    gains = (attn_in_gain, attn_out_gain, ffn_in_gain, ffn_out_gain, query_gain, key_gain)
    lanes = -(-c.R // LANES) * LANES
    packed = jnp.zeros((8 * lanes,), FULL)
    for row, item in enumerate(gains):
        behind = (8 - row) * lanes - item.shape[0]
        packed = packed + jnp.pad(item.astype(FULL), (row * lanes, behind))
    packed = packed.reshape(8, lanes)
    freq = rope_base ** (-np.arange(HD // 2).astype(np.float32) * np.float32(2.0 / HD))
    outs = run_block(
        c,
        seq_lengths,
        jnp.asarray(freq.astype(np.float32)[None, :]),
        block_input,
        out_cotangent,
        packed,
        (q_weight, k_weight, v_weight, o_weight, gate_weight, up_weight, down_weight),
    )
    big = finish(c, outs[:8], outs[8])
    small = [
        big[9][row, : (width if row < 4 else HD) // n_shard] for row in range(len(gains))
    ]
    return (big[7], big[8], *big[:7], *small)


def solution(mesh):
    rows = P(("shard", "ctx"), None)
    split = P("shard", "tp")
    whole = P("shard", None)
    line = P("shard")
    return jax.shard_map(
        per_device,
        mesh=mesh,
        in_specs=(rows, rows, whole, split, whole, whole) + (split,) * 4 + (line,) * 6,
        out_specs=(rows, rows, split, whole, whole) + (split,) * 4 + (line,) * 6,
        check_vma=False,
    )
```

```python
import functools

import jax
import jax.numpy as jnp
import numpy as np
from jax import lax
from jax.experimental import pallas as pl
from jax.experimental.pallas import tpu as pltpu
from jax.sharding import PartitionSpec as P

HD = 256
MESH = pl.DeviceIdType.MESH
LANES = 128
WAYS = 4
TILE = 256
LOW, FULL = (jnp.bfloat16, jnp.float32)
PAIRS = ("xn1", "xn2", "dffn", "dproj", "attended", "hidden", "dgate", "dup", "dqp", "dkvp")
PARTS = ("q", "kv", "o", "gate", "up", "down")

eps = 1e-06
rope_base = 1000000.0
gelu_c = 0.7978845608028654
gelu_k = 0.044715


def dot_plain(left, right):
    return jnp.dot(left, right, preferred_element_type=FULL)


def dot_last(left, right):
    return lax.dot_general(
        left, right, (((1,), (1,)), ((), ())), preferred_element_type=FULL
    )


def dot_first(left, right):
    return lax.dot_general(
        left, right, (((0,), (0,)), ((), ())), preferred_element_type=FULL
    )


def norm_parts(value):
    scale = lax.rsqrt(jnp.mean(value * value, axis=-1, keepdims=True) + eps)
    return (value * scale, scale)


def norm_back(dnormed, unit, scale):
    return scale * (dnormed - unit * jnp.mean(dnormed * unit, axis=-1, keepdims=True))


def rotate(value, cosine, sine):
    half = value.shape[-1] // 2
    first, second = (value[..., :half], value[..., half:])
    return jnp.concatenate(
        [first * cosine - second * sine, second * cosine + first * sine], axis=-1
    )


def unrotate(value, cosine, sine):
    half = value.shape[-1] // 2
    first, second = (value[..., :half], value[..., half:])
    return jnp.concatenate(
        [first * cosine + second * sine, second * cosine - first * sine], axis=-1
    )


def greet(peers):
    barrier = pltpu.get_barrier_semaphore()
    for peer in peers:
        pl.semaphore_signal(barrier, inc=1, device_id=peer, device_id_type=MESH)
    pl.semaphore_wait(barrier, len(peers))


def remote(src, dst, send_sem, recv_sem, peer):
    return pltpu.make_async_remote_copy(
        src_ref=src,
        dst_ref=dst,
        send_sem=send_sem,
        recv_sem=recv_sem,
        device_id=peer,
        device_id_type=MESH,
    )


def send(src, dst, sems, where, peer):
    copy = remote(src, dst, sems[0].at[where], sems[1].at[where], peer)
    copy.start()
    return copy


def columns(member, width):
    return pl.ds(pl.multiple_of(member * width, LANES), width)


def block_rows(index, count):
    return pl.ds(pl.multiple_of(index * count, 16), count)


class Sizes:
    def __init__(self, shard, ctx, tp, tokens, deep, qcols, ff, window):
        self.S, self.C, self.TP = (shard, ctx, tp)
        self.T, self.D, self.R = (tokens, deep, deep // shard)
        self.HQ, self.F, self.W = (qcols, ff, window)
        self.heads = qcols // HD
        self.groups = ctx // WAYS
        self.full = [qcols, 2 * HD, qcols, ff, ff, ff]
        self.width = [item // WAYS for item in self.full]
        self.order = [5, 3, 4, 2, 0, 1]
        self.at = {}
        total = 0
        for a in self.order:
            self.at[a] = total
            total = total + self.width[a]
        self.wide = total


class Named:
    def __init__(self, names, refs):
        for name, ref in zip(names, refs, strict=True):
            setattr(self, name, ref)


class Place:
    def __init__(self, c):
        shard, ctx, tp = (
            lax.axis_index("shard"),
            lax.axis_index("ctx"),
            lax.axis_index("tp"),
        )
        core = lax.rem(ctx, 2)
        high = lax.rem(lax.div(ctx, 2), 2)
        near, far = (ctx + 1 - 2 * core, ctx + 2 - 4 * high)
        self.shard, self.ctx, self.tp = (shard, ctx, tp)
        self.member, self.other = (lax.rem(ctx, WAYS), lax.rem(far, WAYS))
        self.core, self.high = (core, high)
        self.group = lax.div(ctx, WAYS)
        self.near_id, self.far_id = ((shard, near, tp), (shard, far, tp))
        self.diag_id = (shard, near + far - ctx, tp)
        left, right = (shard, c.S - 1 - shard)
        least = jnp.minimum(left, right)
        self.far_by = []
        for i in range(c.S - 1):
            hop = i // 2 + 1
            both = hop if i % 2 == 0 else c.S - hop
            alone = i - least + 1
            alone = jnp.where(left > right, alone, c.S - alone)
            self.far_by.append(jnp.where(i < 2 * least, both, alone))
        self.last = c.S - 1
        self.at_end = (shard == 0) | (shard == c.S - 1)
        self.next_to_end = (shard == 1) | (shard == c.S - 2)
        self.after_id = (jnp.minimum(shard + 1, c.S - 1), ctx, tp)
        self.before_id = (jnp.maximum(shard - 1, 0), ctx, tp)
        self.z_ids = [(lax.rem(shard + d, c.S), ctx, tp) for d in range(1, c.S)]
        self.up_ids = [(shard, lax.rem(ctx + d, c.C), tp) for d in range(1, c.C)]
        self.down_ids = [
            (shard, lax.rem(ctx - d + c.C, c.C), tp) for d in range(1, c.C)
        ]
        self.g_ids = [
            (shard, lax.rem(ctx + WAYS * d, c.C), tp) for d in range(1, c.groups)
        ]
        self.t_ids = [(shard, ctx, lax.rem(tp + d, c.TP)) for d in range(1, c.TP)]


    def by_early(self, d):
        last = self.last
        first_end = (self.shard == 0) & (d == last)
        return first_end | ((self.shard == last) & (d == 1))

    def joined(self, d):
        last = self.last
        low = (self.shard == 1) & (d == last - 1)
        return low | ((self.shard == last - 1) & (d == 2))

    def not_from(self, d):
        last = self.last
        return ((self.shard == last) & (d == last)) | ((self.shard == 0) & (d == 1))


class Gather:
    def __init__(self, c, p, k):
        self.c, self.p, self.k = (c, p, k)
        self.src = [k.q_in, None, k.o_in, k.gate_in, k.up_in, k.down_in]
        self.dst = [k.qw, k.kvw, k.ow, k.gw, k.uw, k.dw]
        self.first, self.across, self.landing, self.own = ([], {}, {}, [])

    def local(self, src, dst):
        copy = pltpu.make_async_copy(src, dst, self.k.local.at[len(self.own)])
        copy.start()
        self.own.append(copy)

    def start_own(self):
        c, p, k = (self.c, self.p, self.k)
        rows = block_rows(p.shard, c.R)
        self.local(k.k_in, k.kvw.at[rows, pl.ds(0, HD)])
        self.local(k.v_in, k.kvw.at[rows, pl.ds(HD, HD)])
        for a in (0, 2, 3, 4, 5):
            self.local(self.src[a], self.dst[a].at[rows])

    def start(self, a):
        c, p, k = (self.c, self.p, self.k)
        cols = columns(p.member, c.width[a])
        rows = block_rows(p.shard, c.R)
        src = self.dst[a].at[rows, cols] if a == 1 else self.src[a].at[:, cols]
        for side, ok, peer, at in (
            (0, p.shard < c.S - 1, p.after_id, 0),
            (1, p.shard > 0, p.before_id, c.S - 2),
        ):
            copy = remote(
                src,
                self.dst[a].at[rows, cols],
                k.zo_s.at[side, a],
                k.za_r.at[at, a],
                peer,
            )
            pl.when(ok)(copy.start)
            self.first.append((ok, copy))

    def piece(self, i, a, member):
        c, p = (self.c, self.p)
        source = lax.rem(p.shard - p.far_by[i] + c.S, c.S)
        return self.dst[a].at[block_rows(source, c.R), columns(member, c.width[a])]

    def relay(self, a, i):
        c, p, k = (self.c, self.p, self.k)
        middle = (p.shard > 0) & (p.shard < c.S - 1)
        d = p.far_by[i]
        block = self.piece(i, a, p.member)
        up = d <= p.shard
        target = jnp.where(up, p.shard + 1, p.shard - 1)
        target = jnp.clip(target, 0, c.S - 1)
        there = jnp.clip(jnp.where(up, d, d - 2), 0, c.S - 2)
        copy = remote(
            block,
            block,
            k.zf_s.at[i, a],
            k.za_r.at[there, a],
            (target, p.ctx, p.tp),
        )
        remote(block, block, k.zf_s.at[i, a], k.za_r.at[d - 1, a], p.far_id).wait_recv()
        pl.when(middle)(copy.start)
        self.first.append((middle, copy))
        self.across[i, a] = send(block, block, (k.fa_s, k.fa_r), (i, a), p.far_id)
        self.landing.setdefault(a, []).append(
            send(block, block, (k.na_s, k.na_r), (i, a), p.near_id)
        )

    def pass_on(self, a, i):
        p, k = (self.p, self.k)
        self.across[i, a].wait_recv()
        block = self.piece(i, a, p.other)
        self.landing[a].append(send(block, block, (k.ca_s, k.ca_r), (i, a), p.near_id))

    def ready(self, a):
        for item in self.landing[a]:
            item.wait_recv()

    def end(self):
        for ok, copy in self.first:
            pl.when(ok)(copy.wait_send)
        for group in (self.across.values(), *self.landing.values()):
            for item in group:
                item.wait_send()


class Reduce:
    def __init__(self, c, p, k):
        self.c, self.p, self.k = (c, p, k)
        self.grads = [k.g_q, k.g_kv, k.g_o, k.g_gate, k.g_up, k.g_down]
        self.outs = [k.o_q, k.o_kv, k.o_o, k.o_gate, k.o_up, k.o_down]
        self.near, self.along, self.early, self.shared, self.ends = ({}, {}, {}, {}, [])

    def span(self, a):
        return pl.ds(self.c.at[a], self.c.width[a])

    def start(self, a):
        c, p, k = (self.c, self.p, self.k)
        self.near[a] = send(
            self.grads[a].at[:, columns(1 - p.core, c.width[a])],
            k.half.at[:, self.span(a)],
            (k.gc_s, k.gc_r),
            a,
            p.near_id,
        )

    def summed(self, a):
        c, p, k = (self.c, self.p, self.k)
        self.near[a].wait_recv()
        return k.half[:, self.span(a)].astype(FULL) + self.grads[a][
            :, columns(p.core, c.width[a])
        ].astype(FULL)

    def spread(self, a, total=None):
        c, p, k = (self.c, self.p, self.k)
        total = self.summed(a) if total is None else total
        k.mine[:, self.span(a)] = total.astype(LOW)
        span = self.span(a)
        self.along[a] = [
            remote(
                k.mine.at[block_rows(p.z_ids[d - 1][0], c.R), span],
                k.arrived.at[d - 1, :, span],
                k.gz_s.at[d - 1, a],
                k.gz_r.at[d - 1, a],
                p.z_ids[d - 1],
            )
            for d in range(1, c.S)
        ]
        opposite = block_rows(c.S - 1 - p.shard, c.R)
        self.early[a] = remote(
            k.mine.at[opposite, span],
            k.early.at[:, span],
            k.ge_s.at[a],
            k.ge_r.at[a],
            (jnp.where(p.shard == 0, 1, c.S - 2), p.ctx, p.tp),
        )
        pl.when(p.at_end)(self.early[a].start)
        for d in range(1, c.S):
            ok = jnp.logical_not(p.by_early(d) | p.joined(d))
            pl.when(ok)(self.along[a][d - 1].start)

    def forward(self, a):
        c, p, k = (self.c, self.p, self.k)
        span = self.span(a)

        @pl.when(p.next_to_end)
        def _():
            self.early[a].wait_recv()
            rows = block_rows(jnp.where(p.shard == 1, c.S - 1, 0), c.R)
            total = k.mine[rows, span].astype(FULL) + k.early[:, span].astype(FULL)
            k.mine[rows, span] = total.astype(LOW)

        for d in sorted({2, c.S - 2}):
            pl.when(p.joined(d))(self.along[a][d - 1].start)

    def collect(self, a):
        c, p, k = (self.c, self.p, self.k)
        span = self.span(a)
        k.total[:, span] = k.mine[block_rows(p.shard, c.R), span].astype(FULL)
        for d in range(1, c.S):
            ok = jnp.logical_not(p.not_from(d))

            @pl.when(ok)
            def _(d=d):
                self.along[a][d - 1].wait_recv()
                k.total[:, span] = k.total[:, span] + k.arrived[d - 1, :, span].astype(FULL)

        total = k.total[:, span]
        if c.groups > 1:
            k.grouped[p.group, :, span] = total.astype(LOW)
            piece = k.grouped.at[p.group, :, span]
            moved = [
                send(piece, piece, (k.gg_s, k.gg_r), (d - 1, a), p.g_ids[d - 1])
                for d in range(1, c.groups)
            ]
            for item in moved:
                item.wait_recv()
            self.ends.extend(moved)
            total = k.grouped[0, :, span].astype(FULL)
            for g in range(1, c.groups):
                total = total + k.grouped[g, :, span].astype(FULL)
        return total

    def share(self, a, total):
        c, p, k = (self.c, self.p, self.k)
        cols = columns(p.member, c.width[a])
        self.outs[a][:, cols] = total.astype(LOW)
        piece = self.outs[a].at[:, cols]
        peers = (p.far_id, p.near_id) if a > 2 else (p.far_id, p.near_id, p.diag_id)
        self.shared[a] = [
            send(piece, piece, (k.gs_s, k.gs_r), (at, a), peer)
            for at, peer in enumerate(peers)
        ]

    def pass_on(self, a):
        c, p, k = (self.c, self.p, self.k)
        self.shared[a][0].wait_recv()
        piece = self.outs[a].at[:, columns(p.other, c.width[a])]
        self.shared[a].append(send(piece, piece, (k.gs_s, k.gs_r), (2, a), p.near_id))

    def arrived(self, a):
        for item in self.shared[a][1 if a > 2 else 0 :]:
            item.wait_recv()

    def end(self):
        for a in self.c.order:
            pl.when(self.p.at_end)(self.early[a].wait_send)
            for d in range(1, self.c.S):
                ok = jnp.logical_not(self.p.by_early(d))
                pl.when(ok)(self.along[a][d - 1].wait_send)
        for group in (
            self.near.values(),
            *self.shared.values(),
            self.ends,
        ):
            for item in group:
                item.wait_send()


def block_kernel(c, names, *refs):
    k = Named(names, refs)
    p = Place(c)
    T, D, F, W, S, TP = (c.T, c.D, c.F, c.W, c.S, c.TP)
    scaling = HD ** (-0.5)
    sent = []
    left = []

    def leave(src, dst):
        copy = pltpu.make_async_copy(src, dst, k.leave.at[len(left)])
        copy.start()
        left.append(copy)

    def tp_start(slot, value):
        k.part[slot] = value.astype(LOW)
        copies = [
            send(
                k.part.at[slot],
                k.part_in.at[slot, d - 1],
                (k.tp_s, k.tp_r),
                (slot, d - 1),
                p.t_ids[d - 1],
            )
            for d in range(1, TP)
        ]
        sent.extend(copies)
        return copies

    def tp_total(slot, copies):
        total = k.part[slot].astype(FULL)
        for d in range(1, TP):
            copies[d - 1].wait_recv()
            total = total + k.part_in[slot, d - 1].astype(FULL)
        return total

    paired = {}
    held = c.C == WAYS and W > 2

    def pair(name, value, half=False):
        width = value.shape[1] // 2
        src = value.at[:, columns(1 - p.high, width)] if half else value
        order = PAIRS.index(name)
        paired[name] = send(
            src, getattr(k, "far_" + name), (k.px_s, k.px_r), order, p.far_id
        )
        sent.append(paired[name])

    weights = Gather(c, p, k)
    weights.start_own()
    k.gains_at[p.shard] = k.gain_in[...]
    greet(p.z_ids + p.up_ids + p.t_ids)
    gain_copies = [
        send(
            k.gains_at.at[p.shard],
            k.gains_at.at[p.shard],
            (k.gn_s, k.gn_r),
            d - 1,
            p.z_ids[d - 1],
        )
        for d in range(1, S)
    ]
    sent.extend(gain_copies)
    weights.start(0)
    weights.own[0].wait()
    weights.own[1].wait()
    for a in range(1, 6):
        weights.start(a)
    unit1, r1 = norm_parts(k.x[...])
    k.unit1[...] = unit1
    k.r1[...] = r1
    k.unit_low[...] = unit1.astype(LOW)
    unit_copies = [
        send(
            k.unit_low,
            k.unit_win.at[pl.ds((d - 1) * T, T)],
            (k.un_s, k.un_r),
            d - 1,
            p.up_ids[d - 1],
        )
        for d in range(1, W)
    ]
    sent.extend(unit_copies)

    count = k.lengths.shape[1]
    lens = [k.lengths[0, j] for j in range(count)]
    ends = []
    for item in lens:
        ends.append(item if not ends else ends[-1] + item)

    def segment_of(index):
        return sum([(index >= end).astype(jnp.int32) for end in ends])

    def place_of(index):
        return index - sum([jnp.where(index >= e, n, 0) for e, n in zip(ends, lens)])

    q_index = p.ctx * T + lax.broadcasted_iota(jnp.int32, (T, T), 0)
    q_seg = segment_of(q_index)
    for d in range(W):
        base = lax.rem(p.ctx - d + c.C, c.C) * T
        k_index = base + lax.broadcasted_iota(jnp.int32, (T, T), 1)
        allowed = (q_seg == segment_of(k_index)) & (k_index <= q_index)
        k.mask[:, pl.ds(d * T, T)] = allowed.astype(FULL)
        rows = base + lax.broadcasted_iota(jnp.int32, (T, HD // 2), 0)
        angle = place_of(rows).astype(FULL) * k.freq[...]
        k.cosine[pl.ds(d * T, T)] = jnp.cos(angle)
        k.sine[pl.ds(d * T, T)] = jnp.sin(angle)

    for item in gain_copies:
        item.wait_recv()
    wide_gain = jnp.zeros((8, D), FULL)
    head_gain = jnp.zeros((8, HD), FULL)
    lanes = k.gain_in.shape[1]
    for s in range(S):
        part = k.gains_at[s].astype(LOW)
        for total in ("wide", "head"):
            width = D if total == "wide" else HD
            row = lax.broadcasted_iota(jnp.int32, (lanes, width), 0)
            col = lax.broadcasted_iota(jnp.int32, (lanes, width), 1)
            pick = (col == row + s * (width // S)).astype(FULL).astype(LOW)
            if total == "wide":
                wide_gain = wide_gain + dot_plain(part, pick)
            else:
                head_gain = head_gain + dot_plain(part, pick)
    k.wide_gain[...] = wide_gain
    k.head_gain[...] = head_gain

    def gain(row):
        return k.wide_gain[row : row + 1, :]

    g_q, g_k = (lambda: k.head_gain[4:5, :]), (lambda: k.head_gain[5:6, :])

    k.xn1[...] = (k.unit1[...] * gain(0)).astype(LOW)
    for item in weights.own[2:]:
        item.wait()

    def project():
        weights.ready(0)
        qp = dot_plain(k.xn1[...], k.qw[...])
        cos0, sin0 = (k.cosine[pl.ds(0, T)], k.sine[pl.ds(0, T)])
        for h in range(c.heads):
            cols = pl.ds(h * HD, HD)
            unit, scale = norm_parts(qp[:, h * HD : (h + 1) * HD])
            k.qunit[:, cols] = unit
            k.rq[h] = scale
            k.queries[:, cols] = rotate(unit * g_q(), cos0, sin0).astype(LOW)
        weights.ready(1)
        for d in range(W):
            rows = pl.ds(d * T, T)
            if d == 0:
                xw = k.xn1[...]
            else:
                unit_copies[d - 1].wait_recv()
                low = k.unit_win[pl.ds((d - 1) * T, T)]
                xw = (low.astype(FULL) * gain(0)).astype(LOW)
            kvp = dot_plain(xw, k.kvw[...])
            unit, scale = norm_parts(kvp[:, :HD])
            if d == 0:
                k.kunit[...] = unit
                k.rk[...] = scale
            k.keys[rows] = rotate(unit * g_k(), k.cosine[rows], k.sine[rows]).astype(LOW)
            k.values[rows] = kvp[:, HD:].astype(LOW)

    def attend(h):
        cols = pl.ds(h * HD, HD)
        raw = dot_last(k.queries[:, cols], k.keys[...]) * scaling
        logits = jnp.where(k.mask[...] > 0.5, raw, -1e30)
        peak = jnp.max(logits, axis=1, keepdims=True)
        lifted = jnp.exp(logits - peak)
        w = lifted * (1.0 / jnp.sum(lifted, axis=1, keepdims=True))
        k.w[h] = w
        k.attended[:, cols] = dot_plain(w.astype(LOW), k.values[...]).astype(LOW)

    proj_copies = []

    def output():
        weights.ready(2)
        proj_copies.extend(tp_start(0, dot_last(k.attended[...], k.ow[...])))

    steps = []
    reach = 0.0
    for a in range(6):
        reach = reach + c.width[a] / LANES
        for i in range(S - 1):
            steps.append((reach + 3.5 * i, len(steps), functools.partial(weights.relay, a, i)))
            steps.append((reach + 3.5 * i + 4.0, len(steps), functools.partial(weights.pass_on, a, i)))
    ready = 2.0 + 3.5 * (S - 2) + 4.0
    steps.append((ready + 0.3, len(steps), project))
    for h in range(c.heads):
        steps.append((ready + 0.6 + 0.3 * h, len(steps), functools.partial(attend, h)))
    steps.append((max(ready + 0.6 + 0.3 * c.heads, ready + 1.5), len(steps), output))
    for _, _, step in sorted(steps, key=lambda item: item[:2]):
        step()
    proj = tp_total(0, proj_copies)
    aunit, ra = norm_parts(proj)
    k.aunit[...] = aunit
    k.ra[...] = ra
    h1 = k.x[...] + aunit * gain(1)
    k.h1[...] = h1
    unit2, r2 = norm_parts(h1)
    k.unit2[...] = unit2
    k.r2[...] = r2
    k.xn2[...] = (unit2 * gain(2)).astype(LOW)
    pair("xn2", k.xn2)
    pair("attended", k.attended, True)
    weights.ready(3)
    weights.ready(4)

    for at in range(0, F, TILE):
        cols = pl.ds(at, TILE)
        gate = dot_plain(k.xn2[...], k.gw[:, cols])
        up = dot_plain(k.xn2[...], k.uw[:, cols])
        square = gate * gate
        bent = jnp.tanh(gelu_c * (gate + gelu_k * (square * gate)))
        half = 0.5 * (1.0 + bent)
        act = gate * half
        slope = half + 0.5 * gate * (1.0 - bent * bent) * (
            gelu_c * (1.0 + 3.0 * gelu_k * square)
        )
        k.act[:, cols] = act
        k.slope[:, cols] = up * slope
        k.hidden[:, cols] = (act * up).astype(LOW)
    pair("hidden", k.hidden, True)
    weights.ready(5)
    ffn = tp_total(1, tp_start(1, dot_last(k.hidden[...], k.dw[...])))
    funit, rf = norm_parts(ffn)
    k.y[...] = k.h1[...] + funit * gain(3)
    leave(k.y, k.h_y)

    grads = Reduce(c, p, k)
    share = 1.0 / TP
    dy = k.dy[...]
    k.gsum_own[...] = jnp.zeros(k.gsum_own.shape, FULL)
    k.gsum_own[3:4, :] = jnp.sum(dy * funit, axis=0, keepdims=True) * share
    dffn = norm_back(dy * gain(3), funit, rf).astype(LOW)
    k.dffn[...] = dffn

    pair("dffn", k.dffn)

    def transposed(name, own):
        if name == "xn1" and held:
            low = k.unit_win[pl.ds(T, T)]
            k.far_xn1[...] = (low.astype(FULL) * gain(0)).astype(LOW)
        else:
            paired[name].wait_recv()
        k.left_t[:, pl.ds(0, T)] = jnp.transpose(own[...].astype(FULL)).astype(LOW)
        far = getattr(k, "far_" + name)
        k.left_t[:, pl.ds(T, T)] = jnp.transpose(far[...].astype(FULL)).astype(LOW)

    def grad(a, name, own):
        paired[name].wait_recv()
        half = c.full[a] // 2
        k.right[pl.ds(0, T), pl.ds(0, half)] = own[:, columns(p.high, half)]
        k.right[pl.ds(T, T), pl.ds(0, half)] = getattr(k, "far_" + name)[...]
        for at in range(0, half, TILE):
            cols = pl.ds(at, TILE)
            grads.grads[a][:, cols] = dot_plain(k.left_t[...], k.right[:, cols]).astype(LOW)
        grads.start(a)

    for at in range(0, F, TILE):
        cols = pl.ds(at, TILE)
        dhid = dot_plain(k.dffn[...], k.dw[:, cols])
        k.dup[:, cols] = (dhid * k.act[:, cols]).astype(LOW)
        k.dgate[:, cols] = (dhid * k.slope[:, cols]).astype(LOW)
    pair("dgate", k.dgate, True)
    pair("dup", k.dup, True)
    if not held:
        pair("xn1", k.xn1)
    back = tp_start(
        2, dot_last(k.dgate[...], k.gw[...]) + dot_last(k.dup[...], k.uw[...])
    )
    transposed("dffn", k.dffn)
    grad(5, "hidden", k.hidden)
    grads.spread(5)
    dxn2 = tp_total(2, back)
    unit2 = k.unit2[...]
    k.gsum_own[2:3, :] = jnp.sum(dxn2 * unit2, axis=0, keepdims=True) * share
    dh1 = k.dy[...] + norm_back(dxn2 * gain(2), unit2, k.r2[...])
    k.dh1[...] = dh1
    aunit = k.aunit[...]
    k.gsum_own[1:2, :] = jnp.sum(dh1 * aunit, axis=0, keepdims=True) * share
    k.dproj[...] = norm_back(dh1 * gain(1), aunit, k.ra[...]).astype(LOW)
    pair("dproj", k.dproj)
    transposed("xn2", k.xn2)
    grad(3, "dgate", k.dgate)
    grad(4, "dup", k.dup)
    k.dout[...] = dot_plain(k.dproj[...], k.ow[...]).astype(LOW)

    key_terms = jnp.zeros((W * T, HD), FULL)
    value_terms = jnp.zeros((W * T, HD), FULL)
    for h in range(c.heads):
        cols = pl.ds(h * HD, HD)
        w = k.w[h]
        dout = k.dout[:, cols]
        query = k.queries[:, cols]
        delta = jnp.sum(
            dout.astype(FULL) * k.attended[:, cols].astype(FULL), axis=1, keepdims=True
        )
        dprob = dot_last(dout, k.values[...])
        dscore = w * (dprob - delta) * scaling
        k.dq[:, cols] = dot_plain(dscore.astype(LOW), k.keys[...])
        key_terms = key_terms + dot_plain(jnp.transpose(dscore).astype(LOW), query)
        value_terms = value_terms + dot_plain(jnp.transpose(w).astype(LOW), dout)
    k.terms[:, pl.ds(0, HD)] = key_terms.astype(LOW)
    k.terms[:, pl.ds(HD, HD)] = value_terms.astype(LOW)
    scatter = [
        send(
            k.terms.at[pl.ds(d * T, T)],
            k.terms_in.at[d - 1],
            (k.sc_s, k.sc_r),
            d - 1,
            p.down_ids[d - 1],
        )
        for d in range(1, W)
    ]
    sent.extend(scatter)
    grads.forward(5)
    cos0, sin0 = (k.cosine[pl.ds(0, T)], k.sine[pl.ds(0, T)])
    dg_q = jnp.zeros((1, HD), FULL)
    for h in range(c.heads):
        cols = pl.ds(h * HD, HD)
        dqn = unrotate(k.dq[:, cols], cos0, sin0)
        unit = k.qunit[:, cols]
        dg_q = dg_q + jnp.sum(dqn * unit, axis=0, keepdims=True)
        k.dqp[:, cols] = norm_back(dqn * g_q(), unit, k.rq[h]).astype(LOW)
    k.gsum_own[4:5, pl.ds(0, HD)] = dg_q
    pair("dqp", k.dqp, True)
    dxn1 = dot_last(k.dqp[...], k.qw[...])
    grads.spread(3)
    dkv = k.terms[pl.ds(0, T), :].astype(FULL)
    for d in range(1, W):
        scatter[d - 1].wait_recv()
        dkv = dkv + k.terms_in[d - 1].astype(FULL)
    dkn = unrotate(dkv[:, :HD], cos0, sin0)
    kunit = k.kunit[...]
    k.gsum_own[5:6, pl.ds(0, HD)] = jnp.sum(dkn * kunit, axis=0, keepdims=True)
    k.dkvp[:, pl.ds(0, HD)] = norm_back(dkn * g_k(), kunit, k.rk[...]).astype(LOW)
    k.dkvp[:, pl.ds(HD, HD)] = dkv[:, HD:].astype(LOW)
    pair("dkvp", k.dkvp, True)
    last = tp_start(3, dxn1 + dot_last(k.dkvp[...], k.kvw[...]))
    grads.forward(3)
    grads.spread(4)
    transposed("dproj", k.dproj)
    grad(2, "attended", k.attended)
    grads.share(5, grads.collect(5))
    transposed("xn1", k.xn1)
    grad(0, "dqp", k.dqp)
    grads.forward(4)
    grads.spread(2)
    dxn1 = tp_total(3, last)
    unit1 = k.unit1[...]
    k.gsum_own[0:1, :] = jnp.sum(dxn1 * unit1, axis=0, keepdims=True) * share
    grad(1, "dkvp", k.dkvp)
    grads.forward(2)
    grads.spread(0)
    k.kv_done[...] = grads.summed(1).astype(LOW)
    kvs = [
        send(k.kv_done, k.kv_in.at[d - 1], (k.kt_s, k.kt_r), d - 1, p.t_ids[d - 1])
        for d in range(1, TP)
    ]
    sent.extend(kvs)
    gain_near = send(k.gsum_own, k.gsum_in.at[0], (k.gr_s, k.gr_r), 0, p.near_id)
    k.xg[...] = k.dh1[...] + norm_back(dxn1 * gain(0), unit1, k.r1[...])
    leave(k.xg, k.h_xg)
    grads.share(3, grads.collect(3))
    grads.pass_on(5)
    gain_near.wait_recv()
    k.gsum_mid[0] = k.gsum_own[...] + k.gsum_in[0]
    gain_far = send(k.gsum_mid.at[0], k.gsum_in.at[1], (k.gr_s, k.gr_r), 1, p.far_id)
    sent.extend([gain_near, gain_far])
    total = k.kv_done[...].astype(FULL)
    for d in range(1, TP):
        kvs[d - 1].wait_recv()
        total = total + k.kv_in[d - 1].astype(FULL)
    grads.spread(1, total)
    grads.forward(0)
    grads.share(4, grads.collect(4))
    grads.pass_on(3)
    gain_far.wait_recv()
    k.gsum_z[p.shard] = k.gsum_mid[0] + k.gsum_in[1]
    gains_z = [
        send(k.gsum_z.at[p.shard], k.gsum_z.at[p.shard], (k.gh_s, k.gh_r), d - 1, p.z_ids[d - 1])
        for d in range(1, S)
    ]
    sent.extend(gains_z)
    grads.forward(1)
    grads.share(2, grads.collect(2))
    grads.pass_on(4)
    for item in gains_z:
        item.wait_recv()
    total = k.gsum_z[0]
    for s in range(1, S):
        total = total + k.gsum_z[s]
    if c.groups > 1:
        k.gsum_g[p.group] = total
        moved = [
            send(k.gsum_g.at[p.group], k.gsum_g.at[p.group], (k.gi_s, k.gi_r), d - 1, p.g_ids[d - 1])
            for d in range(1, c.groups)
        ]
        sent.extend(moved)
        for item in moved:
            item.wait_recv()
        total = k.gsum_g[0]
        for g in range(1, c.groups):
            total = total + k.gsum_g[g]
    k.gsum_t[p.tp] = total
    gains_t = [
        send(k.gsum_t.at[p.tp], k.gsum_t.at[p.tp], (k.gj_s, k.gj_r), d - 1, p.t_ids[d - 1])
        for d in range(1, TP)
    ]
    sent.extend(gains_t)
    grads.share(0, grads.collect(0))
    grads.share(1, grads.collect(1))
    for item in gains_t:
        item.wait_recv()
    total = k.gsum_t[0]
    for t in range(1, TP):
        total = total + k.gsum_t[t]
    k.gsum[...] = total
    hbm = [k.h_q, k.h_kv, k.h_o, k.h_gate, k.h_up, k.h_down]
    for a in c.order:
        grads.arrived(a)
        leave(grads.outs[a], hbm[a])
    grads.end()
    weights.end()
    for item in left:
        item.wait()
    for item in sent:
        item.wait_send()


def run_block(c, lengths, freq, x, dy, gain_in, weights):
    T, D, R, S, W, F, HQ = (c.T, c.D, c.R, c.S, c.W, c.F, c.HQ)
    names, operands, in_specs = ([], [], [])
    vm, anywhere = (
        pl.BlockSpec(memory_space=pltpu.VMEM),
        pl.BlockSpec(memory_space=pl.ANY),
    )

    def operand(name, value, spec):
        names.append(name)
        operands.append(value)
        in_specs.append(spec)

    operand("lengths", lengths, pl.BlockSpec(memory_space=pltpu.SMEM))
    operand("freq", freq, vm)
    operand("x", x, vm)
    operand("dy", dy, vm)
    operand("gain_in", gain_in, vm)
    for name, value in zip(("q", "k", "v", "o", "gate", "up", "down"), weights):
        operand(name + "_in", value, anywhere)
    outs = [(f"h_{name}", (R, width), LOW) for name, width in zip(PARTS, c.full)]
    outs.extend([("h_y", (T, D), FULL), ("h_xg", (T, D), FULL), ("gsum", (8, D), FULL)])
    names.extend([item[0] for item in outs])
    scratch = []

    def vmem(name, shape, dtype):
        names.append(name)
        scratch.append(pltpu.VMEM(shape, dtype))

    def sem(name, *shape):
        for end in ("_s", "_r"):
            names.append(name + end)
            scratch.append(pltpu.SemaphoreType.DMA(shape))

    for name, width in zip(PARTS, c.full):
        vmem("o_" + name, (R, width), LOW)
    vmem("y", (T, D), FULL)
    vmem("xg", (T, D), FULL)
    names.append("leave")
    scratch.append(pltpu.SemaphoreType.DMA((8,)))
    for name, width in zip(("qw", "kvw", "ow", "gw", "uw", "dw"), c.full):
        vmem(name, (D, width), LOW)
    vmem("gains_at", (S,) + gain_in.shape, FULL)
    vmem("wide_gain", (8, D), FULL)
    vmem("head_gain", (8, HD), FULL)
    for name in ("unit1", "aunit", "h1", "unit2", "dh1"):
        vmem(name, (T, D), FULL)
    for name in ("r1", "ra", "r2", "rk"):
        vmem(name, (T, 1), FULL)
    for name in ("unit_low", "xn1", "xn2", "dffn"):
        vmem(name, (T, D), LOW)
    vmem("unit_win", (max(W - 1, 1) * T, D), LOW)
    vmem("left_t", (D, 2 * T), LOW)
    for name in ("cosine", "sine"):
        vmem(name, (W * T, HD // 2), FULL)
    vmem("mask", (T, W * T), FULL)
    vmem("qunit", (T, HQ), FULL)
    vmem("rq", (c.heads, T, 1), FULL)
    for name in ("queries", "attended", "dout", "dqp"):
        vmem(name, (T, HQ), LOW)
    vmem("dq", (T, HQ), FULL)
    vmem("dkvp", (T, 2 * HD), LOW)
    for name in ("keys", "values"):
        vmem(name, (W * T, HD), LOW)
    vmem("kunit", (T, HD), FULL)
    vmem("w", (c.heads, T, W * T), FULL)
    for name in ("act", "slope"):
        vmem(name, (T, F), FULL)
    for name in ("hidden", "dup", "dgate"):
        vmem(name, (T, F), LOW)
    vmem("part", (4, T, D), LOW)
    vmem("part_in", (4, max(c.TP - 1, 1), T, D), LOW)
    vmem("terms", (W * T, 2 * HD), LOW)
    vmem("terms_in", (max(W - 1, 1), T, 2 * HD), LOW)
    for name, width in zip(("g_q", "g_kv", "g_o", "g_gate", "g_up", "g_down"), c.full):
        vmem(name, (D, width // 2), LOW)
    for name in ("half", "mine"):
        vmem(name, (D, c.wide), LOW)
    vmem("right", (2 * T, max(c.full) // 2), LOW)
    for name in PAIRS[:4]:
        vmem("far_" + name, (T, D), LOW)
    for name, width in zip(PAIRS[4:], (HQ, F, F, F, HQ, 2 * HD), strict=True):
        vmem("far_" + name, (T, width // 2), LOW)
    vmem("dproj", (T, D), LOW)
    sem("px", len(PAIRS))
    vmem("arrived", (S - 1, R, c.wide), LOW)
    vmem("early", (R, c.wide), LOW)
    vmem("total", (R, c.wide), FULL)
    sem("ge", 6)
    if c.groups > 1:
        vmem("grouped", (c.groups, R, c.wide), LOW)
        sem("gg", c.groups - 1, 6)
        vmem("gsum_g", (c.groups, 8, D), FULL)
        sem("gi", c.groups - 1)
    vmem("kv_done", (D, c.width[1]), LOW)
    vmem("kv_in", (max(c.TP - 1, 1), D, c.width[1]), LOW)
    vmem("gsum_own", (8, D), FULL)
    vmem("gsum_in", (2, 8, D), FULL)
    vmem("gsum_mid", (1, 8, D), FULL)
    vmem("gsum_z", (S, 8, D), FULL)
    vmem("gsum_t", (c.TP, 8, D), FULL)
    names.append("local")
    scratch.append(pltpu.SemaphoreType.DMA((7,)))
    for name in ("za", "fa", "na", "ca"):
        sem(name, S - 1, 6)
    sem("zo", 2, 6)
    sem("zf", S - 1, 6)
    sem("gn", S - 1)
    sem("un", max(W - 1, 1))
    sem("tp", 4, max(c.TP - 1, 1))
    sem("gc", 6)
    sem("gz", S - 1, 6)
    sem("gs", 3, 6)
    sem("sc", max(W - 1, 1))
    sem("gr", 2)
    sem("gh", S - 1)
    sem("gj", max(c.TP - 1, 1))
    sem("kt", max(c.TP - 1, 1))
    return pl.pallas_call(
        functools.partial(block_kernel, c, names),
        out_shape=[jax.ShapeDtypeStruct(shape, kind) for _, shape, kind in outs],
        in_specs=in_specs,
        out_specs=[anywhere] * 8 + [vm],
        scratch_shapes=scratch,
        compiler_params=pltpu.CompilerParams(
            collective_id=0, has_side_effects=True, vmem_limit_bytes=58 * 1024 * 1024
        ),
        name="block",
    )(*operands)


def finish_kernel(c, *refs):
    ins, gsum, outs, small, stage, lows, through, sems, own_sems = (
        refs[:8],
        refs[8],
        refs[9:18],
        refs[18],
        refs[19:26],
        refs[26:32],
        refs[32],
        refs[33],
        refs[34],
    )
    copies = []

    def put(src, dst):
        copy = pltpu.make_async_copy(src, dst, sems.at[len(copies)])
        copy.start()
        copies.append(copy)

    taken = []
    for a in (5, 3, 4, 0, 2, 1):
        copy = pltpu.make_async_copy(ins[a], lows[a], own_sems.at[a])
        copy.start()
        taken.append((a, copy))
    for a in (6, 7):
        copy = pltpu.make_async_copy(ins[a], through.at[a - 6], own_sems.at[a])
        copy.start()
        taken.append((a, copy))
    shard = lax.axis_index("shard")
    for row, width in ((0, c.D), (4, HD)):
        part = gsum[...] if width == c.D else gsum[:, :HD]
        moved = pltpu.roll(part, lax.rem(width - shard * (width // c.S), width), 1)
        if row == 0:
            small[0:4, :] = moved[0:4, : small.shape[1]]
        else:
            small[4:8, :] = moved[4:8, : small.shape[1]]
    at = {0: (0,), 1: (1, 2), 2: (3,), 3: (4,), 4: (5,), 5: (6,)}
    for a, copy in taken:
        copy.wait()
        if a >= 6:
            put(through.at[a - 6], outs[a + 1])
            continue
        for j, slot in enumerate(at[a]):
            width = stage[slot].shape[1]
            stage[slot][...] = lows[a][:, j * width : (j + 1) * width].astype(FULL)
            put(stage[slot], outs[slot])
    for copy in copies:
        copy.wait()


def finish(c, parts, gsum):
    R = c.R
    widths = [c.HQ, HD, HD, c.HQ, c.F, c.F, c.F]
    vm, anywhere = (
        pl.BlockSpec(memory_space=pltpu.VMEM),
        pl.BlockSpec(memory_space=pl.ANY),
    )
    lanes = max(-(-c.R // LANES) * LANES, LANES)
    return pl.pallas_call(
        functools.partial(finish_kernel, c),
        out_shape=[jax.ShapeDtypeStruct((R, width), FULL) for width in widths]
        + [jax.ShapeDtypeStruct(item.shape, FULL) for item in parts[6:]]
        + [jax.ShapeDtypeStruct((8, lanes), FULL)],
        in_specs=[anywhere] * 8 + [vm],
        out_specs=[anywhere] * 9 + [vm],
        scratch_shapes=[pltpu.VMEM((R, width), FULL) for width in widths]
        + [pltpu.VMEM((R, width), LOW) for width in c.full]
        + [pltpu.VMEM((2,) + parts[6].shape, FULL)]
        + [pltpu.SemaphoreType.DMA((9,)), pltpu.SemaphoreType.DMA((8,))],
        compiler_params=pltpu.CompilerParams(vmem_limit_bytes=58 * 1024 * 1024),
        name="finish",
    )(*parts, gsum)


def per_device(
    block_input,
    out_cotangent,
    seq_lengths,
    q_weight,
    k_weight,
    v_weight,
    o_weight,
    gate_weight,
    up_weight,
    down_weight,
    attn_in_gain,
    attn_out_gain,
    ffn_in_gain,
    ffn_out_gain,
    query_gain,
    key_gain,
):
    tokens, width = block_input.shape
    n_ctx = lax.axis_size("ctx")
    n_shard = lax.axis_size("shard")
    longest = tokens * n_ctx // 2
    window = min(n_ctx, -(-(longest - 1) // tokens) + 1)
    c = Sizes(
        n_shard,
        n_ctx,
        lax.axis_size("tp"),
        tokens,
        width,
        q_weight.shape[1],
        gate_weight.shape[1],
        window,
    )
    gains = (attn_in_gain, attn_out_gain, ffn_in_gain, ffn_out_gain, query_gain, key_gain)
    lanes = -(-c.R // LANES) * LANES
    packed = jnp.zeros((8 * lanes,), FULL)
    for row, item in enumerate(gains):
        behind = (8 - row) * lanes - item.shape[0]
        packed = packed + jnp.pad(item.astype(FULL), (row * lanes, behind))
    packed = packed.reshape(8, lanes)
    freq = rope_base ** (-np.arange(HD // 2).astype(np.float32) * np.float32(2.0 / HD))
    outs = run_block(
        c,
        seq_lengths,
        jnp.asarray(freq.astype(np.float32)[None, :]),
        block_input,
        out_cotangent,
        packed,
        (q_weight, k_weight, v_weight, o_weight, gate_weight, up_weight, down_weight),
    )
    big = finish(c, outs[:8], outs[8])
    small = [
        big[9][row, : (width if row < 4 else HD) // n_shard] for row in range(len(gains))
    ]
    return (big[7], big[8], *big[:7], *small)


def solution(mesh):
    rows = P(("shard", "ctx"), None)
    split = P("shard", "tp")
    whole = P("shard", None)
    line = P("shard")
    return jax.shard_map(
        per_device,
        mesh=mesh,
        in_specs=(rows, rows, whole, split, whole, whole) + (split,) * 4 + (line,) * 6,
        out_specs=(rows, rows, split, whole, whole) + (split,) * 4 + (line,) * 6,
        check_vma=False,
    )
```
